32 devices in a mesh: seq: 8 (over y, x, core), dp: 4 (over z).
Axes of the slice: x: 2, y: 2, z: 4, core: 2. Of those that a mesh axis runs over, the one named last changes fastest.
Arguments:
- history: bfloat16 [9, 1024, 4096], P(None, 'seq', 'dp'), may hold values from -6 to 6
- cotangent: bfloat16 [1024, 4096], P('seq', 'dp'), may hold values from -6 to 6
- bucket_len: int32 [4, 8, 2], P('dp', 'seq'), may hold values from 32 to 96, as said below
- valid_len: int32 [4, 8, 2], P('dp', 'seq'), may hold values from 1 to 96, as said below
- gen_gain: float32 [1024], replicated, may hold values from 0.25 to 1.75
- gen_in: bfloat16 [1024, 40], replicated, may hold values from -0.1875 to 0.1875
- gen_out: float32 [40, 4, 9], replicated, may hold values from -1 to 1
- gen_bias: float32 [4, 9], replicated, may hold values from -3 to 3
- norm_gain: float32 [2, 1024], replicated, may hold values from 0.25 to 1.75
- norm_bias: float32 [2, 1024], replicated, may hold values from -2 to 2
- w_in: bfloat16 [1024, 7, 1024], P('seq'), may hold values from -0.1875 to 0.1875
- in_bias: float32 [7, 1024], replicated, may hold values from -2 to 2
- w_out: bfloat16 [1024, 1024], P('seq'), may hold values from -0.75 to 0.75
- w_down: bfloat16 [1024, 4096], P('seq'), may hold values from -0.09375 to 0.09375
- out_bias: float32 [1024], replicated, may hold values from -2 to 2
Outputs:
- new_state: bfloat16 [1024, 4096], P('seq', 'dp')
- history_grad: bfloat16 [9, 1024, 4096], P(None, 'seq', 'dp')
- mix_mean: float32 [4, 9], replicated
- mix_var: float32 [4, 9], replicated
- gen_gain_grad: float32 [1024], replicated
- gen_in_grad: float32 [1024, 40], replicated
- gen_out_grad: float32 [40, 4, 9], replicated
- gen_bias_grad: float32 [4, 9], replicated
- norm_gain_grad: float32 [2, 1024], replicated
- norm_bias_grad: float32 [2, 1024], replicated
- w_in_grad: float32 [1024, 7, 1024], P('seq')
- in_bias_grad: float32 [7, 1024], replicated
- w_out_grad: float32 [1024, 1024], P('seq')
- w_down_grad: float32 [1024, 4096], P('seq')
- out_bias_grad: float32 [1024], replicated
The draws below stay inside these ranges and needn't reach their ends.
Inputs may be any that keep to these rules, and one draw needn't show every extreme that they name: `bucket_len`: the two buckets of one token block together hold 128 tokens. Each bucket's valid tokens are its first valid_len tokens, at least one and at most the bucket's length.
All inputs are finite; a program needn't handle non-finite values.
Results may differ from the reference program's by a relative error of at most 0.015.
Values may be sent and summed in bfloat16 or wider, within the bound.
A program may use at most 256 MiB of HBM per device.

```python
import math
import jax
import jax.numpy as jnp
from jax import lax

D = 1024
HEADS = 16
HEAD_DIM = 64
ROT = 16
FF = 4096
GEN_HID = 40
STATES = 9
STREAMS = 4
TOK_DEV = 128
TOKENS = 4096
N_SEQ = 8
N_DP = 4


def bucket_pair(key):
    base_key = jax.random.fold_in(key, 41)
    key_len, key_valid = jax.random.split(base_key)
    first_len = jax.random.randint(key_len, (N_DP, N_SEQ), TOK_DEV // 4, 3 * TOK_DEV // 4 + 1, dtype=jnp.int32)
    first_len = first_len.at[N_DP - 1, N_SEQ - 1].set(3 * TOK_DEV // 4)
    lengths = jnp.stack([first_len, TOK_DEV - first_len], axis=-1)
    device_rank = jnp.arange(N_DP, dtype=jnp.int32)[:, None] + N_DP * jnp.arange(N_SEQ, dtype=jnp.int32)[None, :]
    denominator = max(N_DP * N_SEQ - 1, 1)
    ceiling = lengths * (denominator + 2 * device_rank[:, :, None]) // (3 * denominator)
    ceiling = jnp.maximum(ceiling, 1)
    lowered = jax.random.randint(key_valid, (N_DP, N_SEQ, 2), 0, ceiling // 2 + 1, dtype=jnp.int32)
    counts = ceiling - lowered
    counts = counts.at[N_DP - 1, N_SEQ - 1].set(lengths[N_DP - 1, N_SEQ - 1])
    return (lengths, counts)


def draw_bucket_len(key, part):
    lengths, counts = bucket_pair(key)
    return lengths


def draw_valid_len(key, part):
    lengths, counts = bucket_pair(key)
    return counts


def shard_levels(key, shape, cuts, smallest, largest):
    loudness = 1.0
    for axis_at, blocks in cuts:
        draws = jax.random.uniform(jax.random.fold_in(jax.random.fold_in(key, 6), axis_at), (blocks,), jnp.float32, smallest / len(cuts), largest / len(cuts))
        loudness = loudness * jnp.repeat(jnp.exp(draws), shape[axis_at] // blocks).reshape((-1,) + (1,) * (len(shape) - 1 - axis_at))
    return loudness


def noise(own_key, shape, scale, bound, cuts=(), held_as=jnp.bfloat16):
    values = scale * jax.random.normal(own_key, shape, jnp.float32)
    if cuts:
        values = values * shard_levels(own_key, shape, cuts, -0.22, 0.18)
    return jnp.clip(values, -bound, bound).astype(held_as)


def setup_inputs(seed: int = 0) -> dict:
    key_list = jax.random.split(jax.random.key(seed), 16)
    return {
        "history": noise(key_list[0], (STATES, D, TOKENS), 1.0, 6.0, ((1, 8), (2, 4))),
        "cotangent": noise(key_list[1], (D, TOKENS), 1.0, 6.0, ((0, 8), (1, 4))),
        "bucket_len": draw_bucket_len(jax.random.fold_in(key_list[15], 71), 0),
        "valid_len": draw_valid_len(jax.random.fold_in(key_list[15], 71), 0),
        "gen_gain": jnp.clip(1.0 + 0.15 * jax.random.normal(key_list[4], (D,), jnp.float32), 0.25, 1.75),
        "gen_in": noise(key_list[5], (D, GEN_HID), D ** -0.5, 0.1875),
        "gen_out": noise(key_list[6], (GEN_HID, STREAMS, STATES), GEN_HID ** -0.5, 1.0, (), jnp.float32),
        "gen_bias": noise(key_list[7], (STREAMS, STATES), 0.5, 3.0, (), jnp.float32),
        "norm_gain": jnp.clip(1.0 + 0.15 * jax.random.normal(key_list[8], (2, D), jnp.float32), 0.25, 1.75),
        "norm_bias": noise(key_list[9], (2, D), 0.3, 2.0, (), jnp.float32),
        "w_in": noise(key_list[10], (D, 7, D), D ** -0.5, 0.1875, ((0, 8),)),
        "in_bias": noise(key_list[11], (7, D), 0.3, 2.0, (), jnp.float32),
        "w_out": noise(key_list[12], (D, D), (D // 16) ** -0.5, 0.75, ((0, 8),)),
        "w_down": noise(key_list[13], (D, FF), FF ** -0.5, 0.09375, ((0, 8),)),
        "out_bias": noise(key_list[14], (D,), 0.3, 2.0, (), jnp.float32),
    }


@jax.custom_vjp
def low(v):
    return lax.optimization_barrier(v.astype(jnp.bfloat16)).astype(jnp.float32)

@jax.custom_vjp
def low_back(v):
    return v

def low_keep(v):
    return (low(v), None)

def low_pass(kept, grad):
    return (grad,)

def back_keep(v):
    return (v, None)

def back_low(kept, grad):
    return (low(grad),)
low.defvjp(low_keep, low_pass)
low_back.defvjp(back_keep, back_low)
ln_eps = 1e-05
rms_eps = 1e-06
masked_score = -1e+30
highest = lax.Precision.HIGHEST

def gelu_exact(values):
    return jax.nn.gelu(values, approximate=False)

def rotary_tables(position):
    freq_index = jnp.arange(ROT // 2, dtype=jnp.float32)
    inverse_freq = jnp.exp(freq_index * (-2.0 * math.log(10000.0) / ROT))
    angles = position.astype(jnp.float32)[:, None] * inverse_freq[None, :]
    return (jnp.cos(angles), jnp.sin(angles))

def rotate(values, cosine, sine):
    half = ROT // 2
    former = values[..., :half]
    latter = values[..., half:ROT]
    cos_heads = cosine[:, None, :]
    sin_heads = sine[:, None, :]
    return jnp.concatenate([former * cos_heads - latter * sin_heads, latter * cos_heads + former * sin_heads, values[..., ROT:]], axis=-1)

def token_layout(lengths, counts):
    index = jnp.arange(TOK_DEV, dtype=jnp.int32)[None, :]
    second = index >= lengths[:, 0:1]
    position = index - jnp.where(second, lengths[:, 0:1], 0)
    valid = position < jnp.where(second, counts[:, 1:2], counts[:, 0:1])
    return (second, position, valid)

def layer_norm(stream, gain, bias):
    centre = lax.optimization_barrier(jnp.mean(stream, axis=-1, keepdims=True))
    centred = stream - centre
    spread = lax.optimization_barrier(jnp.mean(centred * centred, axis=-1, keepdims=True))
    return centred * lax.rsqrt(spread + ln_eps) * gain + bias

def attend(block):
    queries, keys, values, second, valid = block
    index = jnp.arange(TOK_DEV, dtype=jnp.int32)
    allowed = (second[:, None] == second[None, :]) & (index[None, :] <= index[:, None]) & valid[None, :]
    scores = low_back(jnp.einsum('qhd,khd->hqk', queries, keys, precision=highest))
    scores = jnp.where(allowed[None], scores, masked_score)
    top = lax.optimization_barrier(jnp.max(scores, axis=-1, keepdims=True))
    weights = jnp.exp(scores - top)
    probs = low(weights / lax.optimization_barrier(jnp.sum(weights, axis=-1, keepdims=True)))
    return jnp.einsum('hqk,khd->qhd', probs, values, precision=highest)

def forward(params, history, layout):
    gen_gain, gen_in, gen_out, gen_bias, norm_gain, norm_bias, w_in, in_bias, w_out, w_down, out_bias = params
    second, position, valid = layout
    group_blocks = second.shape[0]
    tokens = group_blocks * TOK_DEV
    last = history[STATES - 1]
    rms = lax.rsqrt(lax.optimization_barrier(jnp.mean(last * last, axis=-1, keepdims=True)) + rms_eps)
    gen_pre = low_back(jnp.dot(low(last * rms * gen_gain), gen_in, precision=highest))
    gen_hidden = gelu_exact(gen_pre)
    mixing = jnp.einsum('th,hsj->tsj', gen_hidden, gen_out, precision=highest) + gen_bias
    streams = jnp.einsum('tsj,jtd->std', mixing, history, precision=highest)
    normed_attn = low(layer_norm(streams[:3], norm_gain[0], norm_bias[0]))
    normed_mlp = low(layer_norm(streams[3], norm_gain[1], norm_bias[1]))
    proj_attn = low_back(jnp.einsum('stk,nsk->stn', normed_attn, w_in[:, :3], precision=highest)) + in_bias[:3, None, :]
    proj_mlp = low_back(jnp.einsum('tk,njk->jtn', normed_mlp, w_in[:, 3:], precision=highest)) + in_bias[3:, None, :]
    cosine, sine = rotary_tables(position.reshape(tokens))
    heads_shape = (tokens, HEADS, HEAD_DIM)
    queries = low(rotate(proj_attn[0].reshape(heads_shape), cosine, sine) * HEAD_DIM ** (-0.5))
    keys = low(rotate(proj_attn[1].reshape(heads_shape), cosine, sine))
    values = low(proj_attn[2].reshape(heads_shape))
    block_shape = (group_blocks, TOK_DEV, HEADS, HEAD_DIM)
    attended = lax.map(jax.checkpoint(attend), (queries.reshape(block_shape), keys.reshape(block_shape), values.reshape(block_shape), second, valid))
    attn_out = low(low_back(attended.reshape(tokens, D)))
    gelu_up = low(gelu_exact(proj_mlp))
    branch = jnp.einsum('tk,nk->tn', attn_out, w_out, precision=highest)
    branch = branch + jnp.einsum('jtk,njk->tn', gelu_up, w_down.reshape(D, 4, D), precision=highest)
    return (streams[3] + branch + out_bias, mixing)

def reference(history, cotangent, bucket_len, valid_len, gen_gain, gen_in, gen_out, gen_bias, norm_gain, norm_bias, w_in, in_bias, w_out, w_down, out_bias):
    blocks = N_DP * N_SEQ
    per_group = math.gcd(blocks, 16)
    groups = blocks // per_group
    span = per_group * TOK_DEV
    params = tuple((item.astype(jnp.float32) for item in (gen_gain, gen_in, gen_out, gen_bias, norm_gain, norm_bias, w_in, in_bias, w_out, w_down, out_bias)))
    history_rows = jnp.swapaxes(history, 1, 2)
    cotangent_rows = cotangent.T
    hist_groups = jnp.moveaxis(history_rows.reshape(STATES, groups, span, D), 1, 0)
    cot_groups = cotangent_rows.reshape(groups, span, D)
    len_groups = bucket_len.reshape(groups, per_group, 2).astype(jnp.int32)
    valid_groups = valid_len.reshape(groups, per_group, 2).astype(jnp.int32)
    zero_grads = tuple((jnp.zeros(item.shape, jnp.float32) for item in params))
    zero_stats = (jnp.zeros((STREAMS, STATES), jnp.float32), jnp.zeros((STREAMS, STATES), jnp.float32), jnp.zeros((), jnp.float32))

    def group_step(carry, inputs):
        grads, stats = carry
        hist_group, cot_group, len_group, valid_group = inputs
        layout = token_layout(len_group, valid_group)

        def apply_layer(param_list, hist_float):
            return forward(param_list, hist_float, layout)
        output, pullback, mixing = jax.vjp(apply_layer, params, hist_group.astype(jnp.float32), has_aux=True)
        token_mask = layout[2].reshape(span).astype(jnp.float32)
        param_grads, hist_grad = pullback(cot_group.astype(jnp.float32) * token_mask[:, None])
        grads = jax.tree.map(jnp.add, grads, param_grads)
        weighted = mixing * token_mask[:, None, None]
        stats = (stats[0] + lax.optimization_barrier(jnp.sum(weighted, axis=0)), stats[1] + lax.optimization_barrier(jnp.sum(weighted * mixing, axis=0)), stats[2] + jnp.sum(token_mask))
        return ((grads, stats), (output.astype(jnp.bfloat16), hist_grad.astype(jnp.bfloat16)))
    (grads, stats), (outputs, hist_grads) = lax.scan(group_step, (zero_grads, zero_stats), (hist_groups, cot_groups, len_groups, valid_groups))
    new_state = outputs.reshape(TOKENS, D).T
    history_grad = jnp.swapaxes(jnp.moveaxis(hist_grads, 0, 1).reshape(STATES, TOKENS, D), 1, 2)
    mix_mean = stats[0] / stats[2]
    mix_var = stats[1] / stats[2] - mix_mean * mix_mean
    gen_gain_grad, gen_in_grad, gen_out_grad, gen_bias_grad, norm_gain_grad, norm_bias_grad, w_in_grad, in_bias_grad, w_out_grad, w_down_grad, out_bias_grad = grads
    return (new_state, history_grad, mix_mean, mix_var, gen_gain_grad, gen_in_grad, gen_out_grad, gen_bias_grad, norm_gain_grad, norm_bias_grad, w_in_grad, in_bias_grad, w_out_grad, w_down_grad, out_bias_grad)
```

```python
import math

import jax
import jax.numpy as jnp
from jax import lax
from jax.sharding import PartitionSpec as P

HEADS = 16
HEAD_DIM = 64
ROT = 16


ln_eps = 1e-05
rms_eps = 1e-06
masked_score = -1e30
highest = lax.Precision.HIGHEST


def gelu_exact(values):
    return jax.nn.gelu(values, approximate=False)


def rotary_tables(position):
    freq_index = jnp.arange(ROT // 2, dtype=jnp.float32)
    inverse_freq = jnp.exp(freq_index * (-2.0 * math.log(10000.0) / ROT))
    angles = position.astype(jnp.float32)[:, None] * inverse_freq[None, :]
    return (jnp.cos(angles), jnp.sin(angles))


def rotate(values, cosine, sine):
    half = ROT // 2
    former = values[..., :half]
    latter = values[..., half:ROT]
    cos_heads = cosine[:, None, :]
    sin_heads = sine[:, None, :]
    return jnp.concatenate(
        [
            former * cos_heads - latter * sin_heads,
            latter * cos_heads + former * sin_heads,
            values[..., ROT:],
        ],
        axis=-1,
    )


def token_layout(lengths, counts, tokens):
    index = jnp.arange(tokens, dtype=jnp.int32)
    second = index >= lengths[0]
    position = index - jnp.where(second, lengths[0], 0)
    valid = position < jnp.where(second, counts[1], counts[0])
    return (second, position, valid)


def normalize(streams):
    centre = jnp.mean(streams, axis=-1, keepdims=True)
    centred = streams - centre
    inverse = lax.rsqrt(jnp.mean(centred * centred, axis=-1, keepdims=True) + ln_eps)
    return (centred * inverse, inverse)


def normalize_back(grad_scaled, scaled, inverse):
    mean_grad = jnp.mean(grad_scaled, axis=-1, keepdims=True)
    mean_along = jnp.mean(grad_scaled * scaled, axis=-1, keepdims=True)
    return inverse * (grad_scaled - mean_grad - scaled * mean_along)


def per_device(
    history,
    cotangent,
    bucket_len,
    valid_len,
    gen_gain,
    gen_in,
    gen_out,
    gen_bias,
    norm_gain,
    norm_bias,
    w_in,
    in_bias,
    w_out,
    w_down,
    out_bias,
):
    states = history.shape[0]
    stacked = jnp.concatenate([history, cotangent[None]], axis=0)
    arrived = lax.all_to_all(stacked, "seq", split_axis=2, concat_axis=1, tiled=True)
    arrived_rows = jnp.swapaxes(arrived, 1, 2)
    hist_local = arrived_rows[:states]
    cot_local = arrived_rows[states]
    tokens = hist_local.shape[1]
    width = hist_local.shape[2]
    second, position, valid = token_layout(bucket_len.reshape(2), valid_len.reshape(2), tokens)
    valid_float = valid.astype(jnp.float32)
    last = hist_local[states - 1].astype(jnp.float32)
    rms = lax.rsqrt(jnp.mean(last * last, axis=-1, keepdims=True) + rms_eps)
    gen_normed = (last * rms * gen_gain).astype(jnp.bfloat16)
    gen_pre = jnp.dot(gen_normed, gen_in, preferred_element_type=jnp.float32)
    gen_hidden, gen_pull = jax.vjp(gelu_exact, gen_pre)
    mixing = jnp.einsum("th,hsj->tsj", gen_hidden, gen_out, precision=highest) + gen_bias
    weighted = mixing * valid_float[:, None, None]
    stat_sums = jnp.sum(weighted, axis=0)
    stat_squares = jnp.sum(weighted * mixing, axis=0)
    stat_count = jnp.sum(valid_float)
    streams = mixing[:, :, 0].T[:, :, None] * hist_local[0]
    for state in range(1, states):
        streams = streams + mixing[:, :, state].T[:, :, None] * hist_local[state]
    scaled, inverse = normalize(streams)
    normed_attn = (scaled[:3] * norm_gain[0] + norm_bias[0]).astype(jnp.bfloat16)
    normed_mlp = (scaled[3] * norm_gain[1] + norm_bias[1]).astype(jnp.bfloat16)
    piece = lax.all_gather(w_in, "seq", axis=0, tiled=True)
    attn_part = jnp.einsum(
        "stk,nsk->stn", normed_attn, piece[:, :3], preferred_element_type=jnp.float32
    )
    mlp_part = jnp.einsum(
        "tk,njk->jtn", normed_mlp, piece[:, 3:], preferred_element_type=jnp.float32
    )
    projected = jnp.concatenate([attn_part, mlp_part], axis=0) + in_bias[:, None, :]
    cosine, sine = rotary_tables(position)
    heads_shape = (tokens, HEADS, HEAD_DIM)
    queries = (rotate(projected[0].reshape(heads_shape), cosine, sine) * HEAD_DIM ** (-0.5)).astype(
        jnp.bfloat16
    )
    keys = rotate(projected[1].reshape(heads_shape), cosine, sine).astype(jnp.bfloat16)
    values = projected[2].reshape(heads_shape).astype(jnp.bfloat16)
    index = jnp.arange(tokens, dtype=jnp.int32)
    allowed = (
        (second[:, None] == second[None, :]) & (index[None, :] <= index[:, None]) & valid[None, :]
    )
    scores = jnp.einsum("qhd,khd->hqk", queries, keys, preferred_element_type=jnp.float32)
    scores = jnp.where(allowed[None], scores, masked_score)
    top = jnp.max(scores, axis=-1, keepdims=True)
    weights = jnp.exp(scores - top)
    weight_total = jnp.sum(weights, axis=-1, keepdims=True)
    log_total = top + jnp.log(weight_total)
    probs_low = (weights / weight_total).astype(jnp.bfloat16)
    attended = jnp.einsum("hqk,khd->qhd", probs_low, values, preferred_element_type=jnp.float32)
    attn_low = attended.reshape(tokens, width).astype(jnp.bfloat16)
    gelu_up, up_pull = jax.vjp(gelu_exact, projected[3:])
    gelu_low = gelu_up.astype(jnp.bfloat16)
    grad_out_low = jnp.where(valid[:, None], cot_local, jnp.zeros_like(cot_local))
    piece_out, piece_down = lax.all_gather((w_out, w_down), "seq", axis=0, tiled=True)
    down_part = piece_down.reshape(piece_down.shape[0], 4, width)
    result = jnp.einsum("tk,nk->tn", attn_low, piece_out, preferred_element_type=jnp.float32)
    branch = result + jnp.einsum(
        "jtk,njk->tn", gelu_low, down_part, preferred_element_type=jnp.float32
    )
    new_local = (streams[3] + branch + out_bias).astype(jnp.bfloat16)
    piece_out = lax.all_gather(w_out, "seq", axis=0, tiled=True)
    piece_down = lax.all_gather(w_down, "seq", axis=0, tiled=True)
    count = piece_out.shape[0]
    part = grad_out_low
    attn_add = jnp.einsum("tn,nk->tk", part, piece_out, preferred_element_type=jnp.float32)
    gelu_add = jnp.einsum(
        "tn,njk->jtk", part, piece_down.reshape(count, 4, width), preferred_element_type=jnp.float32
    )
    grad_attn = attn_add
    part = grad_out_low
    term_out = jnp.einsum("tn,tk->nk", part, attn_low, preferred_element_type=jnp.float32)
    term_down = jnp.einsum(
        "tn,jtk->njk", part, gelu_low, preferred_element_type=jnp.float32
    ).reshape(lax.axis_size("seq") * w_out.shape[0], 4 * width)
    out_grads = lax.psum_scatter(
        jnp.concatenate([term_out, term_down], axis=1).astype(jnp.bfloat16),
        "seq",
        scatter_dimension=0,
        tiled=True,
    )
    out_bias_grad = jnp.sum(grad_out_low.astype(jnp.float32), axis=0)
    grad_attended = grad_attn.astype(jnp.bfloat16).reshape(heads_shape)
    rescored = jnp.einsum("qhd,khd->hqk", queries, keys, preferred_element_type=jnp.float32)
    probs = jnp.where(allowed[None], jnp.exp(rescored - log_total), 0.0)
    grad_values = jnp.einsum(
        "hqk,qhd->khd",
        probs.astype(jnp.bfloat16),
        grad_attended,
        preferred_element_type=jnp.float32,
    )
    grad_probs = jnp.einsum(
        "qhd,khd->hqk", grad_attended, values, preferred_element_type=jnp.float32
    )
    grad_scores = (
        probs * (grad_probs - jnp.sum(probs * grad_probs, axis=-1, keepdims=True))
    ).astype(jnp.bfloat16)
    grad_queries = jnp.einsum(
        "hqk,khd->qhd", grad_scores, keys, preferred_element_type=jnp.float32
    ) * HEAD_DIM ** (-0.5)
    grad_keys = jnp.einsum("hqk,qhd->khd", grad_scores, queries, preferred_element_type=jnp.float32)
    grad_up = up_pull(gelu_add)[0]
    grad_proj = jnp.concatenate(
        [
            rotate(grad_queries, cosine, -sine).reshape(1, tokens, width),
            rotate(grad_keys, cosine, -sine).reshape(1, tokens, width),
            grad_values.reshape(1, tokens, width),
            grad_up,
        ],
        axis=0,
    )
    in_bias_grad = jnp.sum(grad_proj, axis=1)
    grad_proj_low = grad_proj.astype(jnp.bfloat16)
    piece = lax.all_gather(w_in, "seq", axis=0, tiled=True)
    part = grad_proj_low
    attn_add = jnp.einsum(
        "stn,nsk->stk", part[:3], piece[:, :3], preferred_element_type=jnp.float32
    )
    mlp_add = jnp.einsum("jtn,njk->tk", part[3:], piece[:, 3:], preferred_element_type=jnp.float32)
    part = grad_proj_low
    attn_term = jnp.einsum(
        "stn,stk->nsk", part[:3], normed_attn, preferred_element_type=jnp.float32
    )
    mlp_term = jnp.einsum("jtn,tk->njk", part[3:], normed_mlp, preferred_element_type=jnp.float32)
    in_grads = lax.psum_scatter(
        jnp.concatenate([attn_term, mlp_term], axis=1).astype(jnp.bfloat16),
        "seq",
        scatter_dimension=0,
        tiled=True,
    )
    norm_gain_grad = jnp.stack(
        [jnp.sum(attn_add * scaled[:3], axis=(0, 1)), jnp.sum(mlp_add * scaled[3], axis=0)]
    )
    norm_bias_grad = jnp.stack([jnp.sum(attn_add, axis=(0, 1)), jnp.sum(mlp_add, axis=0)])
    grad_attn_streams = normalize_back(attn_add * norm_gain[0], scaled[:3], inverse[:3])
    grad_mlp_stream = normalize_back(
        mlp_add * norm_gain[1], scaled[3], inverse[3]
    ) + grad_out_low.astype(jnp.float32)
    grad_streams = jnp.concatenate([grad_attn_streams, grad_mlp_stream[None]], axis=0)
    grad_mixing = jnp.stack(
        [
            jnp.einsum(
                "std,td->ts", grad_streams, hist_local[state].astype(jnp.float32), precision=highest
            )
            for state in range(states)
        ],
        axis=-1,
    )
    hist_terms = [
        jnp.einsum("ts,std->td", mixing[:, :, state], grad_streams, precision=highest)
        for state in range(states)
    ]
    gen_bias_grad = jnp.sum(grad_mixing, axis=0)
    gen_out_grad = jnp.einsum("th,tsj->hsj", gen_hidden, grad_mixing, precision=highest)
    grad_hidden = jnp.einsum("tsj,hsj->th", grad_mixing, gen_out, precision=highest)
    grad_pre_low = gen_pull(grad_hidden)[0].astype(jnp.bfloat16)
    gen_in_grad = jnp.einsum(
        "tk,th->kh", gen_normed, grad_pre_low, preferred_element_type=jnp.float32
    )
    grad_gen = jnp.einsum("th,kh->tk", grad_pre_low, gen_in, preferred_element_type=jnp.float32)
    gen_gain_grad = jnp.sum(grad_gen * last * rms, axis=0)
    gained = grad_gen * gen_gain
    grad_last = rms * gained - last * (rms * rms * rms) * jnp.mean(
        gained * last, axis=-1, keepdims=True
    )
    hist_stack = jnp.stack(hist_terms[: states - 1] + [hist_terms[states - 1] + grad_last]).astype(
        jnp.bfloat16
    )
    departing = jnp.swapaxes(jnp.concatenate([new_local[None], hist_stack], axis=0), 1, 2)
    returned = lax.all_to_all(departing, "seq", split_axis=1, concat_axis=2, tiled=True)
    w_in_grad, out_total = (
        lax.psum(in_grads, "dp").astype(jnp.float32),
        lax.psum(out_grads, "dp").astype(jnp.float32),
    )
    w_out_grad = out_total[:, :width]
    w_down_grad = out_total[:, width:]
    joined = lax.psum(
        (
            gen_gain_grad,
            gen_in_grad,
            gen_out_grad,
            gen_bias_grad,
            norm_gain_grad,
            norm_bias_grad,
            in_bias_grad,
            out_bias_grad,
            stat_sums,
            stat_squares,
            stat_count,
        ),
        ("seq", "dp"),
    )
    small_totals = joined[:8]
    stat_totals = joined[8:]
    mix_mean = stat_totals[0] / stat_totals[2]
    mix_var = stat_totals[1] / stat_totals[2] - mix_mean * mix_mean
    return (
        returned[0],
        returned[1:],
        mix_mean,
        mix_var,
        small_totals[0],
        small_totals[1],
        small_totals[2],
        small_totals[3],
        small_totals[4],
        small_totals[5],
        w_in_grad,
        small_totals[6],
        w_out_grad,
        w_down_grad,
        small_totals[7],
    )


def tp_device(
    history, cotangent, bucket_len, valid_len, gen_gain, gen_in, gen_out, gen_bias,
    norm_gain, norm_bias, w_in, in_bias, w_out, w_down, out_bias,
):
    f32, bf16 = jnp.float32, jnp.bfloat16
    n = lax.axis_size("seq")
    me = lax.axis_index("seq")
    states, feats, tokens = history.shape
    width = n * feats
    block = tokens // n
    heads = feats // HEAD_DIM

    def local(array, axis):
        return lax.dynamic_slice_in_dim(array, me * feats, feats, axis)

    def sum_feats(part):
        return lax.psum(part, "seq")

    lens = lax.all_gather(
        jnp.concatenate([bucket_len.reshape(2), valid_len.reshape(2)]), "seq"
    )
    index = jnp.arange(block, dtype=jnp.int32)[None, :]
    second = index >= lens[:, 0:1]
    position = index - jnp.where(second, lens[:, 0:1], 0)
    valid = position < jnp.where(second, lens[:, 3:4], lens[:, 2:3])
    valid_float = valid.reshape(tokens).astype(f32)
    cot_all = lax.all_gather(cotangent, "seq", axis=0, tiled=True)
    grad_out = jnp.where(valid.reshape(1, tokens), cot_all, jnp.zeros_like(cot_all))
    grad_out_local = jnp.where(valid.reshape(1, tokens), cotangent, jnp.zeros_like(cotangent))
    rows = jnp.concatenate([w_out[:, None], w_down.reshape(feats, 4, width)], axis=1)
    cols = lax.all_to_all(
        rows.reshape(feats, 5, n, feats), "seq", split_axis=2, concat_axis=0, tiled=True
    ).reshape(width, 5, feats)
    last = history[states - 1].astype(f32)
    gain_l = local(gen_gain, 0)[:, None]
    gen_in_l = local(gen_in, 0)
    lg = (last * gain_l).astype(bf16)
    part = jnp.einsum("dh,dt->ht", gen_in_l, lg, preferred_element_type=f32)
    part = sum_feats(jnp.concatenate([part, jnp.sum(last * last, axis=0, keepdims=True)], axis=0))
    raw, square = part[:-1], part[-1:]
    rms = lax.rsqrt(square / width + rms_eps)
    gen_pre = raw * rms
    gen_hidden, gen_pull = jax.vjp(gelu_exact, gen_pre)
    out_flat = gen_out.reshape(gen_out.shape[0], 4 * states)
    mixing = jnp.einsum("hm,ht->mt", out_flat, gen_hidden, precision=highest) + gen_bias.reshape(-1, 1)
    weighted = mixing * valid_float
    stat_sums = jnp.sum(weighted, axis=1)
    stat_squares = jnp.sum(weighted * mixing, axis=1)
    stat_count = jnp.sum(valid_float)
    mix = mixing.reshape(4, states, 1, tokens)
    streams = mix[:, 0] * history[0]
    for state in range(1, states):
        streams = streams + mix[:, state] * history[state]
    mean_l = jnp.mean(streams, axis=1)
    m2_l = jnp.sum((streams - mean_l[:, None]) ** 2, axis=1)
    both = lax.all_gather(jnp.stack([mean_l, m2_l]), "seq")
    centre = jnp.mean(both[:, 0], axis=0)
    m2 = jnp.sum(both[:, 1] + feats * (both[:, 0] - centre) ** 2, axis=0)
    inverse = lax.rsqrt(m2 / width + ln_eps)[:, None]
    scaled = (streams - centre[:, None]) * inverse
    which = jnp.array([0, 0, 0, 1])
    ng = local(norm_gain, 1)[which][:, :, None]
    nb = local(norm_bias, 1)[which][:, :, None]
    normed = lax.all_gather((scaled * ng + nb).astype(bf16), "seq", axis=1, tiled=True)
    slot_stream = [0, 1, 2, 3, 3, 3, 3]
    proj = jnp.stack(
        [jnp.dot(w_in[:, s], normed[slot_stream[s]], preferred_element_type=f32) for s in range(7)]
    ) + local(in_bias, 1)[:, :, None]
    cosine, sine = rotary_tables(position.reshape(tokens))
    cosine, sine = cosine.T, sine.T

    def rot(value, sine):
        value = value.reshape(heads, HEAD_DIM, tokens)
        a, b, rest = value[:, :8], value[:, 8:16], value[:, 16:]
        return jnp.concatenate([a * cosine - b * sine, b * cosine + a * sine, rest], axis=1)

    scale = HEAD_DIM ** (-0.5)
    shape = (heads, HEAD_DIM, n, block)
    queries = (rot(proj[0], sine) * scale).astype(bf16).reshape(shape)
    keys = rot(proj[1], sine).astype(bf16).reshape(shape)
    values = proj[2].astype(bf16).reshape(shape)
    ar = jnp.arange(block, dtype=jnp.int32)
    allowed = (
        (second[:, :, None] == second[:, None, :])
        & (ar[:, None] <= ar[None, :])
        & valid[:, :, None]
    )
    scores = jnp.einsum("hdbk,hdbq->hbkq", keys, queries, preferred_element_type=f32)
    scores = jnp.where(allowed, scores, masked_score)
    top = jnp.max(scores, axis=2, keepdims=True)
    weights = jnp.exp(scores - top)
    probs = jnp.where(allowed, weights / jnp.sum(weights, axis=2, keepdims=True), 0.0)
    probs_low = probs.astype(bf16)
    attended = jnp.einsum("hdbk,hbkq->hdbq", values, probs_low, preferred_element_type=f32)
    attn_low = attended.astype(bf16).reshape(feats, tokens)
    gelu_up, up_pull = jax.vjp(gelu_exact, proj[3:])
    act = jnp.concatenate([attn_low[None], gelu_up.astype(bf16)], axis=0)
    branch = jnp.einsum("njk,jkt->nt", cols, act, preferred_element_type=f32)
    branch = lax.psum_scatter(branch.astype(bf16), "seq", scatter_dimension=0, tiled=True)
    new_state = (streams[3] + branch.astype(f32) + local(out_bias, 0)[:, None]).astype(bf16)
    back = jnp.einsum("njk,nt->jkt", cols, grad_out, preferred_element_type=f32)
    col_grads = jnp.einsum("nt,jkt->njk", grad_out, act, preferred_element_type=f32).astype(bf16)
    row_grads = lax.all_to_all(
        col_grads.reshape(n, feats, 5, feats), "seq", split_axis=0, concat_axis=3, tiled=True
    ).reshape(feats, 5 * width)
    row_grads = lax.psum(row_grads, "dp").astype(f32)
    grad_attn = back[0].astype(bf16).reshape(shape)
    grad_values = jnp.einsum("hbkq,hdbq->hdbk", probs_low, grad_attn, preferred_element_type=f32)
    dprob = jnp.einsum("hdbk,hdbq->hbkq", values, grad_attn, preferred_element_type=f32)
    grad_scores = (probs * (dprob - jnp.sum(probs * dprob, axis=2, keepdims=True))).astype(bf16)
    grad_queries = jnp.einsum("hdbk,hbkq->hdbq", keys, grad_scores, preferred_element_type=f32) * scale
    grad_keys = jnp.einsum("hdbq,hbkq->hdbk", queries, grad_scores, preferred_element_type=f32)
    flat = (feats, tokens)
    grad_proj = jnp.concatenate(
        [
            rot(grad_queries.reshape(flat), -sine).reshape((1,) + flat),
            rot(grad_keys.reshape(flat), -sine).reshape((1,) + flat),
            grad_values.reshape((1,) + flat),
            up_pull(back[1:])[0],
        ],
        axis=0,
    )
    in_bias_grad = jnp.sum(grad_proj, axis=2)
    low = grad_proj.astype(bf16)
    w_in_grad = jnp.stack(
        [
            jnp.einsum("nt,kt->nk", low[s], normed[slot_stream[s]], preferred_element_type=f32)
            for s in range(7)
        ],
        axis=1,
    )
    w_in_grad = lax.psum(w_in_grad.astype(bf16), "dp").astype(f32)
    grad_normed = jnp.concatenate(
        [
            jnp.einsum("nsk,snt->skt", w_in[:, :3], low[:3], preferred_element_type=f32),
            jnp.einsum("njk,jnt->kt", w_in[:, 3:], low[3:], preferred_element_type=f32)[None],
        ],
        axis=0,
    ).astype(bf16)
    grad_normed = lax.psum_scatter(grad_normed, "seq", scatter_dimension=1, tiled=True).astype(f32)
    gx = jnp.sum(grad_normed * scaled, axis=2)
    gs = jnp.sum(grad_normed, axis=2)
    norm_gain_grad = jnp.stack([gx[0] + gx[1] + gx[2], gx[3]])
    norm_bias_grad = jnp.stack([gs[0] + gs[1] + gs[2], gs[3]])
    g = grad_normed * ng
    means = sum_feats(jnp.stack([jnp.sum(g, axis=1), jnp.sum(g * scaled, axis=1)])) / width
    grad_streams = inverse * (g - means[0][:, None] - scaled * means[1][:, None])
    grad_streams = grad_streams.at[3].add(grad_out_local.astype(f32))
    grad_mixing = sum_feats(
        jnp.stack(
            [jnp.sum(grad_streams * history[j].astype(f32), axis=1) for j in range(states)], axis=1
        ).reshape(4 * states, tokens)
    )
    gen_bias_grad = jnp.sum(grad_mixing, axis=1)
    gen_out_grad = jnp.einsum("ht,mt->hm", gen_hidden, grad_mixing, precision=highest)
    grad_hidden = jnp.einsum("hm,mt->ht", out_flat, grad_mixing, precision=highest)
    grad_pre = gen_pull(grad_hidden)[0].astype(bf16)
    gen_normed = (last * rms * gain_l).astype(bf16)
    gen_in_grad = jnp.einsum("dt,ht->dh", gen_normed, grad_pre, preferred_element_type=f32)
    grad_gen = jnp.einsum("dh,ht->dt", gen_in_l, grad_pre, preferred_element_type=f32)
    gen_gain_grad = jnp.sum(grad_gen * last * rms, axis=1)
    mz = jnp.sum(grad_pre.astype(f32) * raw, axis=0, keepdims=True) / width
    hist_terms = []
    for j in range(states):
        term = jnp.sum(mix[:, j] * grad_streams, axis=0)
        if j == states - 1:
            term = term + rms * grad_gen * gain_l - last * (rms * rms * rms) * mz
        hist_terms.append(term.astype(bf16))
    history_grad = jnp.stack(hist_terms)
    out_bias_grad = jnp.sum(grad_out_local.astype(f32), axis=1)
    vec = jnp.concatenate(
        [
            in_bias_grad, norm_gain_grad, norm_bias_grad, gen_gain_grad[None],
            out_bias_grad[None], gen_in_grad.T,
        ],
        axis=0,
    )
    vec = lax.all_gather(lax.psum(vec, "dp"), "seq", axis=1, tiled=True)
    shared = lax.psum(
        jnp.concatenate(
            [gen_out_grad.reshape(-1), gen_bias_grad, stat_sums, stat_squares, stat_count[None]]
        ),
        "dp",
    )
    m = 4 * states
    hid = gen_out.shape[0]
    count = shared[-1]
    mix_mean = shared[hid * m + m : hid * m + 2 * m] / count
    mix_var = shared[hid * m + 2 * m : hid * m + 3 * m] / count - mix_mean * mix_mean
    return (
        new_state, history_grad,
        mix_mean.reshape(4, states), mix_var.reshape(4, states),
        vec[11], vec[13:].T, shared[: hid * m].reshape(hid, 4, states),
        shared[hid * m : hid * m + m].reshape(4, states),
        vec[7:9], vec[9:11], w_in_grad, vec[0:7],
        row_grads[:, :width], row_grads[:, width:], vec[12],
    )


def solution(mesh):
    in_specs = (
        P(None, "seq", "dp"),
        P("seq", "dp"),
        P("dp", "seq", None),
        P("dp", "seq", None),
        P(),
        P(),
        P(),
        P(),
        P(),
        P(),
        P("seq", None, None),
        P(),
        P("seq", None),
        P("seq", None),
        P(),
    )
    out_specs = (
        P("seq", "dp"),
        P(None, "seq", "dp"),
        P(),
        P(),
        P(),
        P(),
        P(),
        P(),
        P(),
        P(),
        P("seq", None, None),
        P(),
        P("seq", None),
        P("seq", None),
        P(),
    )
    split_heads = HEADS % mesh.shape["seq"] == 0
    body = tp_device if split_heads else per_device
    return jax.shard_map(
        body, mesh=mesh, in_specs=in_specs, out_specs=out_specs, check_vma=False
    )
```

```python
import functools
import math

import jax
import jax.numpy as jnp
from jax import lax
from jax.experimental import pallas as pl
from jax.experimental.pallas import tpu as pltpu
from jax.sharding import PartitionSpec as P

HEADS = 16
HEAD_DIM = 64
ROT = 16


ln_eps = 1e-05
rms_eps = 1e-06
masked_score = -1e30
highest = lax.Precision.HIGHEST


def gelu_exact(values):
    return jax.nn.gelu(values, approximate=False)


def rotary_tables(position):
    freq_index = jnp.arange(ROT // 2, dtype=jnp.float32)
    inverse_freq = jnp.exp(freq_index * (-2.0 * math.log(10000.0) / ROT))
    angles = position.astype(jnp.float32)[:, None] * inverse_freq[None, :]
    return (jnp.cos(angles), jnp.sin(angles))


def rotate(values, cosine, sine):
    half = ROT // 2
    former = values[..., :half]
    latter = values[..., half:ROT]
    cos_heads = cosine[:, None, :]
    sin_heads = sine[:, None, :]
    return jnp.concatenate(
        [
            former * cos_heads - latter * sin_heads,
            latter * cos_heads + former * sin_heads,
            values[..., ROT:],
        ],
        axis=-1,
    )


def token_layout(lengths, counts, tokens):
    index = jnp.arange(tokens, dtype=jnp.int32)
    second = index >= lengths[0]
    position = index - jnp.where(second, lengths[0], 0)
    valid = position < jnp.where(second, counts[1], counts[0])
    return (second, position, valid)


def normalize(streams):
    centre = jnp.mean(streams, axis=-1, keepdims=True)
    centred = streams - centre
    inverse = lax.rsqrt(jnp.mean(centred * centred, axis=-1, keepdims=True) + ln_eps)
    return (centred * inverse, inverse)


def normalize_back(grad_scaled, scaled, inverse):
    mean_grad = jnp.mean(grad_scaled, axis=-1, keepdims=True)
    mean_along = jnp.mean(grad_scaled * scaled, axis=-1, keepdims=True)
    return inverse * (grad_scaled - mean_grad - scaled * mean_along)


def per_device(
    history,
    cotangent,
    bucket_len,
    valid_len,
    gen_gain,
    gen_in,
    gen_out,
    gen_bias,
    norm_gain,
    norm_bias,
    w_in,
    in_bias,
    w_out,
    w_down,
    out_bias,
):
    states = history.shape[0]
    stacked = jnp.concatenate([history, cotangent[None]], axis=0)
    arrived = lax.all_to_all(stacked, "seq", split_axis=2, concat_axis=1, tiled=True)
    arrived_rows = jnp.swapaxes(arrived, 1, 2)
    hist_local = arrived_rows[:states]
    cot_local = arrived_rows[states]
    tokens = hist_local.shape[1]
    width = hist_local.shape[2]
    second, position, valid = token_layout(bucket_len.reshape(2), valid_len.reshape(2), tokens)
    valid_float = valid.astype(jnp.float32)
    last = hist_local[states - 1].astype(jnp.float32)
    rms = lax.rsqrt(jnp.mean(last * last, axis=-1, keepdims=True) + rms_eps)
    gen_normed = (last * rms * gen_gain).astype(jnp.bfloat16)
    gen_pre = jnp.dot(gen_normed, gen_in, preferred_element_type=jnp.float32)
    gen_hidden, gen_pull = jax.vjp(gelu_exact, gen_pre)
    mixing = jnp.einsum("th,hsj->tsj", gen_hidden, gen_out, precision=highest) + gen_bias
    weighted = mixing * valid_float[:, None, None]
    stat_sums = jnp.sum(weighted, axis=0)
    stat_squares = jnp.sum(weighted * mixing, axis=0)
    stat_count = jnp.sum(valid_float)
    streams = mixing[:, :, 0].T[:, :, None] * hist_local[0]
    for state in range(1, states):
        streams = streams + mixing[:, :, state].T[:, :, None] * hist_local[state]
    scaled, inverse = normalize(streams)
    normed_attn = (scaled[:3] * norm_gain[0] + norm_bias[0]).astype(jnp.bfloat16)
    normed_mlp = (scaled[3] * norm_gain[1] + norm_bias[1]).astype(jnp.bfloat16)
    piece = lax.all_gather(w_in, "seq", axis=0, tiled=True)
    attn_part = jnp.einsum(
        "stk,nsk->stn", normed_attn, piece[:, :3], preferred_element_type=jnp.float32
    )
    mlp_part = jnp.einsum(
        "tk,njk->jtn", normed_mlp, piece[:, 3:], preferred_element_type=jnp.float32
    )
    projected = jnp.concatenate([attn_part, mlp_part], axis=0) + in_bias[:, None, :]
    cosine, sine = rotary_tables(position)
    heads_shape = (tokens, HEADS, HEAD_DIM)
    queries = (rotate(projected[0].reshape(heads_shape), cosine, sine) * HEAD_DIM ** (-0.5)).astype(
        jnp.bfloat16
    )
    keys = rotate(projected[1].reshape(heads_shape), cosine, sine).astype(jnp.bfloat16)
    values = projected[2].reshape(heads_shape).astype(jnp.bfloat16)
    index = jnp.arange(tokens, dtype=jnp.int32)
    allowed = (
        (second[:, None] == second[None, :]) & (index[None, :] <= index[:, None]) & valid[None, :]
    )
    scores = jnp.einsum("qhd,khd->hqk", queries, keys, preferred_element_type=jnp.float32)
    scores = jnp.where(allowed[None], scores, masked_score)
    top = jnp.max(scores, axis=-1, keepdims=True)
    weights = jnp.exp(scores - top)
    weight_total = jnp.sum(weights, axis=-1, keepdims=True)
    log_total = top + jnp.log(weight_total)
    probs_low = (weights / weight_total).astype(jnp.bfloat16)
    attended = jnp.einsum("hqk,khd->qhd", probs_low, values, preferred_element_type=jnp.float32)
    attn_low = attended.reshape(tokens, width).astype(jnp.bfloat16)
    gelu_up, up_pull = jax.vjp(gelu_exact, projected[3:])
    gelu_low = gelu_up.astype(jnp.bfloat16)
    grad_out_low = jnp.where(valid[:, None], cot_local, jnp.zeros_like(cot_local))
    piece_out, piece_down = lax.all_gather((w_out, w_down), "seq", axis=0, tiled=True)
    down_part = piece_down.reshape(piece_down.shape[0], 4, width)
    result = jnp.einsum("tk,nk->tn", attn_low, piece_out, preferred_element_type=jnp.float32)
    branch = result + jnp.einsum(
        "jtk,njk->tn", gelu_low, down_part, preferred_element_type=jnp.float32
    )
    new_local = (streams[3] + branch + out_bias).astype(jnp.bfloat16)
    piece_out = lax.all_gather(w_out, "seq", axis=0, tiled=True)
    piece_down = lax.all_gather(w_down, "seq", axis=0, tiled=True)
    count = piece_out.shape[0]
    part = grad_out_low
    attn_add = jnp.einsum("tn,nk->tk", part, piece_out, preferred_element_type=jnp.float32)
    gelu_add = jnp.einsum(
        "tn,njk->jtk", part, piece_down.reshape(count, 4, width), preferred_element_type=jnp.float32
    )
    grad_attn = attn_add
    part = grad_out_low
    term_out = jnp.einsum("tn,tk->nk", part, attn_low, preferred_element_type=jnp.float32)
    term_down = jnp.einsum(
        "tn,jtk->njk", part, gelu_low, preferred_element_type=jnp.float32
    ).reshape(lax.axis_size("seq") * w_out.shape[0], 4 * width)
    out_grads = lax.psum_scatter(
        jnp.concatenate([term_out, term_down], axis=1).astype(jnp.bfloat16),
        "seq",
        scatter_dimension=0,
        tiled=True,
    )
    out_bias_grad = jnp.sum(grad_out_low.astype(jnp.float32), axis=0)
    grad_attended = grad_attn.astype(jnp.bfloat16).reshape(heads_shape)
    rescored = jnp.einsum("qhd,khd->hqk", queries, keys, preferred_element_type=jnp.float32)
    probs = jnp.where(allowed[None], jnp.exp(rescored - log_total), 0.0)
    grad_values = jnp.einsum(
        "hqk,qhd->khd",
        probs.astype(jnp.bfloat16),
        grad_attended,
        preferred_element_type=jnp.float32,
    )
    grad_probs = jnp.einsum(
        "qhd,khd->hqk", grad_attended, values, preferred_element_type=jnp.float32
    )
    grad_scores = (
        probs * (grad_probs - jnp.sum(probs * grad_probs, axis=-1, keepdims=True))
    ).astype(jnp.bfloat16)
    grad_queries = jnp.einsum(
        "hqk,khd->qhd", grad_scores, keys, preferred_element_type=jnp.float32
    ) * HEAD_DIM ** (-0.5)
    grad_keys = jnp.einsum("hqk,qhd->khd", grad_scores, queries, preferred_element_type=jnp.float32)
    grad_up = up_pull(gelu_add)[0]
    grad_proj = jnp.concatenate(
        [
            rotate(grad_queries, cosine, -sine).reshape(1, tokens, width),
            rotate(grad_keys, cosine, -sine).reshape(1, tokens, width),
            grad_values.reshape(1, tokens, width),
            grad_up,
        ],
        axis=0,
    )
    in_bias_grad = jnp.sum(grad_proj, axis=1)
    grad_proj_low = grad_proj.astype(jnp.bfloat16)
    piece = lax.all_gather(w_in, "seq", axis=0, tiled=True)
    part = grad_proj_low
    attn_add = jnp.einsum(
        "stn,nsk->stk", part[:3], piece[:, :3], preferred_element_type=jnp.float32
    )
    mlp_add = jnp.einsum("jtn,njk->tk", part[3:], piece[:, 3:], preferred_element_type=jnp.float32)
    part = grad_proj_low
    attn_term = jnp.einsum(
        "stn,stk->nsk", part[:3], normed_attn, preferred_element_type=jnp.float32
    )
    mlp_term = jnp.einsum("jtn,tk->njk", part[3:], normed_mlp, preferred_element_type=jnp.float32)
    in_grads = lax.psum_scatter(
        jnp.concatenate([attn_term, mlp_term], axis=1).astype(jnp.bfloat16),
        "seq",
        scatter_dimension=0,
        tiled=True,
    )
    norm_gain_grad = jnp.stack(
        [jnp.sum(attn_add * scaled[:3], axis=(0, 1)), jnp.sum(mlp_add * scaled[3], axis=0)]
    )
    norm_bias_grad = jnp.stack([jnp.sum(attn_add, axis=(0, 1)), jnp.sum(mlp_add, axis=0)])
    grad_attn_streams = normalize_back(attn_add * norm_gain[0], scaled[:3], inverse[:3])
    grad_mlp_stream = normalize_back(
        mlp_add * norm_gain[1], scaled[3], inverse[3]
    ) + grad_out_low.astype(jnp.float32)
    grad_streams = jnp.concatenate([grad_attn_streams, grad_mlp_stream[None]], axis=0)
    grad_mixing = jnp.stack(
        [
            jnp.einsum(
                "std,td->ts", grad_streams, hist_local[state].astype(jnp.float32), precision=highest
            )
            for state in range(states)
        ],
        axis=-1,
    )
    hist_terms = [
        jnp.einsum("ts,std->td", mixing[:, :, state], grad_streams, precision=highest)
        for state in range(states)
    ]
    gen_bias_grad = jnp.sum(grad_mixing, axis=0)
    gen_out_grad = jnp.einsum("th,tsj->hsj", gen_hidden, grad_mixing, precision=highest)
    grad_hidden = jnp.einsum("tsj,hsj->th", grad_mixing, gen_out, precision=highest)
    grad_pre_low = gen_pull(grad_hidden)[0].astype(jnp.bfloat16)
    gen_in_grad = jnp.einsum(
        "tk,th->kh", gen_normed, grad_pre_low, preferred_element_type=jnp.float32
    )
    grad_gen = jnp.einsum("th,kh->tk", grad_pre_low, gen_in, preferred_element_type=jnp.float32)
    gen_gain_grad = jnp.sum(grad_gen * last * rms, axis=0)
    gained = grad_gen * gen_gain
    grad_last = rms * gained - last * (rms * rms * rms) * jnp.mean(
        gained * last, axis=-1, keepdims=True
    )
    hist_stack = jnp.stack(hist_terms[: states - 1] + [hist_terms[states - 1] + grad_last]).astype(
        jnp.bfloat16
    )
    departing = jnp.swapaxes(jnp.concatenate([new_local[None], hist_stack], axis=0), 1, 2)
    returned = lax.all_to_all(departing, "seq", split_axis=1, concat_axis=2, tiled=True)
    w_in_grad, out_total = (
        lax.psum(in_grads, "dp").astype(jnp.float32),
        lax.psum(out_grads, "dp").astype(jnp.float32),
    )
    w_out_grad = out_total[:, :width]
    w_down_grad = out_total[:, width:]
    joined = lax.psum(
        (
            gen_gain_grad,
            gen_in_grad,
            gen_out_grad,
            gen_bias_grad,
            norm_gain_grad,
            norm_bias_grad,
            in_bias_grad,
            out_bias_grad,
            stat_sums,
            stat_squares,
            stat_count,
        ),
        ("seq", "dp"),
    )
    small_totals = joined[:8]
    stat_totals = joined[8:]
    mix_mean = stat_totals[0] / stat_totals[2]
    mix_var = stat_totals[1] / stat_totals[2] - mix_mean * mix_mean
    return (
        returned[0],
        returned[1:],
        mix_mean,
        mix_var,
        small_totals[0],
        small_totals[1],
        small_totals[2],
        small_totals[3],
        small_totals[4],
        small_totals[5],
        w_in_grad,
        small_totals[6],
        w_out_grad,
        w_down_grad,
        small_totals[7],
    )


MESH = pl.DeviceIdType.MESH
HIDDEN_ROWS = 40
ROOT_HALF = math.sqrt(0.5)
INV_ROOT_2PI = 1.0 / math.sqrt(2.0 * math.pi)


def gelu_pair(x):
    half = 0.5 + 0.5 * lax.erf(x * ROOT_HALF)
    return x * half, half + x * (jnp.exp(-0.5 * x * x) * INV_ROOT_2PI)


def contract(a, b, dim_a, dim_b, precision=None):
    return lax.dot_general(
        a, b, (((dim_a,), (dim_b,)), ((), ())),
        precision=precision, preferred_element_type=jnp.float32,
    )


class Links:
    def __init__(self, n):
        self.n = n
        self.me = lax.axis_index("seq")
        core = self.me % 2
        xbit = (self.me // 2) % 2
        ybit = (self.me // 4) % 2
        flip = 1 - 2 * core
        x = self.me + 2 - 4 * xbit
        y = self.me + 4 - 8 * ybit
        self.core = core
        self.a = x * (1 - core) + y * core
        self.b = y * (1 - core) + x * core
        self.dg = x + y - self.me
        self.p = self.me + flip
        self.pa = self.b + flip
        self.pb = self.a + flip
        self.pdg = self.dg + flip

    def greet(self):
        barrier = pltpu.get_barrier_semaphore()
        for k in range(1, self.n):
            pl.semaphore_signal(
                barrier, inc=1, device_id={"seq": (self.me + k) % self.n}, device_id_type=MESH
            )
        pl.semaphore_wait(barrier, self.n - 1)

    def copy(self, src, dst, send, recv, to):
        return pltpu.make_async_remote_copy(
            src_ref=src, dst_ref=dst, send_sem=send, recv_sem=recv,
            device_id={"seq": to}, device_id_type=MESH,
        )


class Gather:
    def __init__(self, links, place, send, recv):
        self.links, self.place, self.send, self.recv = links, place, send, recv

    def _go(self, src, owner, slot, index, to):
        self.links.copy(
            src, self.place(owner), self.send.at[slot], self.recv.at[index], to
        ).start()

    def _got(self, owner, index):
        place = self.place(owner)
        self.links.copy(place, place, self.send.at[0], self.recv.at[index], self.links.p).wait_recv()

    def start(self, src):
        at = self.links
        self._go(src, at.me, 0, 0, at.a)
        self._go(src, at.me, 1, 1, at.b)
        self._go(src, at.me, 2, 3, at.p)

    def near(self):
        at = self.links
        self._got(at.a, 0)
        self._go(self.place(at.a), at.a, 3, 2, at.b)
        self._go(self.place(at.a), at.a, 4, 4, at.p)
        self._got(at.b, 1)
        self._go(self.place(at.b), at.b, 5, 5, at.p)

    def far(self):
        at = self.links
        self._got(at.dg, 2)
        self._go(self.place(at.dg), at.dg, 6, 6, at.p)

    def other(self):
        at = self.links
        for owner, index in ((at.p, 3), (at.pa, 4), (at.pb, 5), (at.pdg, 6)):
            self._got(owner, index)

    def drain(self):
        place = self.place(self.links.me)
        for slot in range(7):
            self.links.copy(
                place, place, self.send.at[slot], self.recv.at[0], self.links.p
            ).wait_send()


class Everyone:
    def __init__(self, links, source, target, arrived, send, recv):
        self.links, self.source, self.target, self.arrived = links, source, target, arrived
        self.send, self.recv = send, recv

    def start(self):
        at = self.links
        for k in range(1, at.n):
            to = (at.me + k) % at.n
            at.copy(
                self.source(to), self.target(k), self.send.at[k], self.recv.at[k], to
            ).start()

    def wait(self, k):
        at = self.links
        origin = (at.me + at.n - k) % at.n
        place = self.arrived(k, origin)
        at.copy(place, place, self.send.at[k], self.recv.at[k], at.p).wait_recv()
        return origin

    def drain(self):
        at = self.links
        for k in range(1, at.n):
            to = (at.me + k) % at.n
            place = self.source(to)
            at.copy(place, place, self.send.at[k], self.recv.at[k], at.p).wait_send()


def front_kernel(
    n,
    hist, cot, lens, vals, gain, gin, gout, gbias, ng, nb, w_out, w_down,
    nbuf, cot_all, cols, pk, raw_out, scaled, st3, stat_out,
    prm, colp, part, part_in, stat, stat_in, streams, nown,
    ex_send, ex_recv, ag_send, ag_recv, local_sem,
):
    f32, bf16 = jnp.float32, jnp.bfloat16
    states, feats, tokens = hist.shape
    block = tokens // n
    width = n * feats
    hid = gin.shape[0]
    at = Links(n)
    me = at.me
    mine = pl.ds(pl.multiple_of(me * feats, feats), feats)

    def rows(owner):
        return pl.ds(pl.multiple_of(owner * feats, feats), feats)

    def lanes(owner):
        return pl.ds(pl.multiple_of(owner * block, block), block)

    gathers = [
        Gather(at, lambda owner, s=s: nbuf.at[s, rows(owner), :], ag_send.at[s], ag_recv.at[s])
        for s in range(4)
    ]
    cots = Gather(at, lambda owner: cot_all.at[rows(owner), :], ag_send.at[4], ag_recv.at[4])
    parts = Everyone(
        at, lambda to: part.at[to], lambda k: part_in.at[k], lambda k, origin: part_in.at[k],
        ex_send.at[0], ex_recv.at[0],
    )
    mixes = Everyone(
        at, lambda to: pk.at[me], lambda k: pk.at[me], lambda k, origin: pk.at[origin],
        ex_send.at[1], ex_recv.at[1],
    )
    stats = Everyone(
        at, lambda to: stat, lambda k: stat_in.at[me], lambda k, origin: stat_in.at[origin],
        ex_send.at[2], ex_recv.at[2],
    )

    at.greet()
    cots.start(cot)
    keep_cot = pltpu.make_async_copy(cot, cot_all.at[mine, :], local_sem.at[0])
    keep_cot.start()

    prm[...] = jnp.zeros_like(prm)
    prm[0:1, :] = gain[:, mine]
    prm[1:3, :] = ng[:, mine]
    prm[3:5, :] = nb[:, mine]
    colp[...] = prm[...].T
    gin_mine = gin[:, mine]
    for b in range(n):
        last = hist[states - 1, :, b * block : (b + 1) * block].astype(f32)
        product = (last * colp[:, 0:1]).astype(bf16)
        part[b, 0:hid, :] = jnp.dot(gin_mine, product, preferred_element_type=f32)
        part[b, hid : hid + 8, :] = jnp.broadcast_to(
            jnp.sum(last * last, axis=0, keepdims=True), (8, block)
        )
    parts.start()
    total = part[me]
    for k in range(1, n):
        parts.wait(k)
        total = total + part_in[k]
    raw_out[...] = total
    rms = lax.rsqrt(total[hid : hid + 1] * (1.0 / width) + rms_eps)
    hidden, _ = gelu_pair(total[0:hid] * rms)
    table = jnp.concatenate([gout[j] for j in range(states)], axis=0)
    mixing = jnp.dot(table, hidden, precision=highest, preferred_element_type=f32)
    for j in range(states):
        pk[me, 4 * j : 4 * j + 4, :] = mixing[4 * j : 4 * j + 4] + gbias[:, j : j + 1]
    row = 4 * states
    pk[me, row : row + 1, :] = rms
    for offset, value in ((1, lens[0, 0, 0]), (2, vals[0, 0, 0]), (3, vals[0, 0, 1])):
        pk[me, row + offset : row + offset + 1, :] = jnp.full((1, block), value.astype(f32))
    mixes.start()

    def column_copies(to, send, recv):
        out = []
        for j in range(5):
            if j == 0:
                src = w_out.at[:, rows(to)]
            else:
                src = w_down.at[:, pl.ds(pl.multiple_of((j - 1) * width + to * feats, feats), feats)]
            out.append((src, cols.at[mine, pl.ds(j * feats, feats)]))
        return out

    for k in range(1, n):
        to = (me + k) % n
        for src, dst in column_copies(to, None, None):
            at.copy(src, dst, ex_send.at[3, k], ex_recv.at[3, k], to).start()
    own_cols = [
        pltpu.make_async_copy(src, dst, local_sem.at[1 + j])
        for j, (src, dst) in enumerate(column_copies(me, None, None))
    ]
    for copy in own_cols:
        copy.start()
    cots.near()

    def mix_block(owner):
        where = lanes(owner)
        for half in range(2):
            part_rows = pl.ds(half * (feats // 2), feats // 2)
            sums = [None] * 4
            for j in range(states):
                value = hist[j, part_rows, where].astype(f32)
                for s in range(4):
                    weight = pk[owner, pl.ds(4 * j + s, 1), :]
                    term = weight * value
                    sums[s] = term if sums[s] is None else sums[s] + term
            for s in range(4):
                streams[s, part_rows, where] = sums[s]
        for s in range(4):
            value = streams[s, :, where]
            mean = jnp.sum(value, axis=0, keepdims=True) * (1.0 / feats)
            off = value - mean
            stat[pl.ds(s, 1), where] = mean
            stat[pl.ds(4 + s, 1), where] = jnp.sum(off * off, axis=0, keepdims=True)

    mix_block(me)

    @pl.loop(1, n)
    def _(k):
        mix_block(mixes.wait(k))

    stats.start()
    cots.far()
    for k in range(1, n):
        stats.wait(k)
    stat_in[me] = stat[...]
    means = stat_in[0, 0:4, :]
    for k in range(1, n):
        means = means + stat_in[k, 0:4, :]
    means = means * (1.0 / n)
    spread = jnp.zeros_like(means)
    for k in range(n):
        away = stat_in[k, 0:4, :] - means
        spread = spread + (stat_in[k, 4:8, :] + feats * (away * away))
    stat_out[0:4, :] = means
    stat_out[4:8, :] = lax.rsqrt(spread * (1.0 / width) + ln_eps)

    keeps = []
    for s in range(4):
        which = 0 if s < 3 else 1
        for b in range(n):
            where = pl.ds(b * block, block)
            xhat = (streams[s, :, where] - stat_out[s : s + 1, where]) * stat_out[4 + s : 5 + s, where]
            scaled[s, :, where] = xhat
            nown[s, :, where] = (
                xhat * colp[:, 1 + which : 2 + which] + colp[:, 3 + which : 4 + which]
            ).astype(bf16)
        gathers[s].start(nown.at[s])
        keep = pltpu.make_async_copy(nown.at[s], nbuf.at[s, mine, :], local_sem.at[6 + s])
        keep.start()
        keeps.append(keep)
    st3[...] = streams[3]
    for s in range(4):
        gathers[s].near()
        if s >= 1:
            gathers[s - 1].far()
    gathers[3].far()
    for g in [cots] + gathers:
        g.other()
    for k in range(1, n):
        place = cols.at[rows((me + n - k) % n), :]
        at.copy(place, place, ex_send.at[3, k], ex_recv.at[3, k], at.p).wait()
    for g in [cots] + gathers:
        g.drain()
    for exchange in (parts, mixes, stats):
        exchange.drain()
    keep_cot.wait()
    for copy in own_cols + keeps:
        copy.wait()


def front(n, history, cotangent, bucket_len, valid_len, gen_gain, gen_in, gen_out, gen_bias, norm_gain, norm_bias, w_out, w_down):
    f32, bf16 = jnp.float32, jnp.bfloat16
    states, feats, tokens = history.shape
    block = tokens // n
    width = n * feats
    hid = gen_in.shape[1]
    vmem = pl.BlockSpec(memory_space=pltpu.VMEM)
    smem = pl.BlockSpec(memory_space=pltpu.SMEM)
    anys = pl.BlockSpec(memory_space=pl.ANY)
    shape = jax.ShapeDtypeStruct
    return pl.pallas_call(
        functools.partial(front_kernel, n),
        out_shape=(
            shape((4, width, tokens), bf16),
            shape((width, tokens), bf16),
            shape((width, 5 * feats), bf16),
            shape((n, 40, block), f32),
            shape((hid + 8, block), f32),
            shape((4, feats, tokens), f32),
            shape((feats, tokens), f32),
            shape((8, tokens), f32),
        ),
        in_specs=[vmem, vmem, smem, smem] + [vmem] * 6 + [anys] * 2,
        out_specs=(anys, anys, anys, vmem, vmem, vmem, vmem, vmem),
        scratch_shapes=[
            pltpu.VMEM((feats, feats), f32),
            pltpu.VMEM((feats, feats), f32),
            pltpu.VMEM((n, hid + 8, block), f32),
            pltpu.VMEM((n, hid + 8, block), f32),
            pltpu.VMEM((8, tokens), f32),
            pltpu.VMEM((n, 8, tokens), f32),
            pltpu.VMEM((4, feats, tokens), f32),
            pltpu.VMEM((4, feats, tokens), bf16),
            pltpu.SemaphoreType.DMA((4, n)),
            pltpu.SemaphoreType.DMA((4, n)),
            pltpu.SemaphoreType.DMA((5, 7)),
            pltpu.SemaphoreType.DMA((5, 7)),
            pltpu.SemaphoreType.DMA((10,)),
        ],
        compiler_params=pltpu.CompilerParams(
            collective_id=1, has_side_effects=True, vmem_limit_bytes=60 * 2**20
        ),
        name="front",
    )(
        history, cotangent, bucket_len, valid_len, gen_gain.reshape(1, width), gen_in.T,
        gen_out.transpose(2, 1, 0), gen_bias, norm_gain, norm_bias, w_out, w_down,
    )


def tp_device(
    history, cotangent, bucket_len, valid_len, gen_gain, gen_in, gen_out, gen_bias,
    norm_gain, norm_bias, w_in, in_bias, w_out, w_down, out_bias,
):
    f32, bf16 = jnp.float32, jnp.bfloat16
    n = lax.axis_size("seq")
    me = lax.axis_index("seq")
    states, feats, tokens = history.shape
    width = n * feats
    block = tokens // n
    heads = feats // HEAD_DIM

    def local(array, axis):
        return lax.dynamic_slice_in_dim(array, me * feats, feats, axis)

    def sum_feats(part):
        return lax.psum(part, "seq")

    normed, cot_all, cols, pk, own, scaled, stream3, stat = front(
        n, history, cotangent, bucket_len, valid_len, gen_gain, gen_in, gen_out, gen_bias,
        norm_gain, norm_bias, w_out, w_down,
    )
    cols = cols.reshape(width, 5, feats)
    m = 4 * states
    hid = gen_out.shape[0]
    index = jnp.arange(block, dtype=jnp.int32)[None, :].astype(f32)
    second = index >= pk[:, m + 1]
    position = index - jnp.where(second, pk[:, m + 1], 0.0)
    valid = position < jnp.where(second, pk[:, m + 3], pk[:, m + 2])
    valid_float = valid.reshape(tokens).astype(f32)
    grad_out = jnp.where(valid.reshape(1, tokens), cot_all, jnp.zeros_like(cot_all))
    grad_out_local = jnp.where(valid.reshape(1, tokens), cotangent, jnp.zeros_like(cotangent))
    last = history[states - 1].astype(f32)
    gain_l = local(gen_gain, 0)[:, None]
    gen_in_l = local(gen_in, 0)
    mixing = jnp.swapaxes(pk[:, :m], 0, 1).reshape(m, tokens)
    rms = pk[:, m].reshape(1, tokens)
    raw = lax.all_gather(own[:hid], "seq", axis=1, tiled=True)
    gen_pre = raw * rms
    gen_hidden, gen_pull = jax.vjp(gelu_exact, gen_pre)
    out_flat = gen_out.transpose(0, 2, 1).reshape(hid, m)
    weighted = mixing * valid_float
    stat_sums = jnp.sum(weighted, axis=1)
    stat_squares = jnp.sum(weighted * mixing, axis=1)
    stat_count = jnp.sum(valid_float)
    mix = mixing.reshape(states, 4, 1, tokens).swapaxes(0, 1)
    streams = [None, None, None, stream3]
    inverse = stat[4:, None]
    which = jnp.array([0, 0, 0, 1])
    ng = local(norm_gain, 1)[which][:, :, None]
    slot_stream = [0, 1, 2, 3, 3, 3, 3]
    proj = jnp.stack(
        [jnp.dot(w_in[:, s], normed[slot_stream[s]], preferred_element_type=f32) for s in range(7)]
    ) + local(in_bias, 1)[:, :, None]
    cosine, sine = rotary_tables(position.reshape(tokens))
    cosine, sine = cosine.T, sine.T

    def rot(value, sine):
        value = value.reshape(heads, HEAD_DIM, tokens)
        a, b, rest = value[:, :8], value[:, 8:16], value[:, 16:]
        return jnp.concatenate([a * cosine - b * sine, b * cosine + a * sine, rest], axis=1)

    scale = HEAD_DIM ** (-0.5)
    shape = (heads, HEAD_DIM, n, block)
    queries = (rot(proj[0], sine) * scale).astype(bf16).reshape(shape)
    keys = rot(proj[1], sine).astype(bf16).reshape(shape)
    values = proj[2].astype(bf16).reshape(shape)
    ar = jnp.arange(block, dtype=jnp.int32)
    allowed = (
        (second[:, :, None] == second[:, None, :])
        & (ar[:, None] <= ar[None, :])
        & valid[:, :, None]
    )
    scores = jnp.einsum("hdbk,hdbq->hbkq", keys, queries, preferred_element_type=f32)
    scores = jnp.where(allowed, scores, masked_score)
    top = jnp.max(scores, axis=2, keepdims=True)
    weights = jnp.exp(scores - top)
    probs = jnp.where(allowed, weights / jnp.sum(weights, axis=2, keepdims=True), 0.0)
    probs_low = probs.astype(bf16)
    attended = jnp.einsum("hdbk,hbkq->hdbq", values, probs_low, preferred_element_type=f32)
    attn_low = attended.astype(bf16).reshape(feats, tokens)
    gelu_up, up_pull = jax.vjp(gelu_exact, proj[3:])
    act = jnp.concatenate([attn_low[None], gelu_up.astype(bf16)], axis=0)
    branch = jnp.einsum("njk,jkt->nt", cols, act, preferred_element_type=f32)
    branch = lax.psum_scatter(branch.astype(bf16), "seq", scatter_dimension=0, tiled=True)
    new_state = (streams[3] + branch.astype(f32) + local(out_bias, 0)[:, None]).astype(bf16)
    back = jnp.einsum("njk,nt->jkt", cols, grad_out, preferred_element_type=f32)
    col_grads = jnp.einsum("nt,jkt->njk", grad_out, act, preferred_element_type=f32).astype(bf16)
    row_grads = lax.all_to_all(
        col_grads.reshape(n, feats, 5, feats), "seq", split_axis=0, concat_axis=3, tiled=True
    ).reshape(feats, 5 * width)
    row_grads = lax.psum(row_grads, "dp").astype(f32)
    grad_attn = back[0].astype(bf16).reshape(shape)
    grad_values = jnp.einsum("hbkq,hdbq->hdbk", probs_low, grad_attn, preferred_element_type=f32)
    dprob = jnp.einsum("hdbk,hdbq->hbkq", values, grad_attn, preferred_element_type=f32)
    grad_scores = (probs * (dprob - jnp.sum(probs * dprob, axis=2, keepdims=True))).astype(bf16)
    grad_queries = jnp.einsum("hdbk,hbkq->hdbq", keys, grad_scores, preferred_element_type=f32) * scale
    grad_keys = jnp.einsum("hdbq,hbkq->hdbk", queries, grad_scores, preferred_element_type=f32)
    flat = (feats, tokens)
    grad_proj = jnp.concatenate(
        [
            rot(grad_queries.reshape(flat), -sine).reshape((1,) + flat),
            rot(grad_keys.reshape(flat), -sine).reshape((1,) + flat),
            grad_values.reshape((1,) + flat),
            up_pull(back[1:])[0],
        ],
        axis=0,
    )
    in_bias_grad = jnp.sum(grad_proj, axis=2)
    low = grad_proj.astype(bf16)
    w_in_grad = jnp.stack(
        [
            jnp.einsum("nt,kt->nk", low[s], normed[slot_stream[s]], preferred_element_type=f32)
            for s in range(7)
        ],
        axis=1,
    )
    w_in_grad = lax.psum(w_in_grad.astype(bf16), "dp").astype(f32)
    grad_normed = jnp.concatenate(
        [
            jnp.einsum("nsk,snt->skt", w_in[:, :3], low[:3], preferred_element_type=f32),
            jnp.einsum("njk,jnt->kt", w_in[:, 3:], low[3:], preferred_element_type=f32)[None],
        ],
        axis=0,
    ).astype(bf16)
    grad_normed = lax.psum_scatter(grad_normed, "seq", scatter_dimension=1, tiled=True).astype(f32)
    gx = jnp.sum(grad_normed * scaled, axis=2)
    gs = jnp.sum(grad_normed, axis=2)
    norm_gain_grad = jnp.stack([gx[0] + gx[1] + gx[2], gx[3]])
    norm_bias_grad = jnp.stack([gs[0] + gs[1] + gs[2], gs[3]])
    g = grad_normed * ng
    means = sum_feats(jnp.stack([jnp.sum(g, axis=1), jnp.sum(g * scaled, axis=1)])) / width
    grad_streams = inverse * (g - means[0][:, None] - scaled * means[1][:, None])
    grad_streams = grad_streams.at[3].add(grad_out_local.astype(f32))
    grad_mixing = sum_feats(
        jnp.stack(
            [jnp.sum(grad_streams * history[j].astype(f32), axis=1) for j in range(states)], axis=0
        ).reshape(4 * states, tokens)
    )
    gen_bias_grad = jnp.sum(grad_mixing, axis=1)
    gen_out_grad = jnp.einsum("ht,mt->hm", gen_hidden, grad_mixing, precision=highest)
    grad_hidden = jnp.einsum("hm,mt->ht", out_flat, grad_mixing, precision=highest)
    grad_pre = gen_pull(grad_hidden)[0].astype(bf16)
    gen_normed = (last * rms * gain_l).astype(bf16)
    gen_in_grad = jnp.einsum("dt,ht->dh", gen_normed, grad_pre, preferred_element_type=f32)
    grad_gen = jnp.einsum("dh,ht->dt", gen_in_l, grad_pre, preferred_element_type=f32)
    gen_gain_grad = jnp.sum(grad_gen * last * rms, axis=1)
    mz = jnp.sum(grad_pre.astype(f32) * raw, axis=0, keepdims=True) / width
    hist_terms = []
    for j in range(states):
        term = jnp.sum(mix[:, j] * grad_streams, axis=0)
        if j == states - 1:
            term = term + rms * grad_gen * gain_l - last * (rms * rms * rms) * mz
        hist_terms.append(term.astype(bf16))
    history_grad = jnp.stack(hist_terms)
    out_bias_grad = jnp.sum(grad_out_local.astype(f32), axis=1)
    vec = jnp.concatenate(
        [
            in_bias_grad, norm_gain_grad, norm_bias_grad, gen_gain_grad[None],
            out_bias_grad[None], gen_in_grad.T,
        ],
        axis=0,
    )
    vec = lax.all_gather(lax.psum(vec, "dp"), "seq", axis=1, tiled=True)
    shared = lax.psum(
        jnp.concatenate(
            [gen_out_grad.reshape(-1), gen_bias_grad, stat_sums, stat_squares, stat_count[None]]
        ),
        "dp",
    )
    count = shared[-1]
    mix_mean = shared[hid * m + m : hid * m + 2 * m] / count
    mix_var = shared[hid * m + 2 * m : hid * m + 3 * m] / count - mix_mean * mix_mean
    return (
        new_state, history_grad,
        mix_mean.reshape(states, 4).T, mix_var.reshape(states, 4).T,
        vec[11], vec[13:].T, shared[: hid * m].reshape(hid, states, 4).swapaxes(1, 2),
        shared[hid * m : hid * m + m].reshape(states, 4).T,
        vec[7:9], vec[9:11], w_in_grad, vec[0:7],
        row_grads[:, :width], row_grads[:, width:], vec[12],
    )


def solution(mesh):
    in_specs = (
        P(None, "seq", "dp"),
        P("seq", "dp"),
        P("dp", "seq", None),
        P("dp", "seq", None),
        P(),
        P(),
        P(),
        P(),
        P(),
        P(),
        P("seq", None, None),
        P(),
        P("seq", None),
        P("seq", None),
        P(),
    )
    out_specs = (
        P("seq", "dp"),
        P(None, "seq", "dp"),
        P(),
        P(),
        P(),
        P(),
        P(),
        P(),
        P(),
        P(),
        P("seq", None, None),
        P(),
        P("seq", None),
        P("seq", None),
        P(),
    )
    split_heads = HEADS % mesh.shape["seq"] == 0
    body = tp_device if split_heads else per_device
    return jax.shard_map(
        body, mesh=mesh, in_specs=in_specs, out_specs=out_specs, check_vma=False
    )
```

```python
import functools
import math

import jax
import jax.numpy as jnp
from jax import lax
from jax.experimental import pallas as pl
from jax.experimental.pallas import tpu as pltpu
from jax.sharding import PartitionSpec as P

HEADS = 16
HEAD_DIM = 64
ROT = 16


ln_eps = 1e-05
rms_eps = 1e-06
masked_score = -1e30
highest = lax.Precision.HIGHEST


def gelu_exact(values):
    return jax.nn.gelu(values, approximate=False)


def rotary_tables(position):
    freq_index = jnp.arange(ROT // 2, dtype=jnp.float32)
    inverse_freq = jnp.exp(freq_index * (-2.0 * math.log(10000.0) / ROT))
    angles = position.astype(jnp.float32)[:, None] * inverse_freq[None, :]
    return (jnp.cos(angles), jnp.sin(angles))


def rotate(values, cosine, sine):
    half = ROT // 2
    former = values[..., :half]
    latter = values[..., half:ROT]
    cos_heads = cosine[:, None, :]
    sin_heads = sine[:, None, :]
    return jnp.concatenate(
        [
            former * cos_heads - latter * sin_heads,
            latter * cos_heads + former * sin_heads,
            values[..., ROT:],
        ],
        axis=-1,
    )


def token_layout(lengths, counts, tokens):
    index = jnp.arange(tokens, dtype=jnp.int32)
    second = index >= lengths[0]
    position = index - jnp.where(second, lengths[0], 0)
    valid = position < jnp.where(second, counts[1], counts[0])
    return (second, position, valid)


def normalize(streams):
    centre = jnp.mean(streams, axis=-1, keepdims=True)
    centred = streams - centre
    inverse = lax.rsqrt(jnp.mean(centred * centred, axis=-1, keepdims=True) + ln_eps)
    return (centred * inverse, inverse)


def normalize_back(grad_scaled, scaled, inverse):
    mean_grad = jnp.mean(grad_scaled, axis=-1, keepdims=True)
    mean_along = jnp.mean(grad_scaled * scaled, axis=-1, keepdims=True)
    return inverse * (grad_scaled - mean_grad - scaled * mean_along)


def per_device(
    history,
    cotangent,
    bucket_len,
    valid_len,
    gen_gain,
    gen_in,
    gen_out,
    gen_bias,
    norm_gain,
    norm_bias,
    w_in,
    in_bias,
    w_out,
    w_down,
    out_bias,
):
    states = history.shape[0]
    stacked = jnp.concatenate([history, cotangent[None]], axis=0)
    arrived = lax.all_to_all(stacked, "seq", split_axis=2, concat_axis=1, tiled=True)
    arrived_rows = jnp.swapaxes(arrived, 1, 2)
    hist_local = arrived_rows[:states]
    cot_local = arrived_rows[states]
    tokens = hist_local.shape[1]
    width = hist_local.shape[2]
    second, position, valid = token_layout(bucket_len.reshape(2), valid_len.reshape(2), tokens)
    valid_float = valid.astype(jnp.float32)
    last = hist_local[states - 1].astype(jnp.float32)
    rms = lax.rsqrt(jnp.mean(last * last, axis=-1, keepdims=True) + rms_eps)
    gen_normed = (last * rms * gen_gain).astype(jnp.bfloat16)
    gen_pre = jnp.dot(gen_normed, gen_in, preferred_element_type=jnp.float32)
    gen_hidden, gen_pull = jax.vjp(gelu_exact, gen_pre)
    mixing = jnp.einsum("th,hsj->tsj", gen_hidden, gen_out, precision=highest) + gen_bias
    weighted = mixing * valid_float[:, None, None]
    stat_sums = jnp.sum(weighted, axis=0)
    stat_squares = jnp.sum(weighted * mixing, axis=0)
    stat_count = jnp.sum(valid_float)
    streams = mixing[:, :, 0].T[:, :, None] * hist_local[0]
    for state in range(1, states):
        streams = streams + mixing[:, :, state].T[:, :, None] * hist_local[state]
    scaled, inverse = normalize(streams)
    normed_attn = (scaled[:3] * norm_gain[0] + norm_bias[0]).astype(jnp.bfloat16)
    normed_mlp = (scaled[3] * norm_gain[1] + norm_bias[1]).astype(jnp.bfloat16)
    piece = lax.all_gather(w_in, "seq", axis=0, tiled=True)
    attn_part = jnp.einsum(
        "stk,nsk->stn", normed_attn, piece[:, :3], preferred_element_type=jnp.float32
    )
    mlp_part = jnp.einsum(
        "tk,njk->jtn", normed_mlp, piece[:, 3:], preferred_element_type=jnp.float32
    )
    projected = jnp.concatenate([attn_part, mlp_part], axis=0) + in_bias[:, None, :]
    cosine, sine = rotary_tables(position)
    heads_shape = (tokens, HEADS, HEAD_DIM)
    queries = (rotate(projected[0].reshape(heads_shape), cosine, sine) * HEAD_DIM ** (-0.5)).astype(
        jnp.bfloat16
    )
    keys = rotate(projected[1].reshape(heads_shape), cosine, sine).astype(jnp.bfloat16)
    values = projected[2].reshape(heads_shape).astype(jnp.bfloat16)
    index = jnp.arange(tokens, dtype=jnp.int32)
    allowed = (
        (second[:, None] == second[None, :]) & (index[None, :] <= index[:, None]) & valid[None, :]
    )
    scores = jnp.einsum("qhd,khd->hqk", queries, keys, preferred_element_type=jnp.float32)
    scores = jnp.where(allowed[None], scores, masked_score)
    top = jnp.max(scores, axis=-1, keepdims=True)
    weights = jnp.exp(scores - top)
    weight_total = jnp.sum(weights, axis=-1, keepdims=True)
    log_total = top + jnp.log(weight_total)
    probs_low = (weights / weight_total).astype(jnp.bfloat16)
    attended = jnp.einsum("hqk,khd->qhd", probs_low, values, preferred_element_type=jnp.float32)
    attn_low = attended.reshape(tokens, width).astype(jnp.bfloat16)
    gelu_up, up_pull = jax.vjp(gelu_exact, projected[3:])
    gelu_low = gelu_up.astype(jnp.bfloat16)
    grad_out_low = jnp.where(valid[:, None], cot_local, jnp.zeros_like(cot_local))
    piece_out, piece_down = lax.all_gather((w_out, w_down), "seq", axis=0, tiled=True)
    down_part = piece_down.reshape(piece_down.shape[0], 4, width)
    result = jnp.einsum("tk,nk->tn", attn_low, piece_out, preferred_element_type=jnp.float32)
    branch = result + jnp.einsum(
        "jtk,njk->tn", gelu_low, down_part, preferred_element_type=jnp.float32
    )
    new_local = (streams[3] + branch + out_bias).astype(jnp.bfloat16)
    piece_out = lax.all_gather(w_out, "seq", axis=0, tiled=True)
    piece_down = lax.all_gather(w_down, "seq", axis=0, tiled=True)
    count = piece_out.shape[0]
    part = grad_out_low
    attn_add = jnp.einsum("tn,nk->tk", part, piece_out, preferred_element_type=jnp.float32)
    gelu_add = jnp.einsum(
        "tn,njk->jtk", part, piece_down.reshape(count, 4, width), preferred_element_type=jnp.float32
    )
    grad_attn = attn_add
    part = grad_out_low
    term_out = jnp.einsum("tn,tk->nk", part, attn_low, preferred_element_type=jnp.float32)
    term_down = jnp.einsum(
        "tn,jtk->njk", part, gelu_low, preferred_element_type=jnp.float32
    ).reshape(lax.axis_size("seq") * w_out.shape[0], 4 * width)
    out_grads = lax.psum_scatter(
        jnp.concatenate([term_out, term_down], axis=1).astype(jnp.bfloat16),
        "seq",
        scatter_dimension=0,
        tiled=True,
    )
    out_bias_grad = jnp.sum(grad_out_low.astype(jnp.float32), axis=0)
    grad_attended = grad_attn.astype(jnp.bfloat16).reshape(heads_shape)
    rescored = jnp.einsum("qhd,khd->hqk", queries, keys, preferred_element_type=jnp.float32)
    probs = jnp.where(allowed[None], jnp.exp(rescored - log_total), 0.0)
    grad_values = jnp.einsum(
        "hqk,qhd->khd",
        probs.astype(jnp.bfloat16),
        grad_attended,
        preferred_element_type=jnp.float32,
    )
    grad_probs = jnp.einsum(
        "qhd,khd->hqk", grad_attended, values, preferred_element_type=jnp.float32
    )
    grad_scores = (
        probs * (grad_probs - jnp.sum(probs * grad_probs, axis=-1, keepdims=True))
    ).astype(jnp.bfloat16)
    grad_queries = jnp.einsum(
        "hqk,khd->qhd", grad_scores, keys, preferred_element_type=jnp.float32
    ) * HEAD_DIM ** (-0.5)
    grad_keys = jnp.einsum("hqk,qhd->khd", grad_scores, queries, preferred_element_type=jnp.float32)
    grad_up = up_pull(gelu_add)[0]
    grad_proj = jnp.concatenate(
        [
            rotate(grad_queries, cosine, -sine).reshape(1, tokens, width),
            rotate(grad_keys, cosine, -sine).reshape(1, tokens, width),
            grad_values.reshape(1, tokens, width),
            grad_up,
        ],
        axis=0,
    )
    in_bias_grad = jnp.sum(grad_proj, axis=1)
    grad_proj_low = grad_proj.astype(jnp.bfloat16)
    piece = lax.all_gather(w_in, "seq", axis=0, tiled=True)
    part = grad_proj_low
    attn_add = jnp.einsum(
        "stn,nsk->stk", part[:3], piece[:, :3], preferred_element_type=jnp.float32
    )
    mlp_add = jnp.einsum("jtn,njk->tk", part[3:], piece[:, 3:], preferred_element_type=jnp.float32)
    part = grad_proj_low
    attn_term = jnp.einsum(
        "stn,stk->nsk", part[:3], normed_attn, preferred_element_type=jnp.float32
    )
    mlp_term = jnp.einsum("jtn,tk->njk", part[3:], normed_mlp, preferred_element_type=jnp.float32)
    in_grads = lax.psum_scatter(
        jnp.concatenate([attn_term, mlp_term], axis=1).astype(jnp.bfloat16),
        "seq",
        scatter_dimension=0,
        tiled=True,
    )
    norm_gain_grad = jnp.stack(
        [jnp.sum(attn_add * scaled[:3], axis=(0, 1)), jnp.sum(mlp_add * scaled[3], axis=0)]
    )
    norm_bias_grad = jnp.stack([jnp.sum(attn_add, axis=(0, 1)), jnp.sum(mlp_add, axis=0)])
    grad_attn_streams = normalize_back(attn_add * norm_gain[0], scaled[:3], inverse[:3])
    grad_mlp_stream = normalize_back(
        mlp_add * norm_gain[1], scaled[3], inverse[3]
    ) + grad_out_low.astype(jnp.float32)
    grad_streams = jnp.concatenate([grad_attn_streams, grad_mlp_stream[None]], axis=0)
    grad_mixing = jnp.stack(
        [
            jnp.einsum(
                "std,td->ts", grad_streams, hist_local[state].astype(jnp.float32), precision=highest
            )
            for state in range(states)
        ],
        axis=-1,
    )
    hist_terms = [
        jnp.einsum("ts,std->td", mixing[:, :, state], grad_streams, precision=highest)
        for state in range(states)
    ]
    gen_bias_grad = jnp.sum(grad_mixing, axis=0)
    gen_out_grad = jnp.einsum("th,tsj->hsj", gen_hidden, grad_mixing, precision=highest)
    grad_hidden = jnp.einsum("tsj,hsj->th", grad_mixing, gen_out, precision=highest)
    grad_pre_low = gen_pull(grad_hidden)[0].astype(jnp.bfloat16)
    gen_in_grad = jnp.einsum(
        "tk,th->kh", gen_normed, grad_pre_low, preferred_element_type=jnp.float32
    )
    grad_gen = jnp.einsum("th,kh->tk", grad_pre_low, gen_in, preferred_element_type=jnp.float32)
    gen_gain_grad = jnp.sum(grad_gen * last * rms, axis=0)
    gained = grad_gen * gen_gain
    grad_last = rms * gained - last * (rms * rms * rms) * jnp.mean(
        gained * last, axis=-1, keepdims=True
    )
    hist_stack = jnp.stack(hist_terms[: states - 1] + [hist_terms[states - 1] + grad_last]).astype(
        jnp.bfloat16
    )
    departing = jnp.swapaxes(jnp.concatenate([new_local[None], hist_stack], axis=0), 1, 2)
    returned = lax.all_to_all(departing, "seq", split_axis=1, concat_axis=2, tiled=True)
    w_in_grad, out_total = (
        lax.psum(in_grads, "dp").astype(jnp.float32),
        lax.psum(out_grads, "dp").astype(jnp.float32),
    )
    w_out_grad = out_total[:, :width]
    w_down_grad = out_total[:, width:]
    joined = lax.psum(
        (
            gen_gain_grad,
            gen_in_grad,
            gen_out_grad,
            gen_bias_grad,
            norm_gain_grad,
            norm_bias_grad,
            in_bias_grad,
            out_bias_grad,
            stat_sums,
            stat_squares,
            stat_count,
        ),
        ("seq", "dp"),
    )
    small_totals = joined[:8]
    stat_totals = joined[8:]
    mix_mean = stat_totals[0] / stat_totals[2]
    mix_var = stat_totals[1] / stat_totals[2] - mix_mean * mix_mean
    return (
        returned[0],
        returned[1:],
        mix_mean,
        mix_var,
        small_totals[0],
        small_totals[1],
        small_totals[2],
        small_totals[3],
        small_totals[4],
        small_totals[5],
        w_in_grad,
        small_totals[6],
        w_out_grad,
        w_down_grad,
        small_totals[7],
    )


MESH = pl.DeviceIdType.MESH
HIDDEN_ROWS = 40
ROOT_HALF = math.sqrt(0.5)
INV_ROOT_2PI = 1.0 / math.sqrt(2.0 * math.pi)


def gelu_pair(x):
    half = 0.5 + 0.5 * lax.erf(x * ROOT_HALF)
    return x * half, half + x * (jnp.exp(-0.5 * x * x) * INV_ROOT_2PI)


def contract(a, b, dim_a, dim_b, precision=None):
    return lax.dot_general(
        a, b, (((dim_a,), (dim_b,)), ((), ())),
        precision=precision, preferred_element_type=jnp.float32,
    )


class Links:
    def __init__(self, n):
        self.n = n
        self.me = lax.axis_index("seq")
        core = self.me % 2
        xbit = (self.me // 2) % 2
        ybit = (self.me // 4) % 2
        flip = 1 - 2 * core
        x = self.me + 2 - 4 * xbit
        y = self.me + 4 - 8 * ybit
        self.core = core
        self.a = x * (1 - core) + y * core
        self.b = y * (1 - core) + x * core
        self.dg = x + y - self.me
        self.p = self.me + flip
        self.pa = self.b + flip
        self.pb = self.a + flip
        self.pdg = self.dg + flip

    def greet(self):
        barrier = pltpu.get_barrier_semaphore()
        for k in range(1, self.n):
            pl.semaphore_signal(
                barrier, inc=1, device_id={"seq": (self.me + k) % self.n}, device_id_type=MESH
            )
        pl.semaphore_wait(barrier, self.n - 1)

    def copy(self, src, dst, send, recv, to):
        return pltpu.make_async_remote_copy(
            src_ref=src, dst_ref=dst, send_sem=send, recv_sem=recv,
            device_id={"seq": to}, device_id_type=MESH,
        )


class Gather:
    def __init__(self, links, place, send, recv):
        self.links, self.place, self.send, self.recv = links, place, send, recv

    def _go(self, src, owner, slot, index, to):
        self.links.copy(
            src, self.place(owner), self.send.at[slot], self.recv.at[index], to
        ).start()

    def _got(self, owner, index):
        place = self.place(owner)
        self.links.copy(place, place, self.send.at[0], self.recv.at[index], self.links.p).wait_recv()

    def start(self, src):
        at = self.links
        self._go(src, at.me, 0, 0, at.a)
        self._go(src, at.me, 1, 1, at.b)
        self._go(src, at.me, 2, 3, at.p)

    def near(self):
        at = self.links
        self._got(at.a, 0)
        self._go(self.place(at.a), at.a, 3, 2, at.b)
        self._go(self.place(at.a), at.a, 4, 4, at.p)
        self._got(at.b, 1)
        self._go(self.place(at.b), at.b, 5, 5, at.p)

    def far(self):
        at = self.links
        self._got(at.dg, 2)
        self._go(self.place(at.dg), at.dg, 6, 6, at.p)

    def other(self):
        at = self.links
        for owner, index in ((at.p, 3), (at.pa, 4), (at.pb, 5), (at.pdg, 6)):
            self._got(owner, index)

    def drain(self):
        place = self.place(self.links.me)
        for slot in range(7):
            self.links.copy(
                place, place, self.send.at[slot], self.recv.at[0], self.links.p
            ).wait_send()


class Everyone:
    def __init__(self, links, source, target, arrived, send, recv):
        self.links, self.source, self.target, self.arrived = links, source, target, arrived
        self.send, self.recv = send, recv

    def start(self):
        at = self.links
        for k in range(1, at.n):
            to = (at.me + k) % at.n
            at.copy(
                self.source(to), self.target(k), self.send.at[k], self.recv.at[k], to
            ).start()

    def wait(self, k):
        at = self.links
        origin = (at.me + at.n - k) % at.n
        place = self.arrived(k, origin)
        at.copy(place, place, self.send.at[k], self.recv.at[k], at.p).wait_recv()
        return origin

    def drain(self):
        at = self.links
        for k in range(1, at.n):
            to = (at.me + k) % at.n
            place = self.source(to)
            at.copy(place, place, self.send.at[k], self.recv.at[k], at.p).wait_send()


def front_kernel(
    n,
    hist, cot, lens, vals, gain, gin, gout, gbias, ng, nb, w_out, w_down,
    nbuf, cot_all, cols, pk, raw_out, scaled, st3, stat_out,
    prm, colp, part, part_in, stat, stat_in, streams, nown,
    ex_send, ex_recv, ag_send, ag_recv, local_sem,
):
    f32, bf16 = jnp.float32, jnp.bfloat16
    states, feats, tokens = hist.shape
    block = tokens // n
    width = n * feats
    hid = gin.shape[0]
    at = Links(n)
    me = at.me
    mine = pl.ds(pl.multiple_of(me * feats, feats), feats)

    def rows(owner):
        return pl.ds(pl.multiple_of(owner * feats, feats), feats)

    def lanes(owner):
        return pl.ds(pl.multiple_of(owner * block, block), block)

    gathers = [
        Gather(at, lambda owner, s=s: nbuf.at[s * n + owner], ag_send.at[s], ag_recv.at[s])
        for s in range(4)
    ]
    cots = Gather(at, lambda owner: cot_all.at[rows(owner), :], ag_send.at[4], ag_recv.at[4])
    parts = Everyone(
        at, lambda to: part.at[to], lambda k: part_in.at[k], lambda k, origin: part_in.at[k],
        ex_send.at[0], ex_recv.at[0],
    )
    mixes = Everyone(
        at, lambda to: pk.at[me], lambda k: pk.at[me], lambda k, origin: pk.at[origin],
        ex_send.at[1], ex_recv.at[1],
    )
    stats = Everyone(
        at, lambda to: stat, lambda k: stat_in.at[me], lambda k, origin: stat_in.at[origin],
        ex_send.at[2], ex_recv.at[2],
    )

    at.greet()
    cots.start(cot)
    keep_cot = pltpu.make_async_copy(cot, cot_all.at[mine, :], local_sem.at[0])
    keep_cot.start()

    prm[...] = jnp.zeros_like(prm)
    prm[0:1, :] = gain[:, mine]
    prm[1:3, :] = ng[:, mine]
    prm[3:5, :] = nb[:, mine]
    colp[...] = prm[...].T
    gin_mine = gin[:, mine]
    for b in range(n):
        last = hist[states - 1, :, b * block : (b + 1) * block].astype(f32)
        product = (last * colp[:, 0:1]).astype(bf16)
        part[b, 0:hid, :] = jnp.dot(gin_mine, product, preferred_element_type=f32)
        part[b, hid : hid + 8, :] = jnp.broadcast_to(
            jnp.sum(last * last, axis=0, keepdims=True), (8, block)
        )
    parts.start()
    total = part[me]
    for k in range(1, n):
        parts.wait(k)
        total = total + part_in[k]
    raw_out[...] = total
    rms = lax.rsqrt(total[hid : hid + 1] * (1.0 / width) + rms_eps)
    hidden, _ = gelu_pair(total[0:hid] * rms)
    table = jnp.concatenate([gout[j] for j in range(states)], axis=0)
    mixing = jnp.dot(table, hidden, precision=highest, preferred_element_type=f32)
    for j in range(states):
        pk[me, 4 * j : 4 * j + 4, :] = mixing[4 * j : 4 * j + 4] + gbias[:, j : j + 1]
    row = 4 * states
    pk[me, row : row + 1, :] = rms
    for offset, value in ((1, lens[0, 0, 0]), (2, vals[0, 0, 0]), (3, vals[0, 0, 1])):
        pk[me, row + offset : row + offset + 1, :] = jnp.full((1, block), value.astype(f32))
    mixes.start()

    def column_copies(to, send, recv):
        out = []
        for j in range(5):
            if j == 0:
                src = w_out.at[:, rows(to)]
            else:
                src = w_down.at[:, pl.ds(pl.multiple_of((j - 1) * width + to * feats, feats), feats)]
            out.append((src, cols.at[mine, pl.ds(j * feats, feats)]))
        return out

    for k in range(1, n):
        to = (me + k) % n
        for src, dst in column_copies(to, None, None):
            at.copy(src, dst, ex_send.at[3, k], ex_recv.at[3, k], to).start()
    own_cols = [
        pltpu.make_async_copy(src, dst, local_sem.at[1 + j])
        for j, (src, dst) in enumerate(column_copies(me, None, None))
    ]
    for copy in own_cols:
        copy.start()
    cots.near()

    def mix_block(owner):
        where = lanes(owner)
        for half in range(2):
            part_rows = pl.ds(half * (feats // 2), feats // 2)
            sums = [None] * 4
            for j in range(states):
                value = hist[j, part_rows, where].astype(f32)
                for s in range(4):
                    weight = pk[owner, pl.ds(4 * j + s, 1), :]
                    term = weight * value
                    sums[s] = term if sums[s] is None else sums[s] + term
            for s in range(4):
                streams[s, part_rows, where] = sums[s]
        for s in range(4):
            value = streams[s, :, where]
            mean = jnp.sum(value, axis=0, keepdims=True) * (1.0 / feats)
            off = value - mean
            stat[pl.ds(s, 1), where] = mean
            stat[pl.ds(4 + s, 1), where] = jnp.sum(off * off, axis=0, keepdims=True)

    mix_block(me)

    @pl.loop(1, n)
    def _(k):
        mix_block(mixes.wait(k))

    stats.start()
    cots.far()
    for k in range(1, n):
        stats.wait(k)
    stat_in[me] = stat[...]
    means = stat_in[0, 0:4, :]
    for k in range(1, n):
        means = means + stat_in[k, 0:4, :]
    means = means * (1.0 / n)
    spread = jnp.zeros_like(means)
    for k in range(n):
        away = stat_in[k, 0:4, :] - means
        spread = spread + (stat_in[k, 4:8, :] + feats * (away * away))
    stat_out[0:4, :] = means
    stat_out[4:8, :] = lax.rsqrt(spread * (1.0 / width) + ln_eps)

    keeps = []
    for s in range(4):
        which = 0 if s < 3 else 1
        for b in range(n):
            where = pl.ds(b * block, block)
            xhat = (streams[s, :, where] - stat_out[s : s + 1, where]) * stat_out[4 + s : 5 + s, where]
            scaled[s, :, where] = xhat
            nown[s, :, where] = (
                xhat * colp[:, 1 + which : 2 + which] + colp[:, 3 + which : 4 + which]
            ).astype(bf16)
        gathers[s].start(nown.at[s])
        keep = pltpu.make_async_copy(nown.at[s], nbuf.at[s * n + me], local_sem.at[6 + s])
        keep.start()
        keeps.append(keep)
    st3[...] = streams[3]
    for s in range(4):
        gathers[s].near()
        if s >= 1:
            gathers[s - 1].far()
    gathers[3].far()
    for g in [cots] + gathers:
        g.other()
    for k in range(1, n):
        place = cols.at[rows((me + n - k) % n), :]
        at.copy(place, place, ex_send.at[3, k], ex_recv.at[3, k], at.p).wait()
    for g in [cots] + gathers:
        g.drain()
    for exchange in (parts, mixes, stats):
        exchange.drain()
    keep_cot.wait()
    for copy in own_cols + keeps:
        copy.wait()


def front(n, history, cotangent, bucket_len, valid_len, gen_gain, gen_in, gen_out, gen_bias, norm_gain, norm_bias, w_out, w_down):
    f32, bf16 = jnp.float32, jnp.bfloat16
    states, feats, tokens = history.shape
    block = tokens // n
    width = n * feats
    hid = gen_in.shape[1]
    vmem = pl.BlockSpec(memory_space=pltpu.VMEM)
    smem = pl.BlockSpec(memory_space=pltpu.SMEM)
    anys = pl.BlockSpec(memory_space=pl.ANY)
    shape = jax.ShapeDtypeStruct
    return pl.pallas_call(
        functools.partial(front_kernel, n),
        out_shape=(
            shape((4 * n, feats, tokens), bf16),
            shape((width, tokens), bf16),
            shape((width, 5 * feats), bf16),
            shape((n, 40, block), f32),
            shape((hid + 8, block), f32),
            shape((4, feats, tokens), f32),
            shape((feats, tokens), f32),
            shape((8, tokens), f32),
        ),
        in_specs=[vmem, vmem, smem, smem] + [vmem] * 6 + [anys] * 2,
        out_specs=(anys, anys, anys, vmem, vmem, vmem, vmem, vmem),
        scratch_shapes=[
            pltpu.VMEM((feats, feats), f32),
            pltpu.VMEM((feats, feats), f32),
            pltpu.VMEM((n, hid + 8, block), f32),
            pltpu.VMEM((n, hid + 8, block), f32),
            pltpu.VMEM((8, tokens), f32),
            pltpu.VMEM((n, 8, tokens), f32),
            pltpu.VMEM((4, feats, tokens), f32),
            pltpu.VMEM((4, feats, tokens), bf16),
            pltpu.SemaphoreType.DMA((4, n)),
            pltpu.SemaphoreType.DMA((4, n)),
            pltpu.SemaphoreType.DMA((5, 7)),
            pltpu.SemaphoreType.DMA((5, 7)),
            pltpu.SemaphoreType.DMA((10,)),
        ],
        compiler_params=pltpu.CompilerParams(
            collective_id=1, has_side_effects=True, vmem_limit_bytes=60 * 2**20
        ),
        name="front",
    )(
        history, cotangent, bucket_len, valid_len, gen_gain.reshape(1, width), gen_in.T,
        gen_out.transpose(2, 1, 0), gen_bias, norm_gain, norm_bias, w_out, w_down,
    )


def back_kernel(
    n, zn,
    nbuf, cot_all, cols_in, history, scaled_in,
    w_in, pk, raw, st3, stat, gain, gin, gout, ng, in_bias, out_bias,
    new_state, hist_grad, totals,
    bias_tot, ngain_tot, nbias_tot, gain_tot, outb_tot, gin_tot, gout_tot,
    gbias_tot, mean_tot, var_tot,
    big, cot, cols, prm, colp, qkv, act, deriv, probs, gattn, gp, gcol, rope, accs, gn,
    ybuf, abuf, from_a, from_b, zown, zin, zmid,
    gsum, gsum_in, gmix, gmix_in, pre, genmsg, gen_in_all, vec, vec_z, vec_sum, vec_all,
    load_sem, rs_send, rs_recv, ex_send, ex_recv, z_send, z_recv, out_sem,
):
    f32, bf16 = jnp.float32, jnp.bfloat16
    states = history.shape[0]
    feats, tokens = st3.shape
    block = tokens // n
    width = n * feats
    hid = gin.shape[0]
    heads = feats // HEAD_DIM
    scale = HEAD_DIM ** (-0.5)
    m = 4 * states
    wide = 2 * block
    chunks = tokens // wide
    at = Links(n)
    me = at.me
    zc = lax.axis_index("dp")

    def rows(owner):
        return pl.ds(pl.multiple_of(owner * feats, feats), feats)

    def lanes(index, size=block):
        return pl.ds(pl.multiple_of(index * size, size), size)

    loads = [
        pltpu.make_async_copy(
            nbuf.at[pl.ds(s * n, n)], big.at[pl.ds(s * n, n)], load_sem.at[s]
        )
        for s in range(4)
    ]
    loads.append(pltpu.make_async_copy(cot_all, cot, load_sem.at[4]))
    loads.append(pltpu.make_async_copy(cols_in, cols, load_sem.at[5]))
    for index in (0, 1, 2, 3, 5, 4):
        loads[index].start()
    load_scaled = pltpu.make_async_copy(scaled_in, deriv, load_sem.at[6])
    load_hist = pltpu.make_async_copy(history, big.at[pl.ds(0, states)], load_sem.at[7])

    barrier = pltpu.get_barrier_semaphore()
    for k in range(1, n):
        pl.semaphore_signal(
            barrier, inc=1, device_id={"seq": (me + k) % n}, device_id_type=MESH
        )
    for k in range(1, zn):
        pl.semaphore_signal(
            barrier, inc=1, device_id={"dp": (zc + k) % zn}, device_id_type=MESH
        )

    prm[...] = jnp.zeros_like(prm)
    prm[0:1, :] = gain[:, rows(me)]
    prm[1:3, :] = ng[:, rows(me)]
    prm[3:4, :] = out_bias[:, rows(me)]
    prm[8:15, :] = in_bias[:, rows(me)]
    colp[...] = prm[...].T
    accs[...] = jnp.zeros_like(accs)

    spot = lax.broadcasted_iota(jnp.int32, (1, block), 1).astype(f32)
    freq = jnp.exp(
        lax.broadcasted_iota(jnp.int32, (8, block), 0).astype(f32)
        * (-2.0 * math.log(10000.0) / ROT)
    )

    def place(owner, index):
        cut = pk[owner, m + 1 : m + 2, :]
        second = index >= cut
        position = index - jnp.where(second, cut, 0.0)
        limit = jnp.where(second, pk[owner, m + 3 : m + 4, :], pk[owner, m + 2 : m + 3, :])
        return second, position, position < limit

    for b in range(n):
        where = pl.ds(b * block, block)
        _, position, valid = place(b, spot)
        angle = freq * position
        rope[0:8, where] = jnp.cos(angle)
        rope[8:16, where] = jnp.sin(angle)
        rope[16:17, where] = jnp.where(valid, 1.0, 0.0)

    def rotated(value, where, sign):
        cosine, sine = rope[0:8, where], rope[8:16, where] * sign
        out = []
        for h in range(heads):
            base = h * HEAD_DIM
            former, latter = value[base : base + 8], value[base + 8 : base + 16]
            out += [
                former * cosine - latter * sine,
                latter * cosine + former * sine,
                value[base + 16 : base + HEAD_DIM],
            ]
        return jnp.concatenate(out, axis=0)

    def stream(s, where):
        return big[pl.ds(s * n, n), :, where].reshape(width, -1)

    for s in range(3):
        loads[s].wait()

        @pl.loop(0, chunks)
        def _(c, s=s):
            where = lanes(c, wide)
            value = jnp.dot(w_in[s], stream(s, where), preferred_element_type=f32)
            value = value + colp[:, 8 + s : 9 + s]
            if s < 2:
                value = rotated(value, where, 1.0)
            if s == 0:
                value = value * scale
            qkv[s, :, where] = value.astype(bf16)

    loads[3].wait()
    for j in range(4):

        @pl.loop(0, chunks)
        def _(c, j=j):
            where = lanes(c, wide)
            value = jnp.dot(w_in[3 + j], stream(3, where), preferred_element_type=f32)
            up, slope = gelu_pair(value + colp[:, 11 + j : 12 + j])
            act[pl.ds((1 + j) * feats, feats), where] = up.astype(bf16)
            deriv[j, :, where] = slope

    key_at = lax.broadcasted_iota(jnp.int32, (block, block), 0).astype(f32)
    query_at = lax.broadcasted_iota(jnp.int32, (block, block), 1).astype(f32)

    @pl.loop(0, n)
    def _(b):
        where = lanes(b)
        cut = pk[b, m + 1 : m + 2, :]
        _, _, valid = place(b, key_at)
        same = jnp.where(key_at >= cut, 1.0, 0.0) == jnp.where(query_at >= cut, 1.0, 0.0)
        allowed = same & (key_at <= query_at) & valid
        for h in range(heads):
            part = pl.ds(h * HEAD_DIM, HEAD_DIM)
            scores = contract(qkv[1, part, where], qkv[0, part, where], 0, 0)
            scores = jnp.where(allowed, scores, masked_score)
            weights = jnp.exp(scores - jnp.max(scores, axis=0, keepdims=True))
            soft = weights * (1.0 / jnp.sum(weights, axis=0, keepdims=True))
            probs[b * heads + h] = soft
            act[part, where] = jnp.dot(
                qkv[2, part, where], soft.astype(bf16), preferred_element_type=f32
            ).astype(bf16)

    def rs_copy(i, src, dst, slot, to):
        return at.copy(src, dst, rs_send.at[i, slot], rs_recv.at[i, slot], to)

    def rs_first(i):
        return [
            rs_copy(i, ybuf.at[i, rows(owner), :], abuf.at[i, q], q, at.p)
            for q, owner in enumerate((at.p, at.pa, at.pb, at.pdg))
        ]

    def rs_second(i):
        return [
            rs_copy(i, ybuf.at[i, rows(at.a), :], from_a.at[i, 0], 4, at.a),
            rs_copy(i, ybuf.at[i, rows(at.dg), :], from_a.at[i, 1], 5, at.a),
        ]

    def rs_third(i):
        return [rs_copy(i, ybuf.at[i, rows(at.b), :], from_b.at[i], 6, at.b)]

    def rs_start(i):
        for copy in rs_first(i):
            copy.start()

    def rs_fold(i):
        for copy in rs_first(i):
            copy.wait_recv()

        @pl.loop(0, chunks)
        def _(c):
            where = lanes(c, wide)
            for q, owner in ((1, at.a), (3, at.dg)):
                ybuf[i, rows(owner), where] = (
                    ybuf[i, rows(owner), where].astype(f32) + abuf[i, q, :, where].astype(f32)
                ).astype(bf16)

        for copy in rs_second(i):
            copy.start()

    def rs_pass(i):
        for copy in rs_second(i):
            copy.wait_recv()

        @pl.loop(0, chunks)
        def _(c):
            where = lanes(c, wide)
            ybuf[i, rows(at.b), where] = (
                ybuf[i, rows(at.b), where].astype(f32)
                + abuf[i, 2, :, where].astype(f32)
                + from_a[i, 1, :, where].astype(f32)
            ).astype(bf16)

        for copy in rs_third(i):
            copy.start()

    def rs_end(i):
        for copy in rs_third(i):
            copy.wait_recv()

    def rs_value(i, where):
        return (
            ybuf[i, rows(me), where].astype(f32)
            + abuf[i, 0, :, where].astype(f32)
            + from_a[i, 0, :, where].astype(f32)
            + from_b[i, :, where].astype(f32)
        )

    def rs_drain(i):
        for copy in rs_first(i) + rs_second(i) + rs_third(i):
            copy.wait_send()

    outer = (zc == 0) | (zc == 3)
    z_in = 1 + zc // 3
    z_out = 3 * (zc - 1)
    z_over = 3 - zc

    def z_copy(c, src, dst, slot, recv_slot, to):
        return pltpu.make_async_remote_copy(
            src_ref=src, dst_ref=dst, send_sem=z_send.at[c, slot], recv_sem=z_recv.at[c, recv_slot],
            device_id={"dp": to}, device_id_type=MESH,
        )

    def z_up(c):
        return z_copy(c, zown.at[c], zin.at[c], 0, 0, z_in)

    def z_cross(c):
        return z_copy(c, zown.at[c], zmid.at[c], 1, 1, z_over)

    def z_down(c):
        return z_copy(c, zin.at[c], zin.at[c], 2, 0, z_out)

    def z_start(c):
        if zn > 1:

            @pl.when(outer)
            def _():
                z_up(c).start()

    def z_fold(c):
        if zn > 1:

            @pl.when(jnp.logical_not(outer))
            def _():
                z_up(c).wait_recv()

                @pl.loop(0, chunks)
                def _(k):
                    where = lanes(k, wide)
                    zown[c, :, where] = (
                        zown[c, :, where].astype(f32) + zin[c, :, where].astype(f32)
                    ).astype(bf16)

                z_cross(c).start()

    stages = []

    def z_end(c):
        if zn > 1:

            @pl.when(jnp.logical_not(outer))
            def _():
                z_cross(c).wait_recv()

                @pl.loop(0, chunks)
                def _(k):
                    where = lanes(k, wide)
                    zin[c, :, where] = (
                        zown[c, :, where].astype(f32) + zmid[c, :, where].astype(f32)
                    ).astype(bf16)

                z_down(c).start()

            @pl.when(outer)
            def _():
                z_up(c).wait_recv()

        source = zin if zn > 1 else zown
        stages.append(pltpu.make_async_copy(source.at[c], totals.at[c], out_sem.at[c]))
        stages[-1].start()

    def z_drain(c):
        if zn > 1:

            @pl.when(outer)
            def _():
                z_up(c).wait_send()

            @pl.when(jnp.logical_not(outer))
            def _():
                z_cross(c).wait_send()
                z_down(c).wait_send()

    loads[5].wait()
    quarter = width // 4

    @pl.loop(0, chunks)
    def _(c):
        where = lanes(c, wide)
        for r in range(4):
            part = slice(r * quarter, (r + 1) * quarter)
            ybuf[4, part, where] = jnp.dot(
                cols[part, :], act[:, where], preferred_element_type=f32
            ).astype(bf16)

    pl.semaphore_wait(barrier, n - 1 + zn - 1)
    rs_start(4)

    loads[4].wait()

    @pl.loop(0, n)
    def _(b):
        where = lanes(b)
        mask = rope[16:17, where].astype(bf16)
        cot[:, where] = cot[:, where] * mask

    for j in range(5):
        gn[0] = contract(cols[:, j * feats : (j + 1) * feats], cot[...], 0, 0)

        @pl.loop(0, chunks)
        def _(c, j=j):
            where = lanes(c, wide)
            value = gn[0, :, where]
            if j == 0:
                gattn[:, where] = value.astype(bf16)
            else:
                value = value * deriv[j - 1, :, where]
                accs[2 + j] = accs[2 + j] + (value[:, :block] + value[:, block:])
                gp[pl.ds((2 + j) * feats, feats), where] = value.astype(bf16)

    load_scaled.start()
    for r in range(4):
        grads = contract(cot[r * quarter : (r + 1) * quarter, :], act[...], 1, 1).astype(bf16)
        for j in range(5):
            gcol[j, r * quarter : (r + 1) * quarter, :] = grads[:, j * feats : (j + 1) * feats]

    turns = Everyone(
        at,
        lambda to: gcol.at[:, rows(to), :],
        lambda k: zown.at[pl.ds(7, 5), :, rows(me)],
        lambda k, origin: zown.at[pl.ds(7, 5), :, rows(origin)],
        ex_send.at[0], ex_recv.at[0],
    )
    turns.start()
    keep = pltpu.make_async_copy(
        gcol.at[:, rows(me), :], zown.at[pl.ds(7, 5), :, rows(me)], load_sem.at[8]
    )
    keep.start()

    def normed_grad(i, first, count):
        @pl.loop(0, n)
        def _(r):
            weight = jnp.concatenate(
                [w_in[first + s, :, lanes(r, feats)] for s in range(count)], axis=0
            )
            ybuf[i, rows(r), :] = contract(
                weight, gp[first * feats : (first + count) * feats, :], 0, 0
            ).astype(bf16)

        rs_start(i)

    def weight_grad(s, source):
        @pl.loop(0, 4)
        def _(r):
            part = big[pl.ds(source * n + r * (n // 4), n // 4), :, :].reshape(quarter, tokens)
            zown[s, :, lanes(r, quarter)] = contract(
                gp[s * feats : (s + 1) * feats, :], part, 1, 1
            ).astype(bf16)

        z_start(s)

    normed_grad(3, 3, 4)
    for s in range(3, 7):
        weight_grad(s, 3)
    rs_fold(4)

    @pl.loop(0, n)
    def _(b):
        where = lanes(b)
        grads = [[], [], []]
        for h in range(heads):
            part = pl.ds(h * HEAD_DIM, HEAD_DIM)
            soft = probs[b * heads + h]
            grad = gattn[part, where]
            grads[2].append(contract(grad, soft.astype(bf16), 1, 1))
            dprob = contract(qkv[2, part, where], grad, 0, 0)
            inner = jnp.sum(soft * dprob, axis=0, keepdims=True)
            low = (soft * (dprob - inner)).astype(bf16)
            grads[0].append(
                jnp.dot(qkv[1, part, where], low, preferred_element_type=f32) * scale
            )
            grads[1].append(contract(qkv[0, part, where], low, 1, 1))
        for s in range(3):
            value = jnp.concatenate(grads[s], axis=0)
            if s < 2:
                value = rotated(value, where, -1.0)
            accs[s] = accs[s] + value
            gp[pl.ds(s * feats, feats), where] = value.astype(bf16)

    rs_fold(3)
    rs_pass(4)
    for s in range(3):
        normed_grad(s, s, 1)
    z_fold(3)
    for k in range(1, n):
        turns.wait(k)
    keep.wait()
    for c in range(7, 12):
        z_start(c)
    for s in range(3):
        weight_grad(s, s)
    load_hist.start()
    rs_fold(0)
    z_fold(4)
    rs_pass(3)
    rs_fold(1)
    z_fold(5)
    rs_pass(0)
    rs_fold(2)
    z_fold(6)
    rs_pass(1)
    z_end(3)
    rs_end(4)

    @pl.loop(0, n)
    def _(b):
        where = lanes(b)
        new_state[:, where] = (st3[:, where] + rs_value(4, where) + colp[:, 3:4]).astype(bf16)

    rs_pass(2)
    z_fold(7)
    z_end(4)
    load_scaled.wait()

    def norm_sums(s):
        which = 0 if s < 3 else 1

        @pl.loop(0, n)
        def _(b):
            where = lanes(b)
            value = rs_value(s, where)
            xhat = deriv[s, :, where]
            along = value * xhat
            accs[7 + which] = accs[7 + which] + along
            accs[9 + which] = accs[9 + which] + value
            factor = colp[:, 1 + which : 2 + which]
            gn[s, :, where] = value * factor
            gsum[s : s + 1, where] = jnp.sum(value * factor, axis=0, keepdims=True)
            gsum[4 + s : 5 + s, where] = jnp.sum(along * factor, axis=0, keepdims=True)

    for s in (3, 0, 1, 2):
        rs_end(s)
        norm_sums(s)
    sums = Everyone(
        at, lambda to: gsum, lambda k: gsum_in.at[me], lambda k, origin: gsum_in.at[origin],
        ex_send.at[1], ex_recv.at[1],
    )
    sums.start()
    z_fold(8)
    z_end(5)
    load_hist.wait()
    for k in range(1, n):
        sums.wait(k)
    gsum_in[me] = gsum[...]
    total = gsum_in[0]
    for k in range(1, n):
        total = total + gsum_in[k]
    pre[0:8, :] = total * (1.0 / width)

    @pl.loop(0, n)
    def _(b):
        where = lanes(b)
        for s in range(4):
            xhat = deriv[s, :, where]
            value = stat[4 + s : 5 + s, where] * (
                gn[s, :, where] - pre[s : s + 1, where] - xhat * pre[4 + s : 5 + s, where]
            )
            if s == 3:
                direct = cot[rows(me), where].astype(f32)
                accs[12] = accs[12] + direct
                value = value + direct
            gn[s, :, where] = value
        for j in range(states):
            past = big[j, :, where].astype(f32)
            for s in range(4):
                gmix[b, 4 * j + s : 4 * j + s + 1, :] = jnp.sum(
                    gn[s, :, where] * past, axis=0, keepdims=True
                )

    mixes = Everyone(
        at, lambda to: gmix.at[to], lambda k: gmix_in.at[k], lambda k, origin: gmix_in.at[k],
        ex_send.at[2], ex_recv.at[2],
    )
    mixes.start()
    z_fold(9)
    z_end(6)

    @pl.loop(0, n)
    def _(b):
        where = lanes(b)
        for j in range(states - 1):
            value = pk[b, pl.ds(4 * j, 1), :] * gn[0, :, where]
            for s in range(1, 4):
                value = value + pk[b, pl.ds(4 * j + s, 1), :] * gn[s, :, where]
            hist_grad[j, :, where] = value.astype(bf16)

    total = gmix[me]
    for k in range(1, n):
        mixes.wait(k)
        total = total + gmix_in[k]
    grad_mix = total[0:m]
    table = jnp.concatenate([gout[j] for j in range(states)], axis=0)
    hidden, slope = gelu_pair(raw[0:hid, :] * pk[me, m : m + 1, :])
    grad_hidden = contract(table, grad_mix, 0, 0, precision=highest)
    low = (grad_hidden * slope).astype(bf16).astype(f32)
    genmsg[0:hid, :] = low
    genmsg[hid : hid + 8, :] = jnp.broadcast_to(
        jnp.sum(low * raw[0:hid, :], axis=0, keepdims=True) * (1.0 / width), (8, block)
    )
    owns = Everyone(
        at, lambda to: genmsg, lambda k: gen_in_all.at[me], lambda k, origin: gen_in_all.at[origin],
        ex_send.at[3], ex_recv.at[3],
    )
    owns.start()
    z_fold(10)
    z_end(7)
    _, _, valid = place(me, spot)
    kept = jnp.where(valid, 1.0, 0.0)
    ones = jnp.ones((8, block), f32)
    mixing = pk[me, 0:m, :]
    vec[...] = jnp.zeros_like(vec)
    vec[56 : 56 + hid, 0:m] = contract(hidden, grad_mix, 1, 1, precision=highest)
    for index, value in enumerate((grad_mix, mixing * kept, mixing * mixing * kept)):
        vec[96 + index : 97 + index, 0:m] = contract(ones, value, 1, 1, precision=highest)[0:1]
    vec[99:100, :] = jnp.broadcast_to(jnp.sum(kept, axis=1, keepdims=True), (1, block))
    gen_in_all[me] = genmsg[...]
    for k in range(1, n):
        owns.wait(k)
    gin_mine = gin[:, rows(me)]

    @pl.loop(0, n)
    def _(b):
        where = lanes(b)
        low_b = gen_in_all[b, 0:hid, :].astype(bf16)
        rms = pk[b, m : m + 1, :]
        last = big[states - 1, :, where].astype(f32)
        grad_gen = contract(gin_mine, low_b, 0, 0)
        accs[11] = accs[11] + grad_gen * last * rms
        normed = (last * rms * colp[:, 0:1]).astype(bf16)
        vec[16 : 16 + hid, :] = vec[16 : 16 + hid, :] + contract(low_b, normed, 1, 1)
        value = rms * grad_gen * colp[:, 0:1]
        value = value - last * (rms * rms * rms * gen_in_all[b, hid : hid + 1, :])
        for s in range(4):
            value = value + pk[b, pl.ds(4 * (states - 1) + s, 1), :] * gn[s, :, where]
        hist_grad[states - 1, :, where] = value.astype(bf16)

    prm[...] = jnp.zeros_like(prm)
    for index in range(13):
        prm[:, index : index + 1] = jnp.sum(accs[index], axis=1, keepdims=True)
    vec[0:16, :] = prm[...].T[0:16]
    for k in range(1, zn):
        pltpu.make_async_remote_copy(
            src_ref=vec, dst_ref=vec_z.at[zc], send_sem=ex_send.at[4, k], recv_sem=ex_recv.at[4, k],
            device_id={"dp": (zc + k) % zn}, device_id_type=MESH,
        ).start()
    z_fold(11)
    z_end(8)
    vec_z[zc] = vec[...]
    for k in range(1, zn):
        place_z = vec_z.at[(zc + zn - k) % zn]
        pltpu.make_async_remote_copy(
            src_ref=place_z, dst_ref=place_z, send_sem=ex_send.at[4, k], recv_sem=ex_recv.at[4, k],
            device_id={"dp": (zc + k) % zn}, device_id_type=MESH,
        ).wait()
    total = vec_z[0]
    for k in range(1, zn):
        total = total + vec_z[k]
    vec_sum[...] = total
    vec_all[me] = total
    alls = Everyone(
        at, lambda to: vec_sum, lambda k: vec_all.at[me], lambda k, origin: vec_all.at[origin],
        ex_send.at[5], ex_recv.at[5],
    )
    alls.start()
    z_fold(2)
    z_fold(1)
    z_end(9)
    z_end(10)
    for k in range(1, n):
        alls.wait(k)
    shared = vec_all[0, 56:104, :]
    for k in range(1, n):
        shared = shared + vec_all[k, 56:104, :]
    prm[...] = jnp.zeros_like(prm)
    prm[0:40, :] = shared[0:40]
    count = shared[43:44, 0:1]
    mean = shared[41:42] / count
    prm[40:41, :] = shared[40:41]
    prm[41:42, :] = mean
    prm[42:43, :] = shared[42:43] / count - mean * mean
    turned = prm[...].T
    for j in range(states):
        gout_tot[j] = turned[4 * j : 4 * j + 4, 0:hid]
        gbias_tot[:, j : j + 1] = turned[4 * j : 4 * j + 4, 40:41]
        mean_tot[:, j : j + 1] = turned[4 * j : 4 * j + 4, 41:42]
        var_tot[:, j : j + 1] = turned[4 * j : 4 * j + 4, 42:43]
    for k in range(n):
        where = pl.ds(k * feats, feats)
        bias_tot[:, where] = vec_all[k, 0:7, :]
        ngain_tot[:, where] = vec_all[k, 7:9, :]
        nbias_tot[:, where] = vec_all[k, 9:11, :]
        gain_tot[:, where] = vec_all[k, 11:12, :]
        outb_tot[:, where] = vec_all[k, 12:13, :]
        gin_tot[:, where] = vec_all[k, 16 : 16 + hid, :]
    z_fold(0)
    z_end(11)
    for c in (2, 1, 0):
        z_end(c)
    for c in range(12):
        z_drain(c)
    for i in range(5):
        rs_drain(i)
    for exchange in (turns, sums, mixes, owns, alls):
        exchange.drain()
    for copy in stages:
        copy.wait()


def back(n, zn, nbuf, cot_all, cols, pk, raw, scaled, st3, stat, history, gen_gain, gen_in, gen_out, norm_gain, in_bias, out_bias, w_in):
    f32, bf16 = jnp.float32, jnp.bfloat16
    states, feats, tokens = history.shape
    block = tokens // n
    width = n * feats
    hid = gen_in.shape[1]
    heads = feats // HEAD_DIM
    vmem = pl.BlockSpec(memory_space=pltpu.VMEM)
    anys = pl.BlockSpec(memory_space=pl.ANY)
    shape = jax.ShapeDtypeStruct
    dma = pltpu.SemaphoreType.DMA
    return pl.pallas_call(
        functools.partial(back_kernel, n, zn),
        out_shape=(
            shape((feats, tokens), bf16),
            shape((states, feats, tokens), bf16),
            shape((12, feats, width), bf16),
            shape((7, width), f32),
            shape((2, width), f32),
            shape((2, width), f32),
            shape((1, width), f32),
            shape((1, width), f32),
            shape((hid, width), f32),
            shape((states, 4, hid), f32),
            shape((4, states), f32),
            shape((4, states), f32),
            shape((4, states), f32),
        ),
        in_specs=[anys] * 5 + [vmem] * 11,
        out_specs=(vmem, vmem, anys) + (vmem,) * 10,
        scratch_shapes=[
            pltpu.VMEM((4 * n, feats, tokens), bf16),
            pltpu.VMEM((width, tokens), bf16),
            pltpu.VMEM((width, 5 * feats), bf16),
            pltpu.VMEM((feats, feats), f32),
            pltpu.VMEM((feats, feats), f32),
            pltpu.VMEM((3, feats, tokens), bf16),
            pltpu.VMEM((5 * feats, tokens), bf16),
            pltpu.VMEM((4, feats, tokens), f32),
            pltpu.VMEM((n * heads, block, block), f32),
            pltpu.VMEM((feats, tokens), bf16),
            pltpu.VMEM((7 * feats, tokens), bf16),
            pltpu.VMEM((5, width, feats), bf16),
            pltpu.VMEM((24, tokens), f32),
            pltpu.VMEM((13, feats, block), f32),
            pltpu.VMEM((4, feats, tokens), f32),
            pltpu.VMEM((5, width, tokens), bf16),
            pltpu.VMEM((5, 4, feats, tokens), bf16),
            pltpu.VMEM((5, 2, feats, tokens), bf16),
            pltpu.VMEM((5, feats, tokens), bf16),
            pltpu.VMEM((12, feats, width), bf16),
            pltpu.VMEM((12, feats, width), bf16),
            pltpu.VMEM((12, feats, width), bf16),
            pltpu.VMEM((8, tokens), f32),
            pltpu.VMEM((n, 8, tokens), f32),
            pltpu.VMEM((n, 40, block), f32),
            pltpu.VMEM((n, 40, block), f32),
            pltpu.VMEM((8, tokens), f32),
            pltpu.VMEM((hid + 8, block), f32),
            pltpu.VMEM((n, hid + 8, block), f32),
            pltpu.VMEM((104, feats), f32),
            pltpu.VMEM((zn, 104, feats), f32),
            pltpu.VMEM((104, feats), f32),
            pltpu.VMEM((n, 104, feats), f32),
            dma((9,)), dma((5, 7)), dma((5, 7)), dma((6, n)), dma((6, n)),
            dma((12, 3)), dma((12, 2)), dma((12,)),
        ],
        compiler_params=pltpu.CompilerParams(
            collective_id=2, has_side_effects=True, vmem_limit_bytes=67043328
        ),
        name="back",
    )(
        nbuf, cot_all, cols, history, scaled,
        w_in.transpose(1, 0, 2), pk, raw, st3, stat, gen_gain.reshape(1, width), gen_in.T,
        gen_out.transpose(2, 1, 0), norm_gain, in_bias, out_bias.reshape(1, width),
    )


def tp_device(
    history, cotangent, bucket_len, valid_len, gen_gain, gen_in, gen_out, gen_bias,
    norm_gain, norm_bias, w_in, in_bias, w_out, w_down, out_bias,
):
    n, zn = lax.axis_size("seq"), lax.axis_size("dp")
    nbuf, cot_all, cols, pk, raw, scaled, st3, stat = front(
        n, history, cotangent, bucket_len, valid_len, gen_gain, gen_in, gen_out, gen_bias,
        norm_gain, norm_bias, w_out, w_down,
    )
    (
        new_state, history_grad, totals, bias, ngain, nbias, gain, outb, gin, gout, gbias, mean, var,
    ) = back(
        n, zn, nbuf, cot_all, cols, pk, raw, scaled, st3, stat, history, gen_gain, gen_in, gen_out,
        norm_gain, in_bias, out_bias, w_in,
    )
    totals = totals.astype(jnp.float32)
    feats, width = totals.shape[1:]
    return (
        new_state, history_grad, mean, var, gain.reshape(width), gin.T, gout.transpose(2, 1, 0),
        gbias, ngain, nbias, totals[:7].transpose(1, 0, 2), bias, totals[7],
        totals[8:].transpose(1, 0, 2).reshape(feats, 4 * width), outb.reshape(width),
    )


def solution(mesh):
    in_specs = (
        P(None, "seq", "dp"),
        P("seq", "dp"),
        P("dp", "seq", None),
        P("dp", "seq", None),
        P(),
        P(),
        P(),
        P(),
        P(),
        P(),
        P("seq", None, None),
        P(),
        P("seq", None),
        P("seq", None),
        P(),
    )
    out_specs = (
        P("seq", "dp"),
        P(None, "seq", "dp"),
        P(),
        P(),
        P(),
        P(),
        P(),
        P(),
        P(),
        P(),
        P("seq", None, None),
        P(),
        P("seq", None),
        P("seq", None),
        P(),
    )
    by_feature = mesh.shape["seq"] == 8 and mesh.shape["dp"] in (1, 4)
    body = tp_device if by_feature else per_device
    return jax.shard_map(
        body, mesh=mesh, in_specs=in_specs, out_specs=out_specs, check_vma=False
    )
```

```python
import functools
import math

import jax
import jax.numpy as jnp
from jax import lax
from jax.experimental import pallas as pl
from jax.experimental.pallas import tpu as pltpu
from jax.sharding import PartitionSpec as P

HEADS = 16
HEAD_DIM = 64
ROT = 16


ln_eps = 1e-05
rms_eps = 1e-06
masked_score = -1e30
highest = lax.Precision.HIGHEST


def gelu_exact(values):
    return jax.nn.gelu(values, approximate=False)


def rotary_tables(position):
    freq_index = jnp.arange(ROT // 2, dtype=jnp.float32)
    inverse_freq = jnp.exp(freq_index * (-2.0 * math.log(10000.0) / ROT))
    angles = position.astype(jnp.float32)[:, None] * inverse_freq[None, :]
    return (jnp.cos(angles), jnp.sin(angles))


def rotate(values, cosine, sine):
    half = ROT // 2
    former = values[..., :half]
    latter = values[..., half:ROT]
    cos_heads = cosine[:, None, :]
    sin_heads = sine[:, None, :]
    return jnp.concatenate(
        [
            former * cos_heads - latter * sin_heads,
            latter * cos_heads + former * sin_heads,
            values[..., ROT:],
        ],
        axis=-1,
    )


def token_layout(lengths, counts, tokens):
    index = jnp.arange(tokens, dtype=jnp.int32)
    second = index >= lengths[0]
    position = index - jnp.where(second, lengths[0], 0)
    valid = position < jnp.where(second, counts[1], counts[0])
    return (second, position, valid)


def normalize(streams):
    centre = jnp.mean(streams, axis=-1, keepdims=True)
    centred = streams - centre
    inverse = lax.rsqrt(jnp.mean(centred * centred, axis=-1, keepdims=True) + ln_eps)
    return (centred * inverse, inverse)


def normalize_back(grad_scaled, scaled, inverse):
    mean_grad = jnp.mean(grad_scaled, axis=-1, keepdims=True)
    mean_along = jnp.mean(grad_scaled * scaled, axis=-1, keepdims=True)
    return inverse * (grad_scaled - mean_grad - scaled * mean_along)


def per_device(
    history,
    cotangent,
    bucket_len,
    valid_len,
    gen_gain,
    gen_in,
    gen_out,
    gen_bias,
    norm_gain,
    norm_bias,
    w_in,
    in_bias,
    w_out,
    w_down,
    out_bias,
):
    states = history.shape[0]
    stacked = jnp.concatenate([history, cotangent[None]], axis=0)
    arrived = lax.all_to_all(stacked, "seq", split_axis=2, concat_axis=1, tiled=True)
    arrived_rows = jnp.swapaxes(arrived, 1, 2)
    hist_local = arrived_rows[:states]
    cot_local = arrived_rows[states]
    tokens = hist_local.shape[1]
    width = hist_local.shape[2]
    second, position, valid = token_layout(bucket_len.reshape(2), valid_len.reshape(2), tokens)
    valid_float = valid.astype(jnp.float32)
    last = hist_local[states - 1].astype(jnp.float32)
    rms = lax.rsqrt(jnp.mean(last * last, axis=-1, keepdims=True) + rms_eps)
    gen_normed = (last * rms * gen_gain).astype(jnp.bfloat16)
    gen_pre = jnp.dot(gen_normed, gen_in, preferred_element_type=jnp.float32)
    gen_hidden, gen_pull = jax.vjp(gelu_exact, gen_pre)
    mixing = jnp.einsum("th,hsj->tsj", gen_hidden, gen_out, precision=highest) + gen_bias
    weighted = mixing * valid_float[:, None, None]
    stat_sums = jnp.sum(weighted, axis=0)
    stat_squares = jnp.sum(weighted * mixing, axis=0)
    stat_count = jnp.sum(valid_float)
    streams = mixing[:, :, 0].T[:, :, None] * hist_local[0]
    for state in range(1, states):
        streams = streams + mixing[:, :, state].T[:, :, None] * hist_local[state]
    scaled, inverse = normalize(streams)
    normed_attn = (scaled[:3] * norm_gain[0] + norm_bias[0]).astype(jnp.bfloat16)
    normed_mlp = (scaled[3] * norm_gain[1] + norm_bias[1]).astype(jnp.bfloat16)
    piece = lax.all_gather(w_in, "seq", axis=0, tiled=True)
    attn_part = jnp.einsum(
        "stk,nsk->stn", normed_attn, piece[:, :3], preferred_element_type=jnp.float32
    )
    mlp_part = jnp.einsum(
        "tk,njk->jtn", normed_mlp, piece[:, 3:], preferred_element_type=jnp.float32
    )
    projected = jnp.concatenate([attn_part, mlp_part], axis=0) + in_bias[:, None, :]
    cosine, sine = rotary_tables(position)
    heads_shape = (tokens, HEADS, HEAD_DIM)
    queries = (rotate(projected[0].reshape(heads_shape), cosine, sine) * HEAD_DIM ** (-0.5)).astype(
        jnp.bfloat16
    )
    keys = rotate(projected[1].reshape(heads_shape), cosine, sine).astype(jnp.bfloat16)
    values = projected[2].reshape(heads_shape).astype(jnp.bfloat16)
    index = jnp.arange(tokens, dtype=jnp.int32)
    allowed = (
        (second[:, None] == second[None, :]) & (index[None, :] <= index[:, None]) & valid[None, :]
    )
    scores = jnp.einsum("qhd,khd->hqk", queries, keys, preferred_element_type=jnp.float32)
    scores = jnp.where(allowed[None], scores, masked_score)
    top = jnp.max(scores, axis=-1, keepdims=True)
    weights = jnp.exp(scores - top)
    weight_total = jnp.sum(weights, axis=-1, keepdims=True)
    log_total = top + jnp.log(weight_total)
    probs_low = (weights / weight_total).astype(jnp.bfloat16)
    attended = jnp.einsum("hqk,khd->qhd", probs_low, values, preferred_element_type=jnp.float32)
    attn_low = attended.reshape(tokens, width).astype(jnp.bfloat16)
    gelu_up, up_pull = jax.vjp(gelu_exact, projected[3:])
    gelu_low = gelu_up.astype(jnp.bfloat16)
    grad_out_low = jnp.where(valid[:, None], cot_local, jnp.zeros_like(cot_local))
    piece_out, piece_down = lax.all_gather((w_out, w_down), "seq", axis=0, tiled=True)
    down_part = piece_down.reshape(piece_down.shape[0], 4, width)
    result = jnp.einsum("tk,nk->tn", attn_low, piece_out, preferred_element_type=jnp.float32)
    branch = result + jnp.einsum(
        "jtk,njk->tn", gelu_low, down_part, preferred_element_type=jnp.float32
    )
    new_local = (streams[3] + branch + out_bias).astype(jnp.bfloat16)
    piece_out = lax.all_gather(w_out, "seq", axis=0, tiled=True)
    piece_down = lax.all_gather(w_down, "seq", axis=0, tiled=True)
    count = piece_out.shape[0]
    part = grad_out_low
    attn_add = jnp.einsum("tn,nk->tk", part, piece_out, preferred_element_type=jnp.float32)
    gelu_add = jnp.einsum(
        "tn,njk->jtk", part, piece_down.reshape(count, 4, width), preferred_element_type=jnp.float32
    )
    grad_attn = attn_add
    part = grad_out_low
    term_out = jnp.einsum("tn,tk->nk", part, attn_low, preferred_element_type=jnp.float32)
    term_down = jnp.einsum(
        "tn,jtk->njk", part, gelu_low, preferred_element_type=jnp.float32
    ).reshape(lax.axis_size("seq") * w_out.shape[0], 4 * width)
    out_grads = lax.psum_scatter(
        jnp.concatenate([term_out, term_down], axis=1).astype(jnp.bfloat16),
        "seq",
        scatter_dimension=0,
        tiled=True,
    )
    out_bias_grad = jnp.sum(grad_out_low.astype(jnp.float32), axis=0)
    grad_attended = grad_attn.astype(jnp.bfloat16).reshape(heads_shape)
    rescored = jnp.einsum("qhd,khd->hqk", queries, keys, preferred_element_type=jnp.float32)
    probs = jnp.where(allowed[None], jnp.exp(rescored - log_total), 0.0)
    grad_values = jnp.einsum(
        "hqk,qhd->khd",
        probs.astype(jnp.bfloat16),
        grad_attended,
        preferred_element_type=jnp.float32,
    )
    grad_probs = jnp.einsum(
        "qhd,khd->hqk", grad_attended, values, preferred_element_type=jnp.float32
    )
    grad_scores = (
        probs * (grad_probs - jnp.sum(probs * grad_probs, axis=-1, keepdims=True))
    ).astype(jnp.bfloat16)
    grad_queries = jnp.einsum(
        "hqk,khd->qhd", grad_scores, keys, preferred_element_type=jnp.float32
    ) * HEAD_DIM ** (-0.5)
    grad_keys = jnp.einsum("hqk,qhd->khd", grad_scores, queries, preferred_element_type=jnp.float32)
    grad_up = up_pull(gelu_add)[0]
    grad_proj = jnp.concatenate(
        [
            rotate(grad_queries, cosine, -sine).reshape(1, tokens, width),
            rotate(grad_keys, cosine, -sine).reshape(1, tokens, width),
            grad_values.reshape(1, tokens, width),
            grad_up,
        ],
        axis=0,
    )
    in_bias_grad = jnp.sum(grad_proj, axis=1)
    grad_proj_low = grad_proj.astype(jnp.bfloat16)
    piece = lax.all_gather(w_in, "seq", axis=0, tiled=True)
    part = grad_proj_low
    attn_add = jnp.einsum(
        "stn,nsk->stk", part[:3], piece[:, :3], preferred_element_type=jnp.float32
    )
    mlp_add = jnp.einsum("jtn,njk->tk", part[3:], piece[:, 3:], preferred_element_type=jnp.float32)
    part = grad_proj_low
    attn_term = jnp.einsum(
        "stn,stk->nsk", part[:3], normed_attn, preferred_element_type=jnp.float32
    )
    mlp_term = jnp.einsum("jtn,tk->njk", part[3:], normed_mlp, preferred_element_type=jnp.float32)
    in_grads = lax.psum_scatter(
        jnp.concatenate([attn_term, mlp_term], axis=1).astype(jnp.bfloat16),
        "seq",
        scatter_dimension=0,
        tiled=True,
    )
    norm_gain_grad = jnp.stack(
        [jnp.sum(attn_add * scaled[:3], axis=(0, 1)), jnp.sum(mlp_add * scaled[3], axis=0)]
    )
    norm_bias_grad = jnp.stack([jnp.sum(attn_add, axis=(0, 1)), jnp.sum(mlp_add, axis=0)])
    grad_attn_streams = normalize_back(attn_add * norm_gain[0], scaled[:3], inverse[:3])
    grad_mlp_stream = normalize_back(
        mlp_add * norm_gain[1], scaled[3], inverse[3]
    ) + grad_out_low.astype(jnp.float32)
    grad_streams = jnp.concatenate([grad_attn_streams, grad_mlp_stream[None]], axis=0)
    grad_mixing = jnp.stack(
        [
            jnp.einsum(
                "std,td->ts", grad_streams, hist_local[state].astype(jnp.float32), precision=highest
            )
            for state in range(states)
        ],
        axis=-1,
    )
    hist_terms = [
        jnp.einsum("ts,std->td", mixing[:, :, state], grad_streams, precision=highest)
        for state in range(states)
    ]
    gen_bias_grad = jnp.sum(grad_mixing, axis=0)
    gen_out_grad = jnp.einsum("th,tsj->hsj", gen_hidden, grad_mixing, precision=highest)
    grad_hidden = jnp.einsum("tsj,hsj->th", grad_mixing, gen_out, precision=highest)
    grad_pre_low = gen_pull(grad_hidden)[0].astype(jnp.bfloat16)
    gen_in_grad = jnp.einsum(
        "tk,th->kh", gen_normed, grad_pre_low, preferred_element_type=jnp.float32
    )
    grad_gen = jnp.einsum("th,kh->tk", grad_pre_low, gen_in, preferred_element_type=jnp.float32)
    gen_gain_grad = jnp.sum(grad_gen * last * rms, axis=0)
    gained = grad_gen * gen_gain
    grad_last = rms * gained - last * (rms * rms * rms) * jnp.mean(
        gained * last, axis=-1, keepdims=True
    )
    hist_stack = jnp.stack(hist_terms[: states - 1] + [hist_terms[states - 1] + grad_last]).astype(
        jnp.bfloat16
    )
    departing = jnp.swapaxes(jnp.concatenate([new_local[None], hist_stack], axis=0), 1, 2)
    returned = lax.all_to_all(departing, "seq", split_axis=1, concat_axis=2, tiled=True)
    w_in_grad, out_total = (
        lax.psum(in_grads, "dp").astype(jnp.float32),
        lax.psum(out_grads, "dp").astype(jnp.float32),
    )
    w_out_grad = out_total[:, :width]
    w_down_grad = out_total[:, width:]
    joined = lax.psum(
        (
            gen_gain_grad,
            gen_in_grad,
            gen_out_grad,
            gen_bias_grad,
            norm_gain_grad,
            norm_bias_grad,
            in_bias_grad,
            out_bias_grad,
            stat_sums,
            stat_squares,
            stat_count,
        ),
        ("seq", "dp"),
    )
    small_totals = joined[:8]
    stat_totals = joined[8:]
    mix_mean = stat_totals[0] / stat_totals[2]
    mix_var = stat_totals[1] / stat_totals[2] - mix_mean * mix_mean
    return (
        returned[0],
        returned[1:],
        mix_mean,
        mix_var,
        small_totals[0],
        small_totals[1],
        small_totals[2],
        small_totals[3],
        small_totals[4],
        small_totals[5],
        w_in_grad,
        small_totals[6],
        w_out_grad,
        w_down_grad,
        small_totals[7],
    )


MESH = pl.DeviceIdType.MESH
HIDDEN_ROWS = 40
ROOT_HALF = math.sqrt(0.5)
INV_ROOT_2PI = 1.0 / math.sqrt(2.0 * math.pi)


def gelu_pair(x):
    half = 0.5 + 0.5 * lax.erf(x * ROOT_HALF)
    return x * half, half + x * (jnp.exp(-0.5 * x * x) * INV_ROOT_2PI)


def contract(a, b, dim_a, dim_b, precision=None):
    return lax.dot_general(
        a, b, (((dim_a,), (dim_b,)), ((), ())),
        precision=precision, preferred_element_type=jnp.float32,
    )


class Links:
    def __init__(self, n):
        self.n = n
        self.me = lax.axis_index("seq")
        core = self.me % 2
        xbit = (self.me // 2) % 2
        ybit = (self.me // 4) % 2
        flip = 1 - 2 * core
        x = self.me + 2 - 4 * xbit
        y = self.me + 4 - 8 * ybit
        self.core = core
        self.a = x * (1 - core) + y * core
        self.b = y * (1 - core) + x * core
        self.dg = x + y - self.me
        self.p = self.me + flip
        self.pa = self.b + flip
        self.pb = self.a + flip
        self.pdg = self.dg + flip

    def copy(self, src, dst, send, recv, to):
        return pltpu.make_async_remote_copy(
            src_ref=src, dst_ref=dst, send_sem=send, recv_sem=recv,
            device_id={"seq": to}, device_id_type=MESH,
        )


class Gather:
    def __init__(self, links, place, send, recv):
        self.links, self.place, self.send, self.recv = links, place, send, recv

    def _go(self, src, owner, slot, index, to):
        self.links.copy(
            src, self.place(owner), self.send.at[slot], self.recv.at[index], to
        ).start()

    def _got(self, owner, index):
        place = self.place(owner)
        self.links.copy(place, place, self.send.at[0], self.recv.at[index], self.links.p).wait_recv()

    def start(self, src):
        at = self.links
        self._go(src, at.me, 0, 0, at.a)
        self._go(src, at.me, 1, 1, at.b)
        self._go(src, at.me, 2, 3, at.p)

    def near(self):
        at = self.links
        self._got(at.a, 0)
        self._go(self.place(at.a), at.a, 3, 2, at.b)
        self._go(self.place(at.a), at.a, 4, 4, at.p)
        self._got(at.b, 1)
        self._go(self.place(at.b), at.b, 5, 5, at.p)

    def far(self):
        at = self.links
        self._got(at.dg, 2)
        self._go(self.place(at.dg), at.dg, 6, 6, at.p)

    def other(self):
        at = self.links
        for owner, index in ((at.p, 3), (at.pa, 4), (at.pb, 5), (at.pdg, 6)):
            self._got(owner, index)

    def drain(self):
        place = self.place(self.links.me)
        for slot in range(7):
            self.links.copy(
                place, place, self.send.at[slot], self.recv.at[0], self.links.p
            ).wait_send()


class Everyone:
    def __init__(self, links, source, target, arrived, send, recv):
        self.links, self.source, self.target, self.arrived = links, source, target, arrived
        self.send, self.recv = send, recv

    def start(self):
        at = self.links
        for k in range(1, at.n):
            to = (at.me + k) % at.n
            at.copy(
                self.source(to), self.target(k), self.send.at[k], self.recv.at[k], to
            ).start()

    def wait(self, k):
        at = self.links
        origin = (at.me + at.n - k) % at.n
        place = self.arrived(k, origin)
        at.copy(place, place, self.send.at[k], self.recv.at[k], at.p).wait_recv()
        return origin

    def drain(self):
        at = self.links
        for k in range(1, at.n):
            to = (at.me + k) % at.n
            place = self.source(to)
            at.copy(place, place, self.send.at[k], self.recv.at[k], at.p).wait_send()


COLS_EARLY = 2


def layer_kernel(
    n, zn,
    history, cotangent, lens, vals, gain, gin, gout, gbias, ng, nb, w_in, in_bias, w_out, w_down, out_bias,
    new_out, hist_out, totals,
    bias_tot, ngain_tot, nbias_tot, gain_tot, outb_tot, gin_tot, gout_tot,
    gbias_tot, mean_tot, var_tot,
    hist, new_state, big, cot, cols, w_turn, prm, colp, qkv, act, deriv, probs, gattn, gp, gcol, rope, accs, gn,
    scaled, st3, pk, raw, part, part_in, stat, stat_in, stat_out,
    ybuf, abuf, from_a, from_b, zown, zin, zmid,
    gsum, gsum_in, gmix, gmix_in, pre, genmsg, gen_in_all, vec, vec_z, vec_sum, vec_all,
    load_sem, ag_send, ag_recv, rs_send, rs_recv, ex_send, ex_recv, z_send, z_recv, out_sem,
):
    f32, bf16 = jnp.float32, jnp.bfloat16
    states, feats, tokens = hist.shape
    block = tokens // n
    width = n * feats
    hid = gin.shape[0]
    heads = feats // HEAD_DIM
    scale = HEAD_DIM ** (-0.5)
    m = 4 * states
    wide = 2 * block
    chunks = tokens // wide
    quarter = width // 4
    at = Links(n)
    me = at.me
    zc = lax.axis_index("dp")

    def rows(owner):
        return pl.ds(pl.multiple_of(owner * feats, feats), feats)

    def lanes(index, size=block):
        return pl.ds(pl.multiple_of(index * size, size), size)

    mine = rows(me)

    load_last = pltpu.make_async_copy(history.at[states - 1], hist.at[states - 1], load_sem.at[0])
    load_hist = pltpu.make_async_copy(
        history.at[pl.ds(0, states - 1)], hist.at[pl.ds(0, states - 1)], load_sem.at[1]
    )
    load_cot = pltpu.make_async_copy(cotangent, cot.at[mine, :], load_sem.at[2])
    for copy in (load_last, load_hist, load_cot):
        copy.start()
    barrier = pltpu.get_barrier_semaphore()
    for k in range(1, n):
        pl.semaphore_signal(
            barrier, inc=1, device_id={"seq": (me + k) % n}, device_id_type=MESH
        )
    for k in range(1, zn):
        pl.semaphore_signal(
            barrier, inc=1, device_id={"dp": (zc + k) % zn}, device_id_type=MESH
        )

    gathers = [
        Gather(at, lambda owner, s=s: big.at[s * n + owner], ag_send.at[s], ag_recv.at[s])
        for s in range(4)
    ]
    cots = Gather(at, lambda owner: cot.at[rows(owner), :], ag_send.at[4], ag_recv.at[4])
    parts = Everyone(
        at, lambda to: part.at[to], lambda k: part_in.at[k], lambda k, origin: part_in.at[k],
        ex_send.at[6], ex_recv.at[6],
    )
    spread_mix = Everyone(
        at, lambda to: pk.at[me], lambda k: pk.at[me], lambda k, origin: pk.at[origin],
        ex_send.at[7], ex_recv.at[7],
    )
    stats = Everyone(
        at, lambda to: stat, lambda k: stat_in.at[me], lambda k, origin: stat_in.at[origin],
        ex_send.at[8], ex_recv.at[8],
    )

    prm[...] = jnp.zeros_like(prm)
    prm[0:1, :] = gain[:, mine]
    prm[1:3, :] = ng[:, mine]
    prm[3:5, :] = nb[:, mine]
    prm[5:6, :] = out_bias[:, mine]
    prm[8:15, :] = in_bias[:, mine]
    colp[...] = prm[...].T
    accs[...] = jnp.zeros_like(accs)

    gin_mine = gin[:, mine]
    load_last.wait()
    for b in range(n):
        last = hist[states - 1, :, b * block : (b + 1) * block].astype(f32)
        product = (last * colp[:, 0:1]).astype(bf16)
        part[b, 0:hid, :] = jnp.dot(gin_mine, product, preferred_element_type=f32)
        part[b, hid : hid + 8, :] = jnp.broadcast_to(
            jnp.sum(last * last, axis=0, keepdims=True), (8, block)
        )
    pl.semaphore_wait(barrier, n - 1 + zn - 1)
    parts.start()

    @pl.loop(0, n)
    def _(r):
        for j in range(4):
            ybuf[0, rows(r), j * feats : (j + 1) * feats] = w_in[3 + j, :, lanes(r, feats)].T

    load_hist.wait()
    total = part[me]
    for k in range(1, n):
        parts.wait(k)
        total = total + part_in[k]
    raw[...] = total
    rms = lax.rsqrt(total[hid : hid + 1] * (1.0 / width) + rms_eps)
    hidden, _ = gelu_pair(total[0:hid] * rms)
    table = jnp.concatenate([gout[j] for j in range(states)], axis=0)
    mixing = jnp.dot(table, hidden, precision=highest, preferred_element_type=f32)
    for j in range(states):
        pk[me, 4 * j : 4 * j + 4, :] = mixing[4 * j : 4 * j + 4] + gbias[:, j : j + 1]
    pk[me, m : m + 1, :] = rms
    for offset, value in ((1, lens[0, 0, 0]), (2, vals[0, 0, 0]), (3, vals[0, 0, 1])):
        pk[me, m + offset : m + offset + 1, :] = jnp.full((1, block), value.astype(f32))
    spread_mix.start()

    def column_copy(to, j):
        if j == 0:
            src = w_out.at[:, rows(to)]
        else:
            src = w_down.at[:, pl.ds(pl.multiple_of((j - 1) * width + to * feats, feats), feats)]
        return src, cols.at[mine, pl.ds(j * feats, feats)]

    def send_columns(which):
        for j in which:
            for k in range(1, n):
                to = (me + k) % n
                src, dst = column_copy(to, j)
                at.copy(src, dst, ex_send.at[9, k], ex_recv.at[9, k], to).start()

    own_cols = [
        pltpu.make_async_copy(*column_copy(me, j), load_sem.at[3 + j]) for j in range(5)
    ]
    for copy in own_cols:
        copy.start()
    send_columns(range(COLS_EARLY))

    def mix_block(owner):
        where = lanes(owner)
        for half in range(2):
            part_rows = pl.ds(half * (feats // 2), feats // 2)
            sums = [None] * 4
            for j in range(states):
                value = hist[j, part_rows, where].astype(f32)
                for s in range(4):
                    weight = pk[owner, pl.ds(4 * j + s, 1), :]
                    term = weight * value
                    sums[s] = term if sums[s] is None else sums[s] + term
            for s in range(4):
                scaled[s, part_rows, where] = sums[s]
        for s in range(4):
            value = scaled[s, :, where]
            mean = jnp.sum(value, axis=0, keepdims=True) * (1.0 / feats)
            off = value - mean
            stat[pl.ds(s, 1), where] = mean
            stat[pl.ds(4 + s, 1), where] = jnp.sum(off * off, axis=0, keepdims=True)

    mix_block(me)

    @pl.loop(1, n)
    def _(k):
        mix_block(spread_mix.wait(k))

    stats.start()

    spot = lax.broadcasted_iota(jnp.int32, (1, block), 1).astype(f32)
    freq = jnp.exp(
        lax.broadcasted_iota(jnp.int32, (8, block), 0).astype(f32)
        * (-2.0 * math.log(10000.0) / ROT)
    )

    def place(owner, index):
        cut = pk[owner, m + 1 : m + 2, :]
        second = index >= cut
        position = index - jnp.where(second, cut, 0.0)
        limit = jnp.where(second, pk[owner, m + 3 : m + 4, :], pk[owner, m + 2 : m + 3, :])
        return second, position, position < limit

    load_cot.wait()
    for b in range(n):
        where = pl.ds(b * block, block)
        _, position, valid = place(b, spot)
        angle = freq * position
        rope[0:8, where] = jnp.cos(angle)
        rope[8:16, where] = jnp.sin(angle)
        kept = jnp.where(valid, 1.0, 0.0)
        cot[mine, where] = cot[mine, where] * kept.astype(bf16)

    @pl.loop(0, n)
    def _(r):
        for s in range(3):
            w_turn[rows(r), s * feats : (s + 1) * feats] = w_in[s, :, lanes(r, feats)].T

    for k in range(1, n):
        stats.wait(k)
    stat_in[me] = stat[...]
    means = stat_in[0, 0:4, :]
    for k in range(1, n):
        means = means + stat_in[k, 0:4, :]
    means = means * (1.0 / n)
    spread = jnp.zeros_like(means)
    for k in range(n):
        away = stat_in[k, 0:4, :] - means
        spread = spread + (stat_in[k, 4:8, :] + feats * (away * away))
    stat_out[0:4, :] = means
    stat_out[4:8, :] = lax.rsqrt(spread * (1.0 / width) + ln_eps)

    def normalise(s):
        which = 0 if s < 3 else 1

        @pl.loop(0, n)
        def _(b):
            where = lanes(b)
            value = scaled[s, :, where]
            if s == 3:
                st3[:, where] = value
            xhat = (value - stat_out[s : s + 1, where]) * stat_out[4 + s : 5 + s, where]
            scaled[s, :, where] = xhat
            big[s * n + me, :, where] = (
                xhat * colp[:, 1 + which : 2 + which] + colp[:, 3 + which : 4 + which]
            ).astype(bf16)

        gathers[s].start(big.at[s * n + me])

    def rotated(value, where, sign):
        cosine, sine = rope[0:8, where], rope[8:16, where] * sign
        out = []
        for h in range(heads):
            base = h * HEAD_DIM
            former, latter = value[base : base + 8], value[base + 8 : base + 16]
            out += [
                former * cosine - latter * sine,
                latter * cosine + former * sine,
                value[base + 16 : base + HEAD_DIM],
            ]
        return jnp.concatenate(out, axis=0)

    def stream(s, where):
        return big[pl.ds(s * n, n), :, where].reshape(width, -1)

    def project(s):
        @pl.loop(0, chunks)
        def _(c):
            where = lanes(c, wide)
            value = jnp.dot(w_in[s], stream(s, where), preferred_element_type=f32)
            value = value + colp[:, 8 + s : 9 + s]
            if s < 2:
                value = rotated(value, where, 1.0)
            if s == 0:
                value = value * scale
            qkv[s, :, where] = value.astype(bf16)

    def project_up(pair):
        @pl.loop(0, chunks)
        def _(c):
            where = lanes(c, wide)
            weight = w_in[3 + 2 * pair : 5 + 2 * pair].reshape(2 * feats, width)
            both = jnp.dot(weight, stream(3, where), preferred_element_type=f32)
            for i in range(2):
                j = 2 * pair + i
                up, slope = gelu_pair(
                    both[i * feats : (i + 1) * feats] + colp[:, 11 + j : 12 + j]
                )
                act[pl.ds((1 + j) * feats, feats), where] = up.astype(bf16)
                deriv[j, :, where] = slope

    normalise(3)
    normalise(0)
    gathers[3].near()
    normalise(1)
    gathers[0].near()
    normalise(2)
    gathers[3].far()
    gathers[3].other()
    project_up(0)
    gathers[1].near()
    gathers[0].far()
    project_up(1)
    gathers[2].near()
    cots.start(cot.at[mine, :])
    send_columns(range(COLS_EARLY, 5))
    gathers[0].other()
    project(0)
    gathers[1].far()
    gathers[1].other()
    project(1)
    gathers[2].far()
    gathers[2].other()
    project(2)

    key_at = lax.broadcasted_iota(jnp.int32, (block, block), 0).astype(f32)
    query_at = lax.broadcasted_iota(jnp.int32, (block, block), 1).astype(f32)

    @pl.loop(0, n // 2)
    def _(pair):
        chains = []
        for u in range(2):
            b = 2 * pair + u
            where = lanes(b)
            cut = pk[b, m + 1 : m + 2, :]
            _, _, valid = place(b, key_at)
            same = jnp.where(key_at >= cut, 1.0, 0.0) == jnp.where(query_at >= cut, 1.0, 0.0)
            allowed = same & (key_at <= query_at) & valid
            for h in range(heads):
                rows_h = pl.ds(h * HEAD_DIM, HEAD_DIM)
                scores = contract(qkv[1, rows_h, where], qkv[0, rows_h, where], 0, 0)
                chains.append((b, h, rows_h, where, allowed, scores))
        softs = []
        for b, h, rows_h, where, allowed, scores in chains:
            scores = jnp.where(allowed, scores, masked_score)
            weights = jnp.exp(scores - jnp.max(scores, axis=0, keepdims=True))
            softs.append(weights * (1.0 / jnp.sum(weights, axis=0, keepdims=True)))
        for (b, h, rows_h, where, _, _), soft in zip(chains, softs):
            probs[b * heads + h] = soft
            act[rows_h, where] = jnp.dot(
                qkv[2, rows_h, where], soft.astype(bf16), preferred_element_type=f32
            ).astype(bf16)

    def rs_copy(i, src, dst, slot, to):
        return at.copy(src, dst, rs_send.at[i, slot], rs_recv.at[i, slot], to)

    def rs_first(i):
        return [
            rs_copy(i, ybuf.at[i, rows(owner), :], abuf.at[i, q], q, at.p)
            for q, owner in enumerate((at.p, at.pa, at.pb, at.pdg))
        ]

    def rs_second(i):
        return [
            rs_copy(i, ybuf.at[i, rows(at.a), :], from_a.at[i, 0], 4, at.a),
            rs_copy(i, ybuf.at[i, rows(at.dg), :], from_a.at[i, 1], 5, at.a),
        ]

    def rs_third(i):
        return [rs_copy(i, ybuf.at[i, rows(at.b), :], from_b.at[i], 6, at.b)]

    def rs_start(i):
        for copy in rs_first(i):
            copy.start()

    def rs_fold(i):
        for copy in rs_first(i):
            copy.wait_recv()

        @pl.loop(0, chunks)
        def _(c):
            where = lanes(c, wide)
            for q, owner in ((1, at.a), (3, at.dg)):
                ybuf[i, rows(owner), where] = (
                    ybuf[i, rows(owner), where].astype(f32) + abuf[i, q, :, where].astype(f32)
                ).astype(bf16)

        for copy in rs_second(i):
            copy.start()

    def rs_pass(i):
        for copy in rs_second(i):
            copy.wait_recv()

        @pl.loop(0, chunks)
        def _(c):
            where = lanes(c, wide)
            ybuf[i, rows(at.b), where] = (
                ybuf[i, rows(at.b), where].astype(f32)
                + abuf[i, 2, :, where].astype(f32)
                + from_a[i, 1, :, where].astype(f32)
            ).astype(bf16)

        for copy in rs_third(i):
            copy.start()

    def rs_end(i):
        for copy in rs_third(i):
            copy.wait_recv()

    def rs_value(i, where):
        return (
            ybuf[i, rows(me), where].astype(f32)
            + abuf[i, 0, :, where].astype(f32)
            + from_a[i, 0, :, where].astype(f32)
            + from_b[i, :, where].astype(f32)
        )

    def rs_drain(i):
        for copy in rs_first(i) + rs_second(i) + rs_third(i):
            copy.wait_send()

    outer = (zc == 0) | (zc == 3)
    z_in = 1 + zc // 3
    z_out = 3 * (zc - 1)
    z_over = 3 - zc

    def z_copy(c, src, dst, slot, recv_slot, to):
        return pltpu.make_async_remote_copy(
            src_ref=src, dst_ref=dst, send_sem=z_send.at[c, slot], recv_sem=z_recv.at[c, recv_slot],
            device_id={"dp": to}, device_id_type=MESH,
        )

    def z_up(c):
        return z_copy(c, zown.at[c], zin.at[c], 0, 0, z_in)

    def z_cross(c):
        return z_copy(c, zown.at[c], zmid.at[c], 1, 1, z_over)

    def z_down(c):
        return z_copy(c, zin.at[c], zin.at[c], 2, 0, z_out)

    def z_start(c):
        if zn > 1:

            @pl.when(outer)
            def _():
                z_up(c).start()

    def z_fold(c):
        if zn > 1:

            @pl.when(jnp.logical_not(outer))
            def _():
                z_up(c).wait_recv()

                @pl.loop(0, chunks)
                def _(k):
                    where = lanes(k, wide)
                    zown[c, :, where] = (
                        zown[c, :, where].astype(f32) + zin[c, :, where].astype(f32)
                    ).astype(bf16)

                z_cross(c).start()

    stages = []

    def z_end(c):
        if zn > 1:

            @pl.when(jnp.logical_not(outer))
            def _():
                z_cross(c).wait_recv()

                @pl.loop(0, chunks)
                def _(k):
                    where = lanes(k, wide)
                    zin[c, :, where] = (
                        zown[c, :, where].astype(f32) + zmid[c, :, where].astype(f32)
                    ).astype(bf16)

                z_down(c).start()

            @pl.when(outer)
            def _():
                z_up(c).wait_recv()

        source = zin if zn > 1 else zown
        stages.append(pltpu.make_async_copy(source.at[c], totals.at[c], out_sem.at[c]))
        stages[-1].start()

    def z_drain(c):
        if zn > 1:

            @pl.when(outer)
            def _():
                z_up(c).wait_send()

            @pl.when(jnp.logical_not(outer))
            def _():
                z_cross(c).wait_send()
                z_down(c).wait_send()

    z_order = (3, 4, 5, 6, 7, 8, 9, 10, 11, 0, 1, 2)
    z_actions = []
    for t in range(14):
        if t < 12:
            z_actions.append((z_fold, z_order[t]))
        if t >= 2:
            z_actions.append((z_end, z_order[t - 2]))
    z_actions = iter(z_actions)

    def z_step(count):
        for _ in range(count):
            step, c = next(z_actions)
            step(c)


    cots.near()
    for k in range(1, n):
        arrived = cols.at[rows((me + n - k) % n), :]
        at.copy(arrived, arrived, ex_send.at[9, k], ex_recv.at[9, k], at.p).wait()
    for copy in own_cols:
        copy.wait()

    @pl.loop(0, chunks)
    def _(c):
        where = lanes(c, wide)
        for r in range(2):
            half = slice(r * width // 2, (r + 1) * width // 2)
            ybuf[4, half, where] = jnp.dot(
                cols[half, :], act[:, where], preferred_element_type=f32
            ).astype(bf16)

    rs_start(4)
    cots.far()

    @pl.loop(0, n)
    def _(r):
        for j in range(5):
            zown[j, :, lanes(r, feats)] = cols[rows(r), j * feats : (j + 1) * feats].T

    cots.other()

    @pl.loop(0, chunks)
    def _(c):
        where = lanes(c, wide)
        gattn[:, where] = jnp.dot(zown[0], cot[:, where], preferred_element_type=f32).astype(bf16)
        for pair in range(2):
            weight = zown[1 + 2 * pair : 3 + 2 * pair].reshape(2 * feats, width)
            both = jnp.dot(weight, cot[:, where], preferred_element_type=f32)
            for i in range(2):
                j = 2 * pair + i
                value = both[i * feats : (i + 1) * feats] * deriv[j, :, where]
                accs[3 + j] = accs[3 + j] + (value[:, :block] + value[:, block:])
                gp[pl.ds((3 + j) * feats, feats), where] = value.astype(bf16)

    def normed_grad(i, source, first, count):
        @pl.loop(0, chunks)
        def _(c):
            where = lanes(c, wide)
            for r in range(2):
                half = slice(r * width // 2, (r + 1) * width // 2)
                ybuf[i, half, where] = jnp.dot(
                    source[half, :], gp[first * feats : (first + count) * feats, where],
                    preferred_element_type=f32,
                ).astype(bf16)

        rs_start(i)

    def weight_grad(first, count, source):
        @pl.loop(0, 4)
        def _(r):
            part_in_rows = big[pl.ds(source * n + r * (n // 4), n // 4), :, :].reshape(quarter, tokens)
            value = contract(gp[first * feats : (first + count) * feats, :], part_in_rows, 1, 1)
            for s in range(count):
                zown[first + s, :, lanes(r, quarter)] = value[s * feats : (s + 1) * feats].astype(bf16)

        for s in range(first, first + count):
            z_start(s)

    rs_fold(4)
    normed_grad(3, ybuf.at[0, :, 0 : 4 * feats], 3, 4)
    weight_grad(3, 4, 3)
    for r in range(4):
        grads = contract(cot[r * quarter : (r + 1) * quarter, :], act[...], 1, 1).astype(bf16)
        for j in range(5):
            gcol[j, r * quarter : (r + 1) * quarter, :] = grads[:, j * feats : (j + 1) * feats]

    turns = Everyone(
        at,
        lambda to: gcol.at[:, rows(to), :],
        lambda k: zown.at[pl.ds(7, 5), :, mine],
        lambda k, origin: zown.at[pl.ds(7, 5), :, rows(origin)],
        ex_send.at[0], ex_recv.at[0],
    )
    turns.start()
    keep = pltpu.make_async_copy(
        gcol.at[:, mine, :], zown.at[pl.ds(7, 5), :, mine], load_sem.at[8]
    )
    keep.start()
    rs_pass(4)
    rs_fold(3)

    @pl.loop(0, n // 2)
    def _(pair):
        first = []
        for u in range(2):
            b = 2 * pair + u
            where = lanes(b)
            for h in range(heads):
                rows_h = pl.ds(h * HEAD_DIM, HEAD_DIM)
                soft = probs[b * heads + h]
                grad = gattn[rows_h, where]
                dprob = contract(qkv[2, rows_h, where], grad, 0, 0)
                values_grad = contract(grad, soft.astype(bf16), 1, 1)
                first.append((rows_h, where, soft, dprob, values_grad))
        lows = []
        for rows_h, where, soft, dprob, values_grad in first:
            inner = jnp.sum(soft * dprob, axis=0, keepdims=True)
            lows.append((soft * (dprob - inner)).astype(bf16))
        for u in range(2):
            where = first[u * heads][1]
            grads = [[], [], []]
            for h in range(heads):
                rows_h, _, _, _, values_grad = first[u * heads + h]
                low = lows[u * heads + h]
                grads[0].append(
                    jnp.dot(qkv[1, rows_h, where], low, preferred_element_type=f32) * scale
                )
                grads[1].append(contract(qkv[0, rows_h, where], low, 1, 1))
                grads[2].append(values_grad)
            for s in range(3):
                value = jnp.concatenate(grads[s], axis=0)
                if s < 2:
                    value = rotated(value, where, -1.0)
                accs[s] = accs[s] + value
                gp[pl.ds(s * feats, feats), where] = value.astype(bf16)

    for s in range(3):
        normed_grad(s, w_turn.at[:, s * feats : (s + 1) * feats], s, 1)
    rs_pass(3)
    z_step(1)
    rs_fold(0)
    for k in range(1, n):
        turns.wait(k)
    keep.wait()
    for c in range(7, 12):
        z_start(c)
    for s in range(3):
        weight_grad(s, 1, s)
    z_step(2)
    rs_fold(1)
    rs_end(4)

    @pl.loop(0, n)
    def _(b):
        where = lanes(b)
        new_state[:, where] = (st3[:, where] + rs_value(4, where) + colp[:, 5:6]).astype(bf16)

    keep_new = pltpu.make_async_copy(new_state, new_out, load_sem.at[9])
    keep_new.start()
    z_step(1)
    rs_pass(0)
    rs_fold(2)
    z_step(2)

    def norm_sums(s):
        which = 0 if s < 3 else 1

        @pl.loop(0, n)
        def _(b):
            where = lanes(b)
            value = rs_value(s, where)
            xhat = scaled[s, :, where]
            along = value * xhat
            accs[7 + which] = accs[7 + which] + along
            accs[9 + which] = accs[9 + which] + value
            factor = colp[:, 1 + which : 2 + which]
            gn[s, :, where] = value * factor
            gsum[s : s + 1, where] = jnp.sum(value * factor, axis=0, keepdims=True)
            gsum[4 + s : 5 + s, where] = jnp.sum(along * factor, axis=0, keepdims=True)

    rs_end(3)
    norm_sums(3)
    rs_pass(1)
    z_step(1)
    rs_end(0)
    norm_sums(0)
    rs_pass(2)
    z_step(2)
    rs_end(1)
    norm_sums(1)
    rs_end(2)
    norm_sums(2)
    sums = Everyone(
        at, lambda to: gsum, lambda k: gsum_in.at[me], lambda k, origin: gsum_in.at[origin],
        ex_send.at[1], ex_recv.at[1],
    )
    sums.start()
    z_step(2)
    for k in range(1, n):
        sums.wait(k)
    gsum_in[me] = gsum[...]
    total = gsum_in[0]
    for k in range(1, n):
        total = total + gsum_in[k]
    pre[0:8, :] = total * (1.0 / width)

    @pl.loop(0, n)
    def _(b):
        where = lanes(b)
        for s in range(4):
            xhat = scaled[s, :, where]
            value = stat_out[4 + s : 5 + s, where] * (
                gn[s, :, where] - pre[s : s + 1, where] - xhat * pre[4 + s : 5 + s, where]
            )
            if s == 3:
                direct = cot[mine, where].astype(f32)
                accs[12] = accs[12] + direct
                value = value + direct
            gn[s, :, where] = value
        for j in range(states):
            past = hist[j, :, where].astype(f32)
            for s in range(4):
                gmix[b, 4 * j + s : 4 * j + s + 1, :] = jnp.sum(
                    gn[s, :, where] * past, axis=0, keepdims=True
                )

    mixes = Everyone(
        at, lambda to: gmix.at[to], lambda k: gmix_in.at[k], lambda k, origin: gmix_in.at[k],
        ex_send.at[2], ex_recv.at[2],
    )
    mixes.start()
    z_step(2)

    @pl.loop(0, n)
    def _(b):
        where = lanes(b)
        for j in range(states - 1):
            value = pk[b, pl.ds(4 * j, 1), :] * gn[0, :, where]
            for s in range(1, 4):
                value = value + pk[b, pl.ds(4 * j + s, 1), :] * gn[s, :, where]
            hist[j, :, where] = value.astype(bf16)

    keep_hist = pltpu.make_async_copy(
        hist.at[pl.ds(0, states - 1)], hist_out.at[pl.ds(0, states - 1)], load_sem.at[10]
    )
    keep_hist.start()

    total = gmix[me]
    for k in range(1, n):
        mixes.wait(k)
        total = total + gmix_in[k]
    grad_mix = total[0:m]
    table = jnp.concatenate([gout[j] for j in range(states)], axis=0)
    hidden, slope = gelu_pair(raw[0:hid, :] * pk[me, m : m + 1, :])
    grad_hidden = contract(table, grad_mix, 0, 0, precision=highest)
    low = (grad_hidden * slope).astype(bf16).astype(f32)
    genmsg[0:hid, :] = low
    genmsg[hid : hid + 8, :] = jnp.broadcast_to(
        jnp.sum(low * raw[0:hid, :], axis=0, keepdims=True) * (1.0 / width), (8, block)
    )
    owns = Everyone(
        at, lambda to: genmsg, lambda k: gen_in_all.at[me], lambda k, origin: gen_in_all.at[origin],
        ex_send.at[3], ex_recv.at[3],
    )
    owns.start()
    z_step(2)
    _, _, valid = place(me, spot)
    kept = jnp.where(valid, 1.0, 0.0)
    ones = jnp.ones((8, block), f32)
    mixing = pk[me, 0:m, :]
    vec[...] = jnp.zeros_like(vec)
    vec[56 : 56 + hid, 0:m] = contract(hidden, grad_mix, 1, 1, precision=highest)
    for index, value in enumerate((grad_mix, mixing * kept, mixing * mixing * kept)):
        vec[96 + index : 97 + index, 0:m] = contract(ones, value, 1, 1, precision=highest)[0:1]
    vec[99:100, :] = jnp.broadcast_to(jnp.sum(kept, axis=1, keepdims=True), (1, block))
    gen_in_all[me] = genmsg[...]
    for k in range(1, n):
        owns.wait(k)
    gin_mine = gin[:, rows(me)]

    @pl.loop(0, n)
    def _(b):
        where = lanes(b)
        low_b = gen_in_all[b, 0:hid, :].astype(bf16)
        rms = pk[b, m : m + 1, :]
        last = hist[states - 1, :, where].astype(f32)
        grad_gen = contract(gin_mine, low_b, 0, 0)
        accs[11] = accs[11] + grad_gen * last * rms
        normed = (last * rms * colp[:, 0:1]).astype(bf16)
        vec[16 : 16 + hid, :] = vec[16 : 16 + hid, :] + contract(low_b, normed, 1, 1)
        value = rms * grad_gen * colp[:, 0:1]
        value = value - last * (rms * rms * rms * gen_in_all[b, hid : hid + 1, :])
        for s in range(4):
            value = value + pk[b, pl.ds(4 * (states - 1) + s, 1), :] * gn[s, :, where]
        hist[states - 1, :, where] = value.astype(bf16)

    keep_last = pltpu.make_async_copy(hist.at[states - 1], hist_out.at[states - 1], load_sem.at[11])
    keep_last.start()

    prm[...] = jnp.zeros_like(prm)
    for index in range(13):
        prm[:, index : index + 1] = jnp.sum(accs[index], axis=1, keepdims=True)
    vec[0:16, :] = prm[...].T[0:16]
    for k in range(1, zn):
        pltpu.make_async_remote_copy(
            src_ref=vec, dst_ref=vec_z.at[zc], send_sem=ex_send.at[4, k], recv_sem=ex_recv.at[4, k],
            device_id={"dp": (zc + k) % zn}, device_id_type=MESH,
        ).start()
    z_step(2)
    vec_z[zc] = vec[...]
    for k in range(1, zn):
        place_z = vec_z.at[(zc + zn - k) % zn]
        pltpu.make_async_remote_copy(
            src_ref=place_z, dst_ref=place_z, send_sem=ex_send.at[4, k], recv_sem=ex_recv.at[4, k],
            device_id={"dp": (zc + k) % zn}, device_id_type=MESH,
        ).wait()
    total = vec_z[0]
    for k in range(1, zn):
        total = total + vec_z[k]
    vec_sum[...] = total
    vec_all[me] = total
    alls = Everyone(
        at, lambda to: vec_sum, lambda k: vec_all.at[me], lambda k, origin: vec_all.at[origin],
        ex_send.at[5], ex_recv.at[5],
    )
    alls.start()
    z_step(2)
    for k in range(1, n):
        alls.wait(k)
    shared = vec_all[0, 56:104, :]
    for k in range(1, n):
        shared = shared + vec_all[k, 56:104, :]
    prm[...] = jnp.zeros_like(prm)
    prm[0:40, :] = shared[0:40]
    count = shared[43:44, 0:1]
    mean = shared[41:42] / count
    prm[40:41, :] = shared[40:41]
    prm[41:42, :] = mean
    prm[42:43, :] = shared[42:43] / count - mean * mean
    turned = prm[...].T
    for j in range(states):
        gout_tot[j] = turned[4 * j : 4 * j + 4, 0:hid]
        gbias_tot[:, j : j + 1] = turned[4 * j : 4 * j + 4, 40:41]
        mean_tot[:, j : j + 1] = turned[4 * j : 4 * j + 4, 41:42]
        var_tot[:, j : j + 1] = turned[4 * j : 4 * j + 4, 42:43]
    for k in range(n):
        where = pl.ds(k * feats, feats)
        bias_tot[:, where] = vec_all[k, 0:7, :]
        ngain_tot[:, where] = vec_all[k, 7:9, :]
        nbias_tot[:, where] = vec_all[k, 9:11, :]
        gain_tot[:, where] = vec_all[k, 11:12, :]
        outb_tot[:, where] = vec_all[k, 12:13, :]
        gin_tot[:, where] = vec_all[k, 16 : 16 + hid, :]
    for step, c in z_actions:
        step(c)
    for c in range(12):
        z_drain(c)
    for i in range(5):
        rs_drain(i)
    for g in [cots] + gathers:
        g.drain()
    for exchange in (parts, spread_mix, stats, turns, sums, mixes, owns, alls):
        exchange.drain()
    for copy in stages + [keep_new, keep_hist, keep_last]:
        copy.wait()


def layer(n, zn, history, cotangent, bucket_len, valid_len, gen_gain, gen_in, gen_out, gen_bias, norm_gain, norm_bias, w_in, in_bias, w_out, w_down, out_bias):
    f32, bf16 = jnp.float32, jnp.bfloat16
    states, feats, tokens = history.shape
    block = tokens // n
    width = n * feats
    hid = gen_in.shape[1]
    heads = feats // HEAD_DIM
    vmem = pl.BlockSpec(memory_space=pltpu.VMEM)
    smem = pl.BlockSpec(memory_space=pltpu.SMEM)
    anys = pl.BlockSpec(memory_space=pl.ANY)
    shape = jax.ShapeDtypeStruct
    dma = pltpu.SemaphoreType.DMA
    return pl.pallas_call(
        functools.partial(layer_kernel, n, zn),
        out_shape=(
            shape((feats, tokens), bf16),
            shape((states, feats, tokens), bf16),
            shape((12, feats, width), bf16),
            shape((7, width), f32),
            shape((2, width), f32),
            shape((2, width), f32),
            shape((1, width), f32),
            shape((1, width), f32),
            shape((hid, width), f32),
            shape((states, 4, hid), f32),
            shape((4, states), f32),
            shape((4, states), f32),
            shape((4, states), f32),
        ),
        in_specs=[anys] * 2 + [smem] * 2 + [vmem] * 8 + [anys] * 2 + [vmem],
        out_specs=(anys,) * 3 + (vmem,) * 10,
        scratch_shapes=[
            pltpu.VMEM((states, feats, tokens), bf16),
            pltpu.VMEM((feats, tokens), bf16),
            pltpu.VMEM((4 * n, feats, tokens), bf16),
            pltpu.VMEM((width, tokens), bf16),
            pltpu.VMEM((width, 5 * feats), bf16),
            pltpu.VMEM((width, 3 * feats), bf16),
            pltpu.VMEM((feats, feats), f32),
            pltpu.VMEM((feats, feats), f32),
            pltpu.VMEM((3, feats, tokens), bf16),
            pltpu.VMEM((5 * feats, tokens), bf16),
            pltpu.VMEM((4, feats, tokens), f32),
            pltpu.VMEM((n * heads, block, block), f32),
            pltpu.VMEM((feats, tokens), bf16),
            pltpu.VMEM((7 * feats, tokens), bf16),
            pltpu.VMEM((5, width, feats), bf16),
            pltpu.VMEM((16, tokens), f32),
            pltpu.VMEM((13, feats, block), f32),
            pltpu.VMEM((4, feats, tokens), f32),
            pltpu.VMEM((4, feats, tokens), f32),
            pltpu.VMEM((feats, tokens), f32),
            pltpu.VMEM((n, 40, block), f32),
            pltpu.VMEM((hid + 8, block), f32),
            pltpu.VMEM((n, hid + 8, block), f32),
            pltpu.VMEM((n, hid + 8, block), f32),
            pltpu.VMEM((8, tokens), f32),
            pltpu.VMEM((n, 8, tokens), f32),
            pltpu.VMEM((8, tokens), f32),
            pltpu.VMEM((5, width, tokens), bf16),
            pltpu.VMEM((5, 4, feats, tokens), bf16),
            pltpu.VMEM((5, 2, feats, tokens), bf16),
            pltpu.VMEM((5, feats, tokens), bf16),
            pltpu.VMEM((12, feats, width), bf16),
            pltpu.VMEM((12, feats, width), bf16),
            pltpu.VMEM((12, feats, width), bf16),
            pltpu.VMEM((8, tokens), f32),
            pltpu.VMEM((n, 8, tokens), f32),
            pltpu.VMEM((n, 40, block), f32),
            pltpu.VMEM((n, 40, block), f32),
            pltpu.VMEM((8, tokens), f32),
            pltpu.VMEM((hid + 8, block), f32),
            pltpu.VMEM((n, hid + 8, block), f32),
            pltpu.VMEM((104, feats), f32),
            pltpu.VMEM((zn, 104, feats), f32),
            pltpu.VMEM((104, feats), f32),
            pltpu.VMEM((n, 104, feats), f32),
            dma((12,)), dma((5, 7)), dma((5, 7)), dma((5, 7)), dma((5, 7)), dma((10, n)), dma((10, n)),
            dma((12, 3)), dma((12, 2)), dma((12,)),
        ],
        compiler_params=pltpu.CompilerParams(
            collective_id=1, has_side_effects=True, vmem_limit_bytes=67043328
        ),
        name="layer",
    )(
        history, cotangent, bucket_len, valid_len, gen_gain.reshape(1, width), gen_in.T,
        gen_out.transpose(2, 1, 0), gen_bias, norm_gain, norm_bias, w_in.transpose(1, 0, 2), in_bias,
        w_out, w_down, out_bias.reshape(1, width),
    )


def finish_kernel(new_in, hist_in, totals, *refs):
    count = (len(refs) - 10) // 2
    small_in = refs[:count]
    new_out, hist_out, in_out, out_out, down_out = refs[count : count + 5]
    small_out = refs[count + 5 : 2 * count + 5]
    new_buf, hist_buf, low, full, sem_in = refs[2 * count + 5 :]
    width = totals.shape[2]
    states = hist_in.shape[0]
    sources = [(new_in, new_buf)] + [(hist_in.at[j], hist_buf.at[j]) for j in range(states)]
    sources += [(totals.at[c], low.at[c]) for c in range(12)]
    targets = [(new_buf, new_out)] + [(hist_buf.at[j], hist_out.at[j]) for j in range(states)]
    for c in range(12):
        if c < 7:
            targets.append((full.at[c], in_out.at[c]))
        elif c == 7:
            targets.append((full.at[c], out_out))
        else:
            targets.append((full.at[c], down_out.at[:, (c - 8) * width : (c - 7) * width]))
    loads = [pltpu.make_async_copy(a, b, sem_in.at[0, i]) for i, (a, b) in enumerate(sources)]
    stores = [pltpu.make_async_copy(a, b, sem_in.at[1, i]) for i, (a, b) in enumerate(targets)]
    order = list(range(1 + states, 13 + states)) + list(range(1 + states))
    for i in order:
        loads[i].start()
    for a, b in zip(small_in, small_out):
        b[...] = a[...]
    for i in order:
        loads[i].wait()
        if i > states:
            c = i - 1 - states
            full[c] = low[c].astype(jnp.float32)
        stores[i].start()
    for copy in stores:
        copy.wait()


def finish(new_state, history_grad, totals, smalls):
    f32, bf16 = jnp.float32, jnp.bfloat16
    feats, width = totals.shape[1:]
    vmem = pl.BlockSpec(memory_space=pltpu.VMEM)
    anys = pl.BlockSpec(memory_space=pl.ANY)
    shape = jax.ShapeDtypeStruct
    return pl.pallas_call(
        finish_kernel,
        out_shape=(
            shape(new_state.shape, bf16),
            shape(history_grad.shape, bf16),
            shape((7, feats, width), f32),
            shape((feats, width), f32),
            shape((feats, 4 * width), f32),
        ) + tuple(shape(x.shape, x.dtype) for x in smalls),
        in_specs=[anys] * 3 + [vmem] * len(smalls),
        out_specs=(anys,) * 5 + (vmem,) * len(smalls),
        scratch_shapes=[
            pltpu.VMEM(new_state.shape, bf16),
            pltpu.VMEM(history_grad.shape, bf16),
            pltpu.VMEM(totals.shape, bf16),
            pltpu.VMEM(totals.shape, f32),
            pltpu.SemaphoreType.DMA((2, 13 + history_grad.shape[0])),
        ],
        compiler_params=pltpu.CompilerParams(vmem_limit_bytes=40 * 2**20),
        name="finish",
    )(new_state, history_grad, totals, *smalls)


def tp_device(
    history, cotangent, bucket_len, valid_len, gen_gain, gen_in, gen_out, gen_bias,
    norm_gain, norm_bias, w_in, in_bias, w_out, w_down, out_bias,
):
    n, zn = lax.axis_size("seq"), lax.axis_size("dp")
    new_state, history_grad, totals, *smalls = layer(
        n, zn, history, cotangent, bucket_len, valid_len, gen_gain, gen_in, gen_out, gen_bias,
        norm_gain, norm_bias, w_in, in_bias, w_out, w_down, out_bias,
    )
    (
        new_state, history_grad, in_grad, out_grad, down_grad,
        bias, ngain, nbias, gain, outb, gin, gout, gbias, mean, var,
    ) = finish(new_state, history_grad, totals, smalls)
    width = gen_gain.shape[0]
    return (
        new_state, history_grad, mean, var, gain.reshape(width), gin.T, gout.transpose(2, 1, 0),
        gbias, ngain, nbias, in_grad.transpose(1, 0, 2), bias, out_grad, down_grad, outb.reshape(width),
    )


def solution(mesh):
    in_specs = (
        P(None, "seq", "dp"),
        P("seq", "dp"),
        P("dp", "seq", None),
        P("dp", "seq", None),
        P(),
        P(),
        P(),
        P(),
        P(),
        P(),
        P("seq", None, None),
        P(),
        P("seq", None),
        P("seq", None),
        P(),
    )
    out_specs = (
        P("seq", "dp"),
        P(None, "seq", "dp"),
        P(),
        P(),
        P(),
        P(),
        P(),
        P(),
        P(),
        P(),
        P("seq", None, None),
        P(),
        P("seq", None),
        P("seq", None),
        P(),
    )
    by_feature = mesh.shape["seq"] == 8 and mesh.shape["dp"] in (1, 4)
    body = tp_device if by_feature else per_device
    return jax.shard_map(
        body, mesh=mesh, in_specs=in_specs, out_specs=out_specs, check_vma=False
    )
```

```python
import functools
import math

import jax
import jax.numpy as jnp
from jax import lax
from jax.experimental import pallas as pl
from jax.experimental.pallas import tpu as pltpu
from jax.sharding import PartitionSpec as P

HEADS = 16
HEAD_DIM = 64
ROT = 16


ln_eps = 1e-05
rms_eps = 1e-06
masked_score = -1e30
highest = lax.Precision.HIGHEST


def gelu_exact(values):
    return jax.nn.gelu(values, approximate=False)


def rotary_tables(position):
    freq_index = jnp.arange(ROT // 2, dtype=jnp.float32)
    inverse_freq = jnp.exp(freq_index * (-2.0 * math.log(10000.0) / ROT))
    angles = position.astype(jnp.float32)[:, None] * inverse_freq[None, :]
    return (jnp.cos(angles), jnp.sin(angles))


def rotate(values, cosine, sine):
    half = ROT // 2
    former = values[..., :half]
    latter = values[..., half:ROT]
    cos_heads = cosine[:, None, :]
    sin_heads = sine[:, None, :]
    return jnp.concatenate(
        [
            former * cos_heads - latter * sin_heads,
            latter * cos_heads + former * sin_heads,
            values[..., ROT:],
        ],
        axis=-1,
    )


def token_layout(lengths, counts, tokens):
    index = jnp.arange(tokens, dtype=jnp.int32)
    second = index >= lengths[0]
    position = index - jnp.where(second, lengths[0], 0)
    valid = position < jnp.where(second, counts[1], counts[0])
    return (second, position, valid)


def normalize(streams):
    centre = jnp.mean(streams, axis=-1, keepdims=True)
    centred = streams - centre
    inverse = lax.rsqrt(jnp.mean(centred * centred, axis=-1, keepdims=True) + ln_eps)
    return (centred * inverse, inverse)


def normalize_back(grad_scaled, scaled, inverse):
    mean_grad = jnp.mean(grad_scaled, axis=-1, keepdims=True)
    mean_along = jnp.mean(grad_scaled * scaled, axis=-1, keepdims=True)
    return inverse * (grad_scaled - mean_grad - scaled * mean_along)


def per_device(
    history,
    cotangent,
    bucket_len,
    valid_len,
    gen_gain,
    gen_in,
    gen_out,
    gen_bias,
    norm_gain,
    norm_bias,
    w_in,
    in_bias,
    w_out,
    w_down,
    out_bias,
):
    states = history.shape[0]
    stacked = jnp.concatenate([history, cotangent[None]], axis=0)
    arrived = lax.all_to_all(stacked, "seq", split_axis=2, concat_axis=1, tiled=True)
    arrived_rows = jnp.swapaxes(arrived, 1, 2)
    hist_local = arrived_rows[:states]
    cot_local = arrived_rows[states]
    tokens = hist_local.shape[1]
    width = hist_local.shape[2]
    second, position, valid = token_layout(bucket_len.reshape(2), valid_len.reshape(2), tokens)
    valid_float = valid.astype(jnp.float32)
    last = hist_local[states - 1].astype(jnp.float32)
    rms = lax.rsqrt(jnp.mean(last * last, axis=-1, keepdims=True) + rms_eps)
    gen_normed = (last * rms * gen_gain).astype(jnp.bfloat16)
    gen_pre = jnp.dot(gen_normed, gen_in, preferred_element_type=jnp.float32)
    gen_hidden, gen_pull = jax.vjp(gelu_exact, gen_pre)
    mixing = jnp.einsum("th,hsj->tsj", gen_hidden, gen_out, precision=highest) + gen_bias
    weighted = mixing * valid_float[:, None, None]
    stat_sums = jnp.sum(weighted, axis=0)
    stat_squares = jnp.sum(weighted * mixing, axis=0)
    stat_count = jnp.sum(valid_float)
    streams = mixing[:, :, 0].T[:, :, None] * hist_local[0]
    for state in range(1, states):
        streams = streams + mixing[:, :, state].T[:, :, None] * hist_local[state]
    scaled, inverse = normalize(streams)
    normed_attn = (scaled[:3] * norm_gain[0] + norm_bias[0]).astype(jnp.bfloat16)
    normed_mlp = (scaled[3] * norm_gain[1] + norm_bias[1]).astype(jnp.bfloat16)
    piece = lax.all_gather(w_in, "seq", axis=0, tiled=True)
    attn_part = jnp.einsum(
        "stk,nsk->stn", normed_attn, piece[:, :3], preferred_element_type=jnp.float32
    )
    mlp_part = jnp.einsum(
        "tk,njk->jtn", normed_mlp, piece[:, 3:], preferred_element_type=jnp.float32
    )
    projected = jnp.concatenate([attn_part, mlp_part], axis=0) + in_bias[:, None, :]
    cosine, sine = rotary_tables(position)
    heads_shape = (tokens, HEADS, HEAD_DIM)
    queries = (rotate(projected[0].reshape(heads_shape), cosine, sine) * HEAD_DIM ** (-0.5)).astype(
        jnp.bfloat16
    )
    keys = rotate(projected[1].reshape(heads_shape), cosine, sine).astype(jnp.bfloat16)
    values = projected[2].reshape(heads_shape).astype(jnp.bfloat16)
    index = jnp.arange(tokens, dtype=jnp.int32)
    allowed = (
        (second[:, None] == second[None, :]) & (index[None, :] <= index[:, None]) & valid[None, :]
    )
    scores = jnp.einsum("qhd,khd->hqk", queries, keys, preferred_element_type=jnp.float32)
    scores = jnp.where(allowed[None], scores, masked_score)
    top = jnp.max(scores, axis=-1, keepdims=True)
    weights = jnp.exp(scores - top)
    weight_total = jnp.sum(weights, axis=-1, keepdims=True)
    log_total = top + jnp.log(weight_total)
    probs_low = (weights / weight_total).astype(jnp.bfloat16)
    attended = jnp.einsum("hqk,khd->qhd", probs_low, values, preferred_element_type=jnp.float32)
    attn_low = attended.reshape(tokens, width).astype(jnp.bfloat16)
    gelu_up, up_pull = jax.vjp(gelu_exact, projected[3:])
    gelu_low = gelu_up.astype(jnp.bfloat16)
    grad_out_low = jnp.where(valid[:, None], cot_local, jnp.zeros_like(cot_local))
    piece_out, piece_down = lax.all_gather((w_out, w_down), "seq", axis=0, tiled=True)
    down_part = piece_down.reshape(piece_down.shape[0], 4, width)
    result = jnp.einsum("tk,nk->tn", attn_low, piece_out, preferred_element_type=jnp.float32)
    branch = result + jnp.einsum(
        "jtk,njk->tn", gelu_low, down_part, preferred_element_type=jnp.float32
    )
    new_local = (streams[3] + branch + out_bias).astype(jnp.bfloat16)
    piece_out = lax.all_gather(w_out, "seq", axis=0, tiled=True)
    piece_down = lax.all_gather(w_down, "seq", axis=0, tiled=True)
    count = piece_out.shape[0]
    part = grad_out_low
    attn_add = jnp.einsum("tn,nk->tk", part, piece_out, preferred_element_type=jnp.float32)
    gelu_add = jnp.einsum(
        "tn,njk->jtk", part, piece_down.reshape(count, 4, width), preferred_element_type=jnp.float32
    )
    grad_attn = attn_add
    part = grad_out_low
    term_out = jnp.einsum("tn,tk->nk", part, attn_low, preferred_element_type=jnp.float32)
    term_down = jnp.einsum(
        "tn,jtk->njk", part, gelu_low, preferred_element_type=jnp.float32
    ).reshape(lax.axis_size("seq") * w_out.shape[0], 4 * width)
    out_grads = lax.psum_scatter(
        jnp.concatenate([term_out, term_down], axis=1).astype(jnp.bfloat16),
        "seq",
        scatter_dimension=0,
        tiled=True,
    )
    out_bias_grad = jnp.sum(grad_out_low.astype(jnp.float32), axis=0)
    grad_attended = grad_attn.astype(jnp.bfloat16).reshape(heads_shape)
    rescored = jnp.einsum("qhd,khd->hqk", queries, keys, preferred_element_type=jnp.float32)
    probs = jnp.where(allowed[None], jnp.exp(rescored - log_total), 0.0)
    grad_values = jnp.einsum(
        "hqk,qhd->khd",
        probs.astype(jnp.bfloat16),
        grad_attended,
        preferred_element_type=jnp.float32,
    )
    grad_probs = jnp.einsum(
        "qhd,khd->hqk", grad_attended, values, preferred_element_type=jnp.float32
    )
    grad_scores = (
        probs * (grad_probs - jnp.sum(probs * grad_probs, axis=-1, keepdims=True))
    ).astype(jnp.bfloat16)
    grad_queries = jnp.einsum(
        "hqk,khd->qhd", grad_scores, keys, preferred_element_type=jnp.float32
    ) * HEAD_DIM ** (-0.5)
    grad_keys = jnp.einsum("hqk,qhd->khd", grad_scores, queries, preferred_element_type=jnp.float32)
    grad_up = up_pull(gelu_add)[0]
    grad_proj = jnp.concatenate(
        [
            rotate(grad_queries, cosine, -sine).reshape(1, tokens, width),
            rotate(grad_keys, cosine, -sine).reshape(1, tokens, width),
            grad_values.reshape(1, tokens, width),
            grad_up,
        ],
        axis=0,
    )
    in_bias_grad = jnp.sum(grad_proj, axis=1)
    grad_proj_low = grad_proj.astype(jnp.bfloat16)
    piece = lax.all_gather(w_in, "seq", axis=0, tiled=True)
    part = grad_proj_low
    attn_add = jnp.einsum(
        "stn,nsk->stk", part[:3], piece[:, :3], preferred_element_type=jnp.float32
    )
    mlp_add = jnp.einsum("jtn,njk->tk", part[3:], piece[:, 3:], preferred_element_type=jnp.float32)
    part = grad_proj_low
    attn_term = jnp.einsum(
        "stn,stk->nsk", part[:3], normed_attn, preferred_element_type=jnp.float32
    )
    mlp_term = jnp.einsum("jtn,tk->njk", part[3:], normed_mlp, preferred_element_type=jnp.float32)
    in_grads = lax.psum_scatter(
        jnp.concatenate([attn_term, mlp_term], axis=1).astype(jnp.bfloat16),
        "seq",
        scatter_dimension=0,
        tiled=True,
    )
    norm_gain_grad = jnp.stack(
        [jnp.sum(attn_add * scaled[:3], axis=(0, 1)), jnp.sum(mlp_add * scaled[3], axis=0)]
    )
    norm_bias_grad = jnp.stack([jnp.sum(attn_add, axis=(0, 1)), jnp.sum(mlp_add, axis=0)])
    grad_attn_streams = normalize_back(attn_add * norm_gain[0], scaled[:3], inverse[:3])
    grad_mlp_stream = normalize_back(
        mlp_add * norm_gain[1], scaled[3], inverse[3]
    ) + grad_out_low.astype(jnp.float32)
    grad_streams = jnp.concatenate([grad_attn_streams, grad_mlp_stream[None]], axis=0)
    grad_mixing = jnp.stack(
        [
            jnp.einsum(
                "std,td->ts", grad_streams, hist_local[state].astype(jnp.float32), precision=highest
            )
            for state in range(states)
        ],
        axis=-1,
    )
    hist_terms = [
        jnp.einsum("ts,std->td", mixing[:, :, state], grad_streams, precision=highest)
        for state in range(states)
    ]
    gen_bias_grad = jnp.sum(grad_mixing, axis=0)
    gen_out_grad = jnp.einsum("th,tsj->hsj", gen_hidden, grad_mixing, precision=highest)
    grad_hidden = jnp.einsum("tsj,hsj->th", grad_mixing, gen_out, precision=highest)
    grad_pre_low = gen_pull(grad_hidden)[0].astype(jnp.bfloat16)
    gen_in_grad = jnp.einsum(
        "tk,th->kh", gen_normed, grad_pre_low, preferred_element_type=jnp.float32
    )
    grad_gen = jnp.einsum("th,kh->tk", grad_pre_low, gen_in, preferred_element_type=jnp.float32)
    gen_gain_grad = jnp.sum(grad_gen * last * rms, axis=0)
    gained = grad_gen * gen_gain
    grad_last = rms * gained - last * (rms * rms * rms) * jnp.mean(
        gained * last, axis=-1, keepdims=True
    )
    hist_stack = jnp.stack(hist_terms[: states - 1] + [hist_terms[states - 1] + grad_last]).astype(
        jnp.bfloat16
    )
    departing = jnp.swapaxes(jnp.concatenate([new_local[None], hist_stack], axis=0), 1, 2)
    returned = lax.all_to_all(departing, "seq", split_axis=1, concat_axis=2, tiled=True)
    w_in_grad, out_total = (
        lax.psum(in_grads, "dp").astype(jnp.float32),
        lax.psum(out_grads, "dp").astype(jnp.float32),
    )
    w_out_grad = out_total[:, :width]
    w_down_grad = out_total[:, width:]
    joined = lax.psum(
        (
            gen_gain_grad,
            gen_in_grad,
            gen_out_grad,
            gen_bias_grad,
            norm_gain_grad,
            norm_bias_grad,
            in_bias_grad,
            out_bias_grad,
            stat_sums,
            stat_squares,
            stat_count,
        ),
        ("seq", "dp"),
    )
    small_totals = joined[:8]
    stat_totals = joined[8:]
    mix_mean = stat_totals[0] / stat_totals[2]
    mix_var = stat_totals[1] / stat_totals[2] - mix_mean * mix_mean
    return (
        returned[0],
        returned[1:],
        mix_mean,
        mix_var,
        small_totals[0],
        small_totals[1],
        small_totals[2],
        small_totals[3],
        small_totals[4],
        small_totals[5],
        w_in_grad,
        small_totals[6],
        w_out_grad,
        w_down_grad,
        small_totals[7],
    )


MESH = pl.DeviceIdType.MESH
HIDDEN_ROWS = 40
ROOT_HALF = math.sqrt(0.5)
INV_ROOT_2PI = 1.0 / math.sqrt(2.0 * math.pi)


def gelu_pair(x):
    half = 0.5 + 0.5 * lax.erf(x * ROOT_HALF)
    return x * half, half + x * (jnp.exp(-0.5 * x * x) * INV_ROOT_2PI)


def contract(a, b, dim_a, dim_b, precision=None):
    return lax.dot_general(
        a, b, (((dim_a,), (dim_b,)), ((), ())),
        precision=precision, preferred_element_type=jnp.float32,
    )


class Links:
    def __init__(self, n):
        self.n = n
        self.me = lax.axis_index("seq")
        core = self.me % 2
        xbit = (self.me // 2) % 2
        ybit = (self.me // 4) % 2
        flip = 1 - 2 * core
        x = self.me + 2 - 4 * xbit
        y = self.me + 4 - 8 * ybit
        self.core = core
        self.a = x * (1 - core) + y * core
        self.b = y * (1 - core) + x * core
        self.dg = x + y - self.me
        self.p = self.me + flip
        self.pa = self.b + flip
        self.pb = self.a + flip
        self.pdg = self.dg + flip

    def copy(self, src, dst, send, recv, to):
        return pltpu.make_async_remote_copy(
            src_ref=src, dst_ref=dst, send_sem=send, recv_sem=recv,
            device_id={"seq": to}, device_id_type=MESH,
        )


class Gather:
    def __init__(self, links, place, send, recv):
        self.links, self.place, self.send, self.recv = links, place, send, recv

    def _go(self, src, owner, slot, index, to):
        self.links.copy(
            src, self.place(owner), self.send.at[slot], self.recv.at[index], to
        ).start()

    def _got(self, owner, index):
        place = self.place(owner)
        self.links.copy(place, place, self.send.at[0], self.recv.at[index], self.links.p).wait_recv()

    def start(self, src):
        at = self.links
        self._go(src, at.me, 0, 0, at.a)
        self._go(src, at.me, 1, 1, at.b)
        self._go(src, at.me, 2, 3, at.p)

    def near(self):
        at = self.links
        self._got(at.a, 0)
        self._go(self.place(at.a), at.a, 3, 2, at.b)
        self._go(self.place(at.a), at.a, 4, 4, at.p)
        self._got(at.b, 1)
        self._go(self.place(at.b), at.b, 5, 5, at.p)

    def far(self):
        at = self.links
        self._got(at.dg, 2)
        self._go(self.place(at.dg), at.dg, 6, 6, at.p)

    def other(self):
        at = self.links
        for owner, index in ((at.p, 3), (at.pa, 4), (at.pb, 5), (at.pdg, 6)):
            self._got(owner, index)

    def drain(self):
        place = self.place(self.links.me)
        for slot in range(7):
            self.links.copy(
                place, place, self.send.at[slot], self.recv.at[0], self.links.p
            ).wait_send()


class Everyone:
    def __init__(self, links, source, target, arrived, send, recv):
        self.links, self.source, self.target, self.arrived = links, source, target, arrived
        self.send, self.recv = send, recv

    def start(self):
        at = self.links
        for k in range(1, at.n):
            to = (at.me + k) % at.n
            at.copy(
                self.source(to), self.target(k), self.send.at[k], self.recv.at[k], to
            ).start()

    def wait(self, k):
        at = self.links
        origin = (at.me + at.n - k) % at.n
        place = self.arrived(k, origin)
        at.copy(place, place, self.send.at[k], self.recv.at[k], at.p).wait_recv()
        return origin

    def drain(self):
        at = self.links
        for k in range(1, at.n):
            to = (at.me + k) % at.n
            place = self.source(to)
            at.copy(place, place, self.send.at[k], self.recv.at[k], at.p).wait_send()


def layer_kernel(
    n, zn,
    history, cotangent, lens, vals, gain, gin, gout, gbias, ng, nb, w_in, in_bias, w_out, w_down, out_bias,
    new_out, hist_out, totals,
    bias_tot, ngain_tot, nbias_tot, gain_tot, outb_tot, gin_tot, gout_tot,
    gbias_tot, mean_tot, var_tot,
    hist, new_state, big, cot, cols, w_turn, prm, colp, qkv, act, deriv, probs, gattn, gp, gcol, rope, masks, accs, gn,
    scaled, st3, pk, raw, part, part_in, stat, stat_in, stat_out,
    ybuf, abuf, from_a, from_b, zown, zin, zmid,
    gsum, gsum_in, gmix, gmix_in, pre, genmsg, gen_in_all, vec, vec_z, vec_sum, vec_all,
    late, late_z, late_sum, late_all, gproj, gproj_in,
    load_sem, ag_send, ag_recv, rs_send, rs_recv, ex_send, ex_recv, z_send, z_recv, out_sem,
):
    f32, bf16 = jnp.float32, jnp.bfloat16
    states, feats, tokens = hist.shape
    block = tokens // n
    width = n * feats
    hid = gin.shape[0]
    heads = feats // HEAD_DIM
    scale = HEAD_DIM ** (-0.5)
    m = 4 * states
    wide = 2 * block
    chunks = tokens // wide
    quarter = width // 4
    at = Links(n)
    me = at.me
    zc = lax.axis_index("dp")

    def rows(owner):
        return pl.ds(pl.multiple_of(owner * feats, feats), feats)

    def lanes(index, size=block):
        return pl.ds(pl.multiple_of(index * size, size), size)

    mine = rows(me)

    load_last = pltpu.make_async_copy(history.at[states - 1], hist.at[states - 1], load_sem.at[0])
    load_hist = pltpu.make_async_copy(
        history.at[pl.ds(0, states - 1)], hist.at[pl.ds(0, states - 1)], load_sem.at[1]
    )
    load_cot = pltpu.make_async_copy(cotangent, cot.at[mine, :], load_sem.at[2])
    for copy in (load_last, load_hist, load_cot):
        copy.start()
    barrier = pltpu.get_barrier_semaphore()
    for k in range(1, n):
        pl.semaphore_signal(
            barrier, inc=1, device_id={"seq": (me + k) % n}, device_id_type=MESH
        )
    for k in range(1, zn):
        pl.semaphore_signal(
            barrier, inc=1, device_id={"dp": (zc + k) % zn}, device_id_type=MESH
        )

    gathers = [
        Gather(at, lambda owner, s=s: big.at[s * n + owner], ag_send.at[s], ag_recv.at[s])
        for s in range(4)
    ]
    cots = Gather(at, lambda owner: cot.at[rows(owner), :], ag_send.at[4], ag_recv.at[4])
    parts = Everyone(
        at, lambda to: part.at[to], lambda k: part_in.at[k], lambda k, origin: part_in.at[k],
        ex_send.at[6], ex_recv.at[6],
    )
    spread_mix = Everyone(
        at, lambda to: pk.at[me], lambda k: pk.at[me], lambda k, origin: pk.at[origin],
        ex_send.at[7], ex_recv.at[7],
    )
    stats = Everyone(
        at, lambda to: stat, lambda k: stat_in.at[me], lambda k, origin: stat_in.at[origin],
        ex_send.at[8], ex_recv.at[8],
    )

    prm[...] = jnp.zeros_like(prm)
    prm[0:1, :] = gain[:, mine]
    prm[1:3, :] = ng[:, mine]
    prm[3:5, :] = nb[:, mine]
    prm[5:6, :] = out_bias[:, mine]
    prm[8:15, :] = in_bias[:, mine]
    colp[...] = prm[...].T
    accs[...] = jnp.zeros_like(accs)

    gin_mine = gin[:, mine]
    load_last.wait()
    for b in range(n):
        last = hist[states - 1, :, b * block : (b + 1) * block].astype(f32)
        product = (last * colp[:, 0:1]).astype(bf16)
        part[b, 0:hid, :] = jnp.dot(gin_mine, product, preferred_element_type=f32)
        part[b, hid : hid + 8, :] = jnp.broadcast_to(
            jnp.sum(last * last, axis=0, keepdims=True), (8, block)
        )
    pl.semaphore_wait(barrier, n - 1 + zn - 1)
    parts.start()
    load_cot.wait()
    cots.start(cot.at[mine, :])

    @pl.loop(0, n)
    def _(r):
        for j in range(4):
            ybuf[0, rows(r), j * feats : (j + 1) * feats] = w_in[3 + j, :, lanes(r, feats)].T

    load_hist.wait()
    total = part[me]
    for k in range(1, n):
        parts.wait(k)
        total = total + part_in[k]
    raw[...] = total
    rms = lax.rsqrt(total[hid : hid + 1] * (1.0 / width) + rms_eps)
    hidden, _ = gelu_pair(total[0:hid] * rms)
    table = jnp.concatenate([gout[j] for j in range(states)], axis=0)
    mixing = jnp.dot(table, hidden, precision=highest, preferred_element_type=f32)
    for j in range(states):
        pk[me, 4 * j : 4 * j + 4, :] = mixing[4 * j : 4 * j + 4] + gbias[:, j : j + 1]
    pk[me, m : m + 1, :] = rms
    for offset, value in ((1, lens[0, 0, 0]), (2, vals[0, 0, 0]), (3, vals[0, 0, 1])):
        pk[me, m + offset : m + offset + 1, :] = jnp.full((1, block), value.astype(f32))
    spread_mix.start()

    share = feats // zn
    shared_rows = pl.ds(pl.multiple_of(zc * share, share), share)

    def column_copy(to, j):
        if j == 0:
            src = w_out.at[shared_rows, rows(to)]
        else:
            src = w_down.at[
                shared_rows, pl.ds(pl.multiple_of((j - 1) * width + to * feats, feats), feats)
            ]
        return src, cols.at[me, zc, :, pl.ds(j * feats, feats)]

    for k in range(1, n):
        to = (me + k) % n
        for j in range(5):
            src, dst = column_copy(to, j)
            at.copy(src, dst, ex_send.at[9, k], ex_recv.at[9, k], to).start()
    own_cols = [
        pltpu.make_async_copy(*column_copy(me, j), load_sem.at[3 + j]) for j in range(5)
    ]
    for copy in own_cols:
        copy.start()
    cots.near()

    def line_columns(k, owner):
        part_cols = cols.at[:, owner]
        return pltpu.make_async_remote_copy(
            src_ref=part_cols, dst_ref=part_cols, send_sem=ex_send.at[10, k], recv_sem=ex_recv.at[10, k],
            device_id={"dp": (zc + k) % zn}, device_id_type=MESH,
        )

    def share_columns():
        for k in range(1, n):
            arrived = cols.at[(me + n - k) % n, zc]
            at.copy(arrived, arrived, ex_send.at[9, k], ex_recv.at[9, k], at.p).wait()
        for copy in own_cols:
            copy.wait()
        for k in range(1, zn):
            line_columns(k, zc).start()

    def wait_columns():
        for k in range(1, zn):
            line_columns(k, (zc + zn - k) % zn).wait()

    def mix_block(owner):
        where = lanes(owner)
        for half in range(2):
            part_rows = pl.ds(half * (feats // 2), feats // 2)
            sums = [None] * 4
            for j in range(states):
                value = hist[j, part_rows, where].astype(f32)
                for s in range(4):
                    weight = pk[owner, pl.ds(4 * j + s, 1), :]
                    term = weight * value
                    sums[s] = term if sums[s] is None else sums[s] + term
            for s in range(4):
                scaled[s, part_rows, where] = sums[s]
        for s in range(4):
            value = scaled[s, :, where]
            mean = jnp.sum(value, axis=0, keepdims=True) * (1.0 / feats)
            off = value - mean
            stat[pl.ds(s, 1), where] = mean
            stat[pl.ds(4 + s, 1), where] = jnp.sum(off * off, axis=0, keepdims=True)

    mix_block(me)

    @pl.loop(1, n // 2)
    def _(k):
        mix_block(spread_mix.wait(k))

    share_columns()

    @pl.loop(n // 2, n)
    def _(k):
        mix_block(spread_mix.wait(k))

    stats.start()

    spot = lax.broadcasted_iota(jnp.int32, (1, block), 1).astype(f32)
    freq = jnp.exp(
        lax.broadcasted_iota(jnp.int32, (8, block), 0).astype(f32)
        * (-2.0 * math.log(10000.0) / ROT)
    )

    def place(owner, index):
        cut = pk[owner, m + 1 : m + 2, :]
        second = index >= cut
        position = index - jnp.where(second, cut, 0.0)
        limit = jnp.where(second, pk[owner, m + 3 : m + 4, :], pk[owner, m + 2 : m + 3, :])
        return second, position, position < limit

    for b in range(n):
        where = pl.ds(b * block, block)
        _, position, valid = place(b, spot)
        angle = freq * position
        rope[0:8, where] = jnp.cos(angle)
        rope[8:16, where] = jnp.sin(angle)
        masks[0:1, where] = jnp.where(valid, 1.0, 0.0)

    cots.far()

    @pl.loop(0, n)
    def _(r):
        for s in range(3):
            w_turn[rows(r), s * feats : (s + 1) * feats] = w_in[s, :, lanes(r, feats)].T

    for k in range(1, n):
        stats.wait(k)
    stat_in[me] = stat[...]
    means = stat_in[0, 0:4, :]
    for k in range(1, n):
        means = means + stat_in[k, 0:4, :]
    means = means * (1.0 / n)
    spread = jnp.zeros_like(means)
    for k in range(n):
        away = stat_in[k, 0:4, :] - means
        spread = spread + (stat_in[k, 4:8, :] + feats * (away * away))
    stat_out[0:4, :] = means
    stat_out[4:8, :] = lax.rsqrt(spread * (1.0 / width) + ln_eps)

    def normalise(s):
        which = 0 if s < 3 else 1

        @pl.loop(0, n)
        def _(b):
            where = lanes(b)
            value = scaled[s, :, where]
            if s == 3:
                st3[:, where] = value
            xhat = (value - stat_out[s : s + 1, where]) * stat_out[4 + s : 5 + s, where]
            scaled[s, :, where] = xhat
            big[s * n + me, :, where] = (
                xhat * colp[:, 1 + which : 2 + which] + colp[:, 3 + which : 4 + which]
            ).astype(bf16)

        gathers[s].start(big.at[s * n + me])

    def rotated(value, where, sign):
        cosine, sine = rope[0:8, where], rope[8:16, where] * sign
        out = []
        for h in range(heads):
            base = h * HEAD_DIM
            former, latter = value[base : base + 8], value[base + 8 : base + 16]
            out += [
                former * cosine - latter * sine,
                latter * cosine + former * sine,
                value[base + 16 : base + HEAD_DIM],
            ]
        return jnp.concatenate(out, axis=0)

    def stream(s, where):
        return big[pl.ds(s * n, n), :, where].reshape(width, -1)

    def project(s):
        @pl.loop(0, chunks)
        def _(c):
            where = lanes(c, wide)
            value = jnp.dot(w_in[s], stream(s, where), preferred_element_type=f32)
            value = value + colp[:, 8 + s : 9 + s]
            if s < 2:
                value = rotated(value, where, 1.0)
            if s == 0:
                value = value * scale
            qkv[s, :, where] = value.astype(bf16)

    def project_up(pair):
        @pl.loop(0, chunks)
        def _(c):
            where = lanes(c, wide)
            weight = w_in[3 + 2 * pair : 5 + 2 * pair].reshape(2 * feats, width)
            both = jnp.dot(weight, stream(3, where), preferred_element_type=f32)
            for i in range(2):
                j = 2 * pair + i
                up, slope = gelu_pair(
                    both[i * feats : (i + 1) * feats] + colp[:, 11 + j : 12 + j]
                )
                act[pl.ds((1 + j) * feats, feats), where] = up.astype(bf16)
                deriv[j, :, where] = slope

    def rs_copy(i, src, dst, slot, to):
        return at.copy(src, dst, rs_send.at[i, slot], rs_recv.at[i, slot], to)

    def rs_first(i):
        return [
            rs_copy(i, ybuf.at[i, rows(owner), :], abuf.at[i, q], q, at.p)
            for q, owner in enumerate((at.p, at.pa, at.pb, at.pdg))
        ]

    def rs_second(i):
        return [
            rs_copy(i, ybuf.at[i, rows(at.a), :], from_a.at[i, 0], 4, at.a),
            rs_copy(i, ybuf.at[i, rows(at.dg), :], from_a.at[i, 1], 5, at.a),
        ]

    def rs_third(i):
        return [rs_copy(i, ybuf.at[i, rows(at.b), :], from_b.at[i], 6, at.b)]

    def rs_start(i):
        for copy in rs_first(i):
            copy.start()

    def rs_fold(i):
        for copy in rs_first(i):
            copy.wait_recv()

        @pl.loop(0, chunks)
        def _(c):
            where = lanes(c, wide)
            for q, owner in ((1, at.a), (3, at.dg)):
                ybuf[i, rows(owner), where] = (
                    ybuf[i, rows(owner), where].astype(f32) + abuf[i, q, :, where].astype(f32)
                ).astype(bf16)

        for copy in rs_second(i):
            copy.start()

    def rs_pass(i):
        for copy in rs_second(i):
            copy.wait_recv()

        @pl.loop(0, chunks)
        def _(c):
            where = lanes(c, wide)
            ybuf[i, rows(at.b), where] = (
                ybuf[i, rows(at.b), where].astype(f32)
                + abuf[i, 2, :, where].astype(f32)
                + from_a[i, 1, :, where].astype(f32)
            ).astype(bf16)

        for copy in rs_third(i):
            copy.start()

    def rs_end(i):
        for copy in rs_third(i):
            copy.wait_recv()

    def rs_value(i, where):
        return (
            ybuf[i, rows(me), where].astype(f32)
            + abuf[i, 0, :, where].astype(f32)
            + from_a[i, 0, :, where].astype(f32)
            + from_b[i, :, where].astype(f32)
        )

    def rs_drain(i):
        for copy in rs_first(i) + rs_second(i) + rs_third(i):
            copy.wait_send()

    outer = (zc == 0) | (zc == 3)
    z_in = 1 + zc // 3
    z_out = 3 * (zc - 1)
    z_over = 3 - zc

    def z_copy(c, src, dst, slot, recv_slot, to):
        return pltpu.make_async_remote_copy(
            src_ref=src, dst_ref=dst, send_sem=z_send.at[c, slot], recv_sem=z_recv.at[c, recv_slot],
            device_id={"dp": to}, device_id_type=MESH,
        )

    def z_up(c):
        return z_copy(c, zown.at[c], zin.at[c], 0, 0, z_in)

    def z_cross(c):
        return z_copy(c, zown.at[c], zmid.at[c], 1, 1, z_over)

    def z_down(c):
        return z_copy(c, zin.at[c], zin.at[c], 2, 0, z_out)

    def z_start(c):
        if zn > 1:

            @pl.when(outer)
            def _():
                z_up(c).start()

    def z_fold(c):
        if zn > 1:

            @pl.when(jnp.logical_not(outer))
            def _():
                z_up(c).wait_recv()

                @pl.loop(0, chunks)
                def _(k):
                    where = lanes(k, wide)
                    zown[c, :, where] = (
                        zown[c, :, where].astype(f32) + zin[c, :, where].astype(f32)
                    ).astype(bf16)

                z_cross(c).start()

    stages = []

    def z_end(c):
        if zn > 1:

            @pl.when(jnp.logical_not(outer))
            def _():
                z_cross(c).wait_recv()

                @pl.loop(0, chunks)
                def _(k):
                    where = lanes(k, wide)
                    zin[c, :, where] = (
                        zown[c, :, where].astype(f32) + zmid[c, :, where].astype(f32)
                    ).astype(bf16)

                z_down(c).start()

            @pl.when(outer)
            def _():
                z_up(c).wait_recv()

        source = zin if zn > 1 else zown
        stages.append(pltpu.make_async_copy(source.at[c], totals.at[c], out_sem.at[c]))
        stages[-1].start()

    def z_drain(c):
        if zn > 1:

            @pl.when(outer)
            def _():
                z_up(c).wait_send()

            @pl.when(jnp.logical_not(outer))
            def _():
                z_cross(c).wait_send()
                z_down(c).wait_send()

    z_order = (3, 4, 5, 6, 11, 10, 0, 1, 2, 9, 8, 7)
    z_actions = []
    for t in range(14):
        if t < 12:
            z_actions.append((z_fold, z_order[t]))
        if t >= 2:
            z_actions.append((z_end, z_order[t - 2]))
    z_actions = iter(z_actions)

    def z_step(count):
        for _ in range(count):
            step, c = next(z_actions)
            step(c)


    def turn_columns(which):
        @pl.loop(0, n)
        def _(r):
            for j in which:
                zown[j, :, lanes(r, feats)] = (
                    cols[r, :, :, j * feats : (j + 1) * feats].reshape(feats, feats).T
                )

    def back_up(pair):
        @pl.loop(0, chunks)
        def _(c):
            where = lanes(c, wide)
            weight = zown[1 + 2 * pair : 3 + 2 * pair].reshape(2 * feats, width)
            both = jnp.dot(weight, cot[:, where], preferred_element_type=f32)
            for i in range(2):
                j = 2 * pair + i
                value = both[i * feats : (i + 1) * feats] * deriv[j, :, where]
                accs[3 + j] = accs[3 + j] + (value[:, :block] + value[:, block:])
                gp[pl.ds((3 + j) * feats, feats), where] = value.astype(bf16)

    def out_grads(first, count):
        for r in range(4):
            grads = contract(
                cot[r * quarter : (r + 1) * quarter, :],
                act[first * feats : (first + count) * feats, :], 1, 1,
            ).astype(bf16)
            for j in range(count):
                gcol[first + j, r * quarter : (r + 1) * quarter, :] = (
                    grads[:, j * feats : (j + 1) * feats]
                )

    turns = [
        Everyone(
            at,
            lambda to, j=j: gcol.at[j, rows(to), :],
            lambda k, j=j: zown.at[7 + j, :, mine],
            lambda k, origin, j=j: zown.at[7 + j, :, rows(origin)],
            ex_send.at[(0, 11, 12, 13, 14)[j]], ex_recv.at[(0, 11, 12, 13, 14)[j]],
        )
        for j in range(5)
    ]
    keeps = [
        pltpu.make_async_copy(gcol.at[j, mine, :], zown.at[7 + j, :, mine], load_sem.at[12 + j])
        for j in range(5)
    ]

    def turn_start(j):
        turns[j].start()
        keeps[j].start()

    def turn_end(j):
        for k in range(1, n):
            turns[j].wait(k)
        keeps[j].wait()
        z_start(7 + j)

    def normed_grad(i, source, first, count):
        @pl.loop(0, chunks)
        def _(c):
            where = lanes(c, wide)
            for r in range(2):
                half = slice(r * width // 2, (r + 1) * width // 2)
                ybuf[i, half, where] = jnp.dot(
                    source[half, :], gp[first * feats : (first + count) * feats, where],
                    preferred_element_type=f32,
                ).astype(bf16)

        rs_start(i)

    def weight_grad(first, count, source):
        @pl.loop(0, 4)
        def _(r):
            part_in_rows = big[pl.ds(source * n + r * (n // 4), n // 4), :, :].reshape(quarter, tokens)
            value = contract(gp[first * feats : (first + count) * feats, :], part_in_rows, 1, 1)
            for s in range(count):
                zown[first + s, :, lanes(r, quarter)] = value[s * feats : (s + 1) * feats].astype(bf16)

        for s in range(first, first + count):
            z_start(s)

    def along_history():
        @pl.loop(0, n)
        def _(b):
            where = lanes(b)
            for j in range(states):
                past = hist[j, :, where].astype(f32)
                gproj[b, m + j : m + j + 1, :] = jnp.sum(past, axis=0, keepdims=True)
                for s in range(4):
                    gproj[b, 4 * j + s : 4 * j + s + 1, :] = jnp.sum(
                        scaled[s, :, where] * past, axis=0, keepdims=True
                    )

    projs = Everyone(
        at, lambda to: gproj.at[to], lambda k: gproj_in.at[k], lambda k, origin: gproj_in.at[k],
        ex_send.at[15], ex_recv.at[15],
    )

    def norm_sums(s):
        which = 0 if s < 3 else 1

        @pl.loop(0, n)
        def _(b):
            where = lanes(b)
            value = rs_value(s, where)
            along = value * scaled[s, :, where]
            accs[7 + which] = accs[7 + which] + along
            accs[9 + which] = accs[9 + which] + value
            factor = colp[:, 1 + which : 2 + which]
            value = value * factor
            gn[s, :, where] = value
            gsum[s : s + 1, where] = jnp.sum(value, axis=0, keepdims=True)
            gsum[4 + s : 5 + s, where] = jnp.sum(along * factor, axis=0, keepdims=True)
            if s == 3:
                direct = cot[mine, where].astype(f32)
                accs[12] = accs[12] + direct
                value = value + direct * (1.0 / stat_out[4 + s : 5 + s, where])
            for j in range(states):
                gmix[b, 4 * j + s : 4 * j + s + 1, :] = jnp.sum(
                    value * hist[j, :, where].astype(f32), axis=0, keepdims=True
                )

    normalise(3)
    normalise(0)
    cots.other()
    cots.drain()

    @pl.loop(0, n)
    def _(b):
        where = lanes(b)
        cot[:, where] = cot[:, where] * masks[0:1, where].astype(bf16)

    gathers[3].near()
    normalise(1)
    gathers[0].near()
    normalise(2)
    along_history()
    projs.start()
    gathers[3].far()
    wait_columns()
    turn_columns(range(5))

    @pl.loop(0, chunks)
    def _(c):
        where = lanes(c, wide)
        gattn[:, where] = jnp.dot(zown[0], cot[:, where], preferred_element_type=f32).astype(bf16)

    gathers[3].other()
    project_up(0)
    gathers[0].far()
    project_up(1)
    gathers[1].near()
    back_up(0)
    back_up(1)
    gathers[2].near()
    normed_grad(3, ybuf.at[0, :, 0 : 4 * feats], 3, 4)
    weight_grad(3, 4, 3)
    gathers[1].far()
    rs_fold(3)
    out_grads(1, 4)
    for j in (4, 3, 2, 1):
        turn_start(j)
    gathers[0].other()
    project(0)
    gathers[1].other()
    project(1)
    z_step(1)
    gathers[2].far()
    gathers[2].other()
    project(2)
    rs_pass(3)

    key_at = lax.broadcasted_iota(jnp.int32, (block, block), 0).astype(f32)
    query_at = lax.broadcasted_iota(jnp.int32, (block, block), 1).astype(f32)

    @pl.loop(0, n // 2)
    def _(pair):
        chains = []
        for u in range(2):
            b = 2 * pair + u
            where = lanes(b)
            cut = pk[b, m + 1 : m + 2, :]
            _, _, valid = place(b, key_at)
            same = jnp.where(key_at >= cut, 1.0, 0.0) == jnp.where(query_at >= cut, 1.0, 0.0)
            allowed = same & (key_at <= query_at) & valid
            for h in range(heads):
                rows_h = pl.ds(h * HEAD_DIM, HEAD_DIM)
                scores = contract(qkv[1, rows_h, where], qkv[0, rows_h, where], 0, 0)
                chains.append((b, h, rows_h, where, allowed, scores))
        softs = []
        for b, h, rows_h, where, allowed, scores in chains:
            scores = jnp.where(allowed, scores, masked_score)
            weights = jnp.exp(scores - jnp.max(scores, axis=0, keepdims=True))
            softs.append(weights * (1.0 / jnp.sum(weights, axis=0, keepdims=True)))
        for (b, h, rows_h, where, _, _), soft in zip(chains, softs):
            probs[b * heads + h] = soft
            act[rows_h, where] = jnp.dot(
                qkv[2, rows_h, where], soft.astype(bf16), preferred_element_type=f32
            ).astype(bf16)


    @pl.loop(0, chunks)
    def _(c):
        where = lanes(c, wide)
        for r in range(2):
            half = slice(r * width // 2, (r + 1) * width // 2)
            ybuf[4, half, where] = jnp.dot(
                cols[r * n // 2 : (r + 1) * n // 2].reshape(width // 2, 5 * feats), act[:, where],
                preferred_element_type=f32,
            ).astype(bf16)

    rs_start(4)
    z_step(1)
    out_grads(0, 1)
    rs_fold(4)
    turn_start(0)

    @pl.loop(0, n // 2)
    def _(pair):
        first = []
        for u in range(2):
            b = 2 * pair + u
            where = lanes(b)
            for h in range(heads):
                rows_h = pl.ds(h * HEAD_DIM, HEAD_DIM)
                soft = probs[b * heads + h]
                grad = gattn[rows_h, where]
                dprob = contract(qkv[2, rows_h, where], grad, 0, 0)
                values_grad = contract(grad, soft.astype(bf16), 1, 1)
                first.append((rows_h, where, soft, dprob, values_grad))
        lows = []
        for rows_h, where, soft, dprob, values_grad in first:
            inner = jnp.sum(soft * dprob, axis=0, keepdims=True)
            lows.append((soft * (dprob - inner)).astype(bf16))
        for u in range(2):
            where = first[u * heads][1]
            grads = [[], [], []]
            for h in range(heads):
                rows_h, _, _, _, values_grad = first[u * heads + h]
                low = lows[u * heads + h]
                grads[0].append(
                    jnp.dot(qkv[1, rows_h, where], low, preferred_element_type=f32) * scale
                )
                grads[1].append(contract(qkv[0, rows_h, where], low, 1, 1))
                grads[2].append(values_grad)
            for s in range(3):
                value = jnp.concatenate(grads[s], axis=0)
                if s < 2:
                    value = rotated(value, where, -1.0)
                accs[s] = accs[s] + value
                gp[pl.ds(s * feats, feats), where] = value.astype(bf16)

    turn_end(4)
    z_step(2)
    normed_grad(0, w_turn.at[:, 0:feats], 0, 1)
    normed_grad(1, w_turn.at[:, feats : 2 * feats], 1, 1)
    rs_fold(0)
    normed_grad(2, w_turn.at[:, 2 * feats : 3 * feats], 2, 1)
    rs_pass(4)
    rs_fold(1)
    turn_end(3)
    for s in range(3):
        weight_grad(s, 1, s)
    rs_fold(2)
    z_step(2)
    turn_end(2)
    rs_end(3)
    norm_sums(3)
    z_step(2)
    rs_pass(0)
    turn_end(1)
    rs_end(4)

    @pl.loop(0, n)
    def _(b):
        where = lanes(b)
        new_state[:, where] = (st3[:, where] + rs_value(4, where) + colp[:, 5:6]).astype(bf16)

    keep_new = pltpu.make_async_copy(new_state, new_out, load_sem.at[9])
    keep_new.start()
    z_step(2)
    rs_pass(1)
    turn_end(0)
    rs_end(0)
    norm_sums(0)
    z_step(2)
    rs_pass(2)
    rs_end(1)
    norm_sums(1)
    z_step(2)
    rs_end(2)
    norm_sums(2)
    sums = Everyone(
        at, lambda to: gsum, lambda k: gsum_in.at[me], lambda k, origin: gsum_in.at[origin],
        ex_send.at[1], ex_recv.at[1],
    )
    mixes = Everyone(
        at, lambda to: gmix.at[to], lambda k: gmix_in.at[k], lambda k, origin: gmix_in.at[k],
        ex_send.at[2], ex_recv.at[2],
    )
    sums.start()
    mixes.start()
    z_step(2)
    for k in range(1, n):
        sums.wait(k)
    gsum_in[me] = gsum[...]
    total = gsum_in[0]
    for k in range(1, n):
        total = total + gsum_in[k]
    pre[0:8, :] = total * (1.0 / width)

    def stream_block(b):
        where = lanes(b)
        for s in range(4):
            value = stat_out[4 + s : 5 + s, where] * (
                gn[s, :, where] - pre[s : s + 1, where] - scaled[s, :, where] * pre[4 + s : 5 + s, where]
            )
            if s == 3:
                value = value + cot[mine, where].astype(f32)
            gn[s, :, where] = value
        for j in range(states - 1):
            value = pk[b, pl.ds(4 * j, 1), :] * gn[0, :, where]
            for s in range(1, 4):
                value = value + pk[b, pl.ds(4 * j + s, 1), :] * gn[s, :, where]
            hist[j, :, where] = value.astype(bf16)

    pl.loop(0, n // 2)(stream_block)

    total = gmix[me]
    for k in range(1, n):
        mixes.wait(k)
        total = total + gmix_in[k]
    fixed = gproj[me]
    for k in range(1, n):
        projs.wait(k)
        fixed = fixed + gproj_in[k]
    own = lanes(me)

    def each_state(value):
        return jnp.concatenate([value] * states, axis=0)

    history_sum = jnp.concatenate(
        [jnp.broadcast_to(fixed[m + j : m + j + 1], (4, block)) for j in range(states)], axis=0
    )
    grad_mix = each_state(stat_out[4:8, own]) * (
        total[0:m] - each_state(pre[0:4, own]) * history_sum - each_state(pre[4:8, own]) * fixed[0:m]
    )
    table = jnp.concatenate([gout[j] for j in range(states)], axis=0)
    hidden, slope = gelu_pair(raw[0:hid, :] * pk[me, m : m + 1, :])
    grad_hidden = contract(table, grad_mix, 0, 0, precision=highest)
    low = (grad_hidden * slope).astype(bf16).astype(f32)
    genmsg[0:hid, :] = low
    genmsg[hid : hid + 8, :] = jnp.broadcast_to(
        jnp.sum(low * raw[0:hid, :], axis=0, keepdims=True) * (1.0 / width), (8, block)
    )
    owns = Everyone(
        at, lambda to: genmsg, lambda k: gen_in_all.at[me], lambda k, origin: gen_in_all.at[origin],
        ex_send.at[3], ex_recv.at[3],
    )
    owns.start()
    z_step(2)
    _, _, valid = place(me, spot)
    kept = jnp.where(valid, 1.0, 0.0)
    ones = jnp.ones((8, block), f32)
    mixing = pk[me, 0:m, :]
    vec[...] = jnp.zeros_like(vec)
    vec[16 : 16 + hid, 0:m] = contract(hidden, grad_mix, 1, 1, precision=highest)
    for index, value in enumerate((grad_mix, mixing * kept, mixing * mixing * kept)):
        vec[56 + index : 57 + index, 0:m] = contract(ones, value, 1, 1, precision=highest)[0:1]
    vec[59:60, :] = jnp.broadcast_to(jnp.sum(kept, axis=1, keepdims=True), (1, block))
    prm[...] = jnp.zeros_like(prm)
    for index in range(13):
        prm[:, index : index + 1] = jnp.sum(accs[index], axis=1, keepdims=True)
    vec[0:16, :] = prm[...].T[0:16]

    def line(ref, landing, row, k, owner):
        return pltpu.make_async_remote_copy(
            src_ref=ref, dst_ref=landing.at[owner], send_sem=ex_send.at[row, k], recv_sem=ex_recv.at[row, k],
            device_id={"dp": (zc + k) % zn}, device_id_type=MESH,
        )

    def line_start(ref, landing, row):
        for k in range(1, zn):
            line(ref, landing, row, k, zc).start()

    def line_total(ref, landing, row):
        landing[zc] = ref[...]
        for k in range(1, zn):
            line(ref, landing, row, k, (zc + zn - k) % zn).wait()
        value = landing[0]
        for k in range(1, zn):
            value = value + landing[k]
        return value

    line_start(vec, vec_z, 4)
    pl.loop(n // 2, n)(stream_block)
    keep_hist = pltpu.make_async_copy(
        hist.at[pl.ds(0, states - 1)], hist_out.at[pl.ds(0, states - 1)], load_sem.at[10]
    )
    keep_hist.start()
    alls = Everyone(
        at, lambda to: vec_sum, lambda k: vec_all.at[me], lambda k, origin: vec_all.at[origin],
        ex_send.at[5], ex_recv.at[5],
    )
    total = line_total(vec, vec_z, 4)
    vec_sum[...] = total
    vec_all[me] = total
    alls.start()
    gen_in_all[me] = genmsg[...]
    for k in range(1, n):
        owns.wait(k)
    gin_mine = gin[:, rows(me)]
    late[...] = jnp.zeros_like(late)

    @pl.loop(0, n)
    def _(b):
        where = lanes(b)
        low_b = gen_in_all[b, 0:hid, :].astype(bf16)
        rms = pk[b, m : m + 1, :]
        last = hist[states - 1, :, where].astype(f32)
        grad_gen = contract(gin_mine, low_b, 0, 0)
        accs[11] = accs[11] + grad_gen * last * rms
        normed = (last * rms * colp[:, 0:1]).astype(bf16)
        late[0:hid, :] = late[0:hid, :] + contract(low_b, normed, 1, 1)
        value = rms * grad_gen * colp[:, 0:1]
        value = value - last * (rms * rms * rms * gen_in_all[b, hid : hid + 1, :])
        for s in range(4):
            value = value + pk[b, pl.ds(4 * (states - 1) + s, 1), :] * gn[s, :, where]
        hist[states - 1, :, where] = value.astype(bf16)

    keep_last = pltpu.make_async_copy(hist.at[states - 1], hist_out.at[states - 1], load_sem.at[11])
    keep_last.start()

    prm[:, 0:1] = jnp.sum(accs[11], axis=1, keepdims=True)
    late[hid : hid + 8, :] = prm[...].T[0:8]
    line_start(late, late_z, 16)
    z_step(2)
    lates = Everyone(
        at, lambda to: late_sum, lambda k: late_all.at[me], lambda k, origin: late_all.at[origin],
        ex_send.at[17], ex_recv.at[17],
    )
    total = line_total(late, late_z, 16)
    late_sum[...] = total
    late_all[me] = total
    lates.start()
    for k in range(1, n):
        alls.wait(k)
    shared = vec_all[0, 16:64, :]
    for k in range(1, n):
        shared = shared + vec_all[k, 16:64, :]
    prm[...] = jnp.zeros_like(prm)
    prm[0:40, :] = shared[0:40]
    count = shared[43:44, 0:1]
    mean = shared[41:42] / count
    prm[40:41, :] = shared[40:41]
    prm[41:42, :] = mean
    prm[42:43, :] = shared[42:43] / count - mean * mean
    turned = prm[...].T
    for j in range(states):
        gout_tot[j] = turned[4 * j : 4 * j + 4, 0:hid]
        gbias_tot[:, j : j + 1] = turned[4 * j : 4 * j + 4, 40:41]
        mean_tot[:, j : j + 1] = turned[4 * j : 4 * j + 4, 41:42]
        var_tot[:, j : j + 1] = turned[4 * j : 4 * j + 4, 42:43]
    z_step(1)
    for k in range(1, n):
        lates.wait(k)
    for k in range(n):
        where = pl.ds(k * feats, feats)
        bias_tot[:, where] = vec_all[k, 0:7, :]
        ngain_tot[:, where] = vec_all[k, 7:9, :]
        nbias_tot[:, where] = vec_all[k, 9:11, :]
        outb_tot[:, where] = vec_all[k, 12:13, :]
        gain_tot[:, where] = late_all[k, hid : hid + 1, :]
        gin_tot[:, where] = late_all[k, 0:hid, :]
    for step, c in z_actions:
        step(c)
    for c in range(12):
        z_drain(c)
    for i in range(5):
        rs_drain(i)
    for g in gathers:
        g.drain()
    for exchange in [parts, spread_mix, stats, projs, sums, mixes, owns, alls, lates] + turns:
        exchange.drain()
    for copy in stages + [keep_new, keep_hist, keep_last]:
        copy.wait()


def layer(n, zn, history, cotangent, bucket_len, valid_len, gen_gain, gen_in, gen_out, gen_bias, norm_gain, norm_bias, w_in, in_bias, w_out, w_down, out_bias):
    f32, bf16 = jnp.float32, jnp.bfloat16
    states, feats, tokens = history.shape
    block = tokens // n
    width = n * feats
    hid = gen_in.shape[1]
    heads = feats // HEAD_DIM
    vmem = pl.BlockSpec(memory_space=pltpu.VMEM)
    smem = pl.BlockSpec(memory_space=pltpu.SMEM)
    anys = pl.BlockSpec(memory_space=pl.ANY)
    shape = jax.ShapeDtypeStruct
    dma = pltpu.SemaphoreType.DMA
    return pl.pallas_call(
        functools.partial(layer_kernel, n, zn),
        out_shape=(
            shape((feats, tokens), bf16),
            shape((states, feats, tokens), bf16),
            shape((12, feats, width), bf16),
            shape((7, width), f32),
            shape((2, width), f32),
            shape((2, width), f32),
            shape((1, width), f32),
            shape((1, width), f32),
            shape((hid, width), f32),
            shape((states, 4, hid), f32),
            shape((4, states), f32),
            shape((4, states), f32),
            shape((4, states), f32),
        ),
        in_specs=[anys] * 2 + [smem] * 2 + [vmem] * 8 + [anys] * 2 + [vmem],
        out_specs=(anys,) * 3 + (vmem,) * 10,
        scratch_shapes=[
            pltpu.VMEM((states, feats, tokens), bf16),
            pltpu.VMEM((feats, tokens), bf16),
            pltpu.VMEM((4 * n, feats, tokens), bf16),
            pltpu.VMEM((width, tokens), bf16),
            pltpu.VMEM((n, zn, feats // zn, 5 * feats), bf16),
            pltpu.VMEM((width, 3 * feats), bf16),
            pltpu.VMEM((feats, feats), f32),
            pltpu.VMEM((feats, feats), f32),
            pltpu.VMEM((3, feats, tokens), bf16),
            pltpu.VMEM((5 * feats, tokens), bf16),
            pltpu.VMEM((4, feats, tokens), f32),
            pltpu.VMEM((n * heads, block, block), f32),
            pltpu.VMEM((feats, tokens), bf16),
            pltpu.VMEM((7 * feats, tokens), bf16),
            pltpu.VMEM((5, width, feats), bf16),
            pltpu.VMEM((16, tokens), f32),
            pltpu.VMEM((8, tokens), f32),
            pltpu.VMEM((13, feats, block), f32),
            pltpu.VMEM((4, feats, tokens), f32),
            pltpu.VMEM((4, feats, tokens), f32),
            pltpu.VMEM((feats, tokens), f32),
            pltpu.VMEM((n, 40, block), f32),
            pltpu.VMEM((hid + 8, block), f32),
            pltpu.VMEM((n, hid + 8, block), f32),
            pltpu.VMEM((n, hid + 8, block), f32),
            pltpu.VMEM((8, tokens), f32),
            pltpu.VMEM((n, 8, tokens), f32),
            pltpu.VMEM((8, tokens), f32),
            pltpu.VMEM((5, width, tokens), bf16),
            pltpu.VMEM((5, 4, feats, tokens), bf16),
            pltpu.VMEM((5, 2, feats, tokens), bf16),
            pltpu.VMEM((5, feats, tokens), bf16),
            pltpu.VMEM((12, feats, width), bf16),
            pltpu.VMEM((12, feats, width), bf16),
            pltpu.VMEM((12, feats, width), bf16),
            pltpu.VMEM((8, tokens), f32),
            pltpu.VMEM((n, 8, tokens), f32),
            pltpu.VMEM((n, 40, block), f32),
            pltpu.VMEM((n, 40, block), f32),
            pltpu.VMEM((8, tokens), f32),
            pltpu.VMEM((hid + 8, block), f32),
            pltpu.VMEM((n, hid + 8, block), f32),
            pltpu.VMEM((64, feats), f32),
            pltpu.VMEM((zn, 64, feats), f32),
            pltpu.VMEM((64, feats), f32),
            pltpu.VMEM((n, 64, feats), f32),
            pltpu.VMEM((hid + 8, feats), f32),
            pltpu.VMEM((zn, hid + 8, feats), f32),
            pltpu.VMEM((hid + 8, feats), f32),
            pltpu.VMEM((n, hid + 8, feats), f32),
            pltpu.VMEM((n, 48, block), f32),
            pltpu.VMEM((n, 48, block), f32),
            dma((17,)), dma((5, 7)), dma((5, 7)), dma((5, 7)), dma((5, 7)), dma((18, n)), dma((18, n)),
            dma((12, 3)), dma((12, 2)), dma((12,)),
        ],
        compiler_params=pltpu.CompilerParams(
            collective_id=1, has_side_effects=True, vmem_limit_bytes=67043328
        ),
        name="layer",
    )(
        history, cotangent, bucket_len, valid_len, gen_gain.reshape(1, width), gen_in.T,
        gen_out.transpose(2, 1, 0), gen_bias, norm_gain, norm_bias, w_in.transpose(1, 0, 2), in_bias,
        w_out, w_down, out_bias.reshape(1, width),
    )


def finish_kernel(new_in, hist_in, totals, *refs):
    count = (len(refs) - 10) // 2
    small_in = refs[:count]
    new_out, hist_out, in_out, out_out, down_out = refs[count : count + 5]
    small_out = refs[count + 5 : 2 * count + 5]
    new_buf, hist_buf, low, full, sem_in = refs[2 * count + 5 :]
    width = totals.shape[2]
    states = hist_in.shape[0]
    sources = [(new_in, new_buf)] + [(hist_in.at[j], hist_buf.at[j]) for j in range(states)]
    sources += [(totals.at[c], low.at[c]) for c in range(12)]
    targets = [(new_buf, new_out)] + [(hist_buf.at[j], hist_out.at[j]) for j in range(states)]
    for c in range(12):
        if c < 7:
            targets.append((full.at[c], in_out.at[c]))
        elif c == 7:
            targets.append((full.at[c], out_out))
        else:
            targets.append((full.at[c], down_out.at[:, (c - 8) * width : (c - 7) * width]))
    loads = [pltpu.make_async_copy(a, b, sem_in.at[0, i]) for i, (a, b) in enumerate(sources)]
    stores = [pltpu.make_async_copy(a, b, sem_in.at[1, i]) for i, (a, b) in enumerate(targets)]
    order = list(range(1 + states, 13 + states)) + list(range(1 + states))
    for i in order:
        loads[i].start()
    for a, b in zip(small_in, small_out):
        b[...] = a[...]
    for i in order:
        loads[i].wait()
        if i > states:
            c = i - 1 - states
            full[c] = low[c].astype(jnp.float32)
        stores[i].start()
    for copy in stores:
        copy.wait()


def finish(new_state, history_grad, totals, smalls):
    f32, bf16 = jnp.float32, jnp.bfloat16
    feats, width = totals.shape[1:]
    vmem = pl.BlockSpec(memory_space=pltpu.VMEM)
    anys = pl.BlockSpec(memory_space=pl.ANY)
    shape = jax.ShapeDtypeStruct
    return pl.pallas_call(
        finish_kernel,
        out_shape=(
            shape(new_state.shape, bf16),
            shape(history_grad.shape, bf16),
            shape((7, feats, width), f32),
            shape((feats, width), f32),
            shape((feats, 4 * width), f32),
        ) + tuple(shape(x.shape, x.dtype) for x in smalls),
        in_specs=[anys] * 3 + [vmem] * len(smalls),
        out_specs=(anys,) * 5 + (vmem,) * len(smalls),
        scratch_shapes=[
            pltpu.VMEM(new_state.shape, bf16),
            pltpu.VMEM(history_grad.shape, bf16),
            pltpu.VMEM(totals.shape, bf16),
            pltpu.VMEM(totals.shape, f32),
            pltpu.SemaphoreType.DMA((2, 13 + history_grad.shape[0])),
        ],
        compiler_params=pltpu.CompilerParams(vmem_limit_bytes=67043328),
        name="finish",
    )(new_state, history_grad, totals, *smalls)


def tp_device(
    history, cotangent, bucket_len, valid_len, gen_gain, gen_in, gen_out, gen_bias,
    norm_gain, norm_bias, w_in, in_bias, w_out, w_down, out_bias,
):
    n, zn = lax.axis_size("seq"), lax.axis_size("dp")
    new_state, history_grad, totals, *smalls = layer(
        n, zn, history, cotangent, bucket_len, valid_len, gen_gain, gen_in, gen_out, gen_bias,
        norm_gain, norm_bias, w_in, in_bias, w_out, w_down, out_bias,
    )
    (
        new_state, history_grad, in_grad, out_grad, down_grad,
        bias, ngain, nbias, gain, outb, gin, gout, gbias, mean, var,
    ) = finish(new_state, history_grad, totals, smalls)
    width = gen_gain.shape[0]
    return (
        new_state, history_grad, mean, var, gain.reshape(width), gin.T, gout.transpose(2, 1, 0),
        gbias, ngain, nbias, in_grad.transpose(1, 0, 2), bias, out_grad, down_grad, outb.reshape(width),
    )


def solution(mesh):
    in_specs = (
        P(None, "seq", "dp"),
        P("seq", "dp"),
        P("dp", "seq", None),
        P("dp", "seq", None),
        P(),
        P(),
        P(),
        P(),
        P(),
        P(),
        P("seq", None, None),
        P(),
        P("seq", None),
        P("seq", None),
        P(),
    )
    out_specs = (
        P("seq", "dp"),
        P(None, "seq", "dp"),
        P(),
        P(),
        P(),
        P(),
        P(),
        P(),
        P(),
        P(),
        P("seq", None, None),
        P(),
        P("seq", None),
        P("seq", None),
        P(),
    )
    by_feature = mesh.shape["seq"] == 8 and mesh.shape["dp"] in (1, 4)
    body = tp_device if by_feature else per_device
    return jax.shard_map(
        body, mesh=mesh, in_specs=in_specs, out_specs=out_specs, check_vma=False
    )
```

```python
import functools
import math

import jax
import jax.numpy as jnp
from jax import lax
from jax.experimental import pallas as pl
from jax.experimental.pallas import tpu as pltpu
from jax.sharding import PartitionSpec as P

HEADS = 16
HEAD_DIM = 64
ROT = 16


ln_eps = 1e-05
rms_eps = 1e-06
masked_score = -1e30
highest = lax.Precision.HIGHEST


def gelu_exact(values):
    return jax.nn.gelu(values, approximate=False)


def rotary_tables(position):
    freq_index = jnp.arange(ROT // 2, dtype=jnp.float32)
    inverse_freq = jnp.exp(freq_index * (-2.0 * math.log(10000.0) / ROT))
    angles = position.astype(jnp.float32)[:, None] * inverse_freq[None, :]
    return (jnp.cos(angles), jnp.sin(angles))


def rotate(values, cosine, sine):
    half = ROT // 2
    former = values[..., :half]
    latter = values[..., half:ROT]
    cos_heads = cosine[:, None, :]
    sin_heads = sine[:, None, :]
    return jnp.concatenate(
        [
            former * cos_heads - latter * sin_heads,
            latter * cos_heads + former * sin_heads,
            values[..., ROT:],
        ],
        axis=-1,
    )


def token_layout(lengths, counts, tokens):
    index = jnp.arange(tokens, dtype=jnp.int32)
    second = index >= lengths[0]
    position = index - jnp.where(second, lengths[0], 0)
    valid = position < jnp.where(second, counts[1], counts[0])
    return (second, position, valid)


def normalize(streams):
    centre = jnp.mean(streams, axis=-1, keepdims=True)
    centred = streams - centre
    inverse = lax.rsqrt(jnp.mean(centred * centred, axis=-1, keepdims=True) + ln_eps)
    return (centred * inverse, inverse)


def normalize_back(grad_scaled, scaled, inverse):
    mean_grad = jnp.mean(grad_scaled, axis=-1, keepdims=True)
    mean_along = jnp.mean(grad_scaled * scaled, axis=-1, keepdims=True)
    return inverse * (grad_scaled - mean_grad - scaled * mean_along)


def per_device(
    history,
    cotangent,
    bucket_len,
    valid_len,
    gen_gain,
    gen_in,
    gen_out,
    gen_bias,
    norm_gain,
    norm_bias,
    w_in,
    in_bias,
    w_out,
    w_down,
    out_bias,
):
    states = history.shape[0]
    stacked = jnp.concatenate([history, cotangent[None]], axis=0)
    arrived = lax.all_to_all(stacked, "seq", split_axis=2, concat_axis=1, tiled=True)
    arrived_rows = jnp.swapaxes(arrived, 1, 2)
    hist_local = arrived_rows[:states]
    cot_local = arrived_rows[states]
    tokens = hist_local.shape[1]
    width = hist_local.shape[2]
    second, position, valid = token_layout(bucket_len.reshape(2), valid_len.reshape(2), tokens)
    valid_float = valid.astype(jnp.float32)
    last = hist_local[states - 1].astype(jnp.float32)
    rms = lax.rsqrt(jnp.mean(last * last, axis=-1, keepdims=True) + rms_eps)
    gen_normed = (last * rms * gen_gain).astype(jnp.bfloat16)
    gen_pre = jnp.dot(gen_normed, gen_in, preferred_element_type=jnp.float32)
    gen_hidden, gen_pull = jax.vjp(gelu_exact, gen_pre)
    mixing = jnp.einsum("th,hsj->tsj", gen_hidden, gen_out, precision=highest) + gen_bias
    weighted = mixing * valid_float[:, None, None]
    stat_sums = jnp.sum(weighted, axis=0)
    stat_squares = jnp.sum(weighted * mixing, axis=0)
    stat_count = jnp.sum(valid_float)
    streams = mixing[:, :, 0].T[:, :, None] * hist_local[0]
    for state in range(1, states):
        streams = streams + mixing[:, :, state].T[:, :, None] * hist_local[state]
    scaled, inverse = normalize(streams)
    normed_attn = (scaled[:3] * norm_gain[0] + norm_bias[0]).astype(jnp.bfloat16)
    normed_mlp = (scaled[3] * norm_gain[1] + norm_bias[1]).astype(jnp.bfloat16)
    piece = lax.all_gather(w_in, "seq", axis=0, tiled=True)
    attn_part = jnp.einsum(
        "stk,nsk->stn", normed_attn, piece[:, :3], preferred_element_type=jnp.float32
    )
    mlp_part = jnp.einsum(
        "tk,njk->jtn", normed_mlp, piece[:, 3:], preferred_element_type=jnp.float32
    )
    projected = jnp.concatenate([attn_part, mlp_part], axis=0) + in_bias[:, None, :]
    cosine, sine = rotary_tables(position)
    heads_shape = (tokens, HEADS, HEAD_DIM)
    queries = (rotate(projected[0].reshape(heads_shape), cosine, sine) * HEAD_DIM ** (-0.5)).astype(
        jnp.bfloat16
    )
    keys = rotate(projected[1].reshape(heads_shape), cosine, sine).astype(jnp.bfloat16)
    values = projected[2].reshape(heads_shape).astype(jnp.bfloat16)
    index = jnp.arange(tokens, dtype=jnp.int32)
    allowed = (
        (second[:, None] == second[None, :]) & (index[None, :] <= index[:, None]) & valid[None, :]
    )
    scores = jnp.einsum("qhd,khd->hqk", queries, keys, preferred_element_type=jnp.float32)
    scores = jnp.where(allowed[None], scores, masked_score)
    top = jnp.max(scores, axis=-1, keepdims=True)
    weights = jnp.exp(scores - top)
    weight_total = jnp.sum(weights, axis=-1, keepdims=True)
    log_total = top + jnp.log(weight_total)
    probs_low = (weights / weight_total).astype(jnp.bfloat16)
    attended = jnp.einsum("hqk,khd->qhd", probs_low, values, preferred_element_type=jnp.float32)
    attn_low = attended.reshape(tokens, width).astype(jnp.bfloat16)
    gelu_up, up_pull = jax.vjp(gelu_exact, projected[3:])
    gelu_low = gelu_up.astype(jnp.bfloat16)
    grad_out_low = jnp.where(valid[:, None], cot_local, jnp.zeros_like(cot_local))
    piece_out, piece_down = lax.all_gather((w_out, w_down), "seq", axis=0, tiled=True)
    down_part = piece_down.reshape(piece_down.shape[0], 4, width)
    result = jnp.einsum("tk,nk->tn", attn_low, piece_out, preferred_element_type=jnp.float32)
    branch = result + jnp.einsum(
        "jtk,njk->tn", gelu_low, down_part, preferred_element_type=jnp.float32
    )
    new_local = (streams[3] + branch + out_bias).astype(jnp.bfloat16)
    piece_out = lax.all_gather(w_out, "seq", axis=0, tiled=True)
    piece_down = lax.all_gather(w_down, "seq", axis=0, tiled=True)
    count = piece_out.shape[0]
    part = grad_out_low
    attn_add = jnp.einsum("tn,nk->tk", part, piece_out, preferred_element_type=jnp.float32)
    gelu_add = jnp.einsum(
        "tn,njk->jtk", part, piece_down.reshape(count, 4, width), preferred_element_type=jnp.float32
    )
    grad_attn = attn_add
    part = grad_out_low
    term_out = jnp.einsum("tn,tk->nk", part, attn_low, preferred_element_type=jnp.float32)
    term_down = jnp.einsum(
        "tn,jtk->njk", part, gelu_low, preferred_element_type=jnp.float32
    ).reshape(lax.axis_size("seq") * w_out.shape[0], 4 * width)
    out_grads = lax.psum_scatter(
        jnp.concatenate([term_out, term_down], axis=1).astype(jnp.bfloat16),
        "seq",
        scatter_dimension=0,
        tiled=True,
    )
    out_bias_grad = jnp.sum(grad_out_low.astype(jnp.float32), axis=0)
    grad_attended = grad_attn.astype(jnp.bfloat16).reshape(heads_shape)
    rescored = jnp.einsum("qhd,khd->hqk", queries, keys, preferred_element_type=jnp.float32)
    probs = jnp.where(allowed[None], jnp.exp(rescored - log_total), 0.0)
    grad_values = jnp.einsum(
        "hqk,qhd->khd",
        probs.astype(jnp.bfloat16),
        grad_attended,
        preferred_element_type=jnp.float32,
    )
    grad_probs = jnp.einsum(
        "qhd,khd->hqk", grad_attended, values, preferred_element_type=jnp.float32
    )
    grad_scores = (
        probs * (grad_probs - jnp.sum(probs * grad_probs, axis=-1, keepdims=True))
    ).astype(jnp.bfloat16)
    grad_queries = jnp.einsum(
        "hqk,khd->qhd", grad_scores, keys, preferred_element_type=jnp.float32
    ) * HEAD_DIM ** (-0.5)
    grad_keys = jnp.einsum("hqk,qhd->khd", grad_scores, queries, preferred_element_type=jnp.float32)
    grad_up = up_pull(gelu_add)[0]
    grad_proj = jnp.concatenate(
        [
            rotate(grad_queries, cosine, -sine).reshape(1, tokens, width),
            rotate(grad_keys, cosine, -sine).reshape(1, tokens, width),
            grad_values.reshape(1, tokens, width),
            grad_up,
        ],
        axis=0,
    )
    in_bias_grad = jnp.sum(grad_proj, axis=1)
    grad_proj_low = grad_proj.astype(jnp.bfloat16)
    piece = lax.all_gather(w_in, "seq", axis=0, tiled=True)
    part = grad_proj_low
    attn_add = jnp.einsum(
        "stn,nsk->stk", part[:3], piece[:, :3], preferred_element_type=jnp.float32
    )
    mlp_add = jnp.einsum("jtn,njk->tk", part[3:], piece[:, 3:], preferred_element_type=jnp.float32)
    part = grad_proj_low
    attn_term = jnp.einsum(
        "stn,stk->nsk", part[:3], normed_attn, preferred_element_type=jnp.float32
    )
    mlp_term = jnp.einsum("jtn,tk->njk", part[3:], normed_mlp, preferred_element_type=jnp.float32)
    in_grads = lax.psum_scatter(
        jnp.concatenate([attn_term, mlp_term], axis=1).astype(jnp.bfloat16),
        "seq",
        scatter_dimension=0,
        tiled=True,
    )
    norm_gain_grad = jnp.stack(
        [jnp.sum(attn_add * scaled[:3], axis=(0, 1)), jnp.sum(mlp_add * scaled[3], axis=0)]
    )
    norm_bias_grad = jnp.stack([jnp.sum(attn_add, axis=(0, 1)), jnp.sum(mlp_add, axis=0)])
    grad_attn_streams = normalize_back(attn_add * norm_gain[0], scaled[:3], inverse[:3])
    grad_mlp_stream = normalize_back(
        mlp_add * norm_gain[1], scaled[3], inverse[3]
    ) + grad_out_low.astype(jnp.float32)
    grad_streams = jnp.concatenate([grad_attn_streams, grad_mlp_stream[None]], axis=0)
    grad_mixing = jnp.stack(
        [
            jnp.einsum(
                "std,td->ts", grad_streams, hist_local[state].astype(jnp.float32), precision=highest
            )
            for state in range(states)
        ],
        axis=-1,
    )
    hist_terms = [
        jnp.einsum("ts,std->td", mixing[:, :, state], grad_streams, precision=highest)
        for state in range(states)
    ]
    gen_bias_grad = jnp.sum(grad_mixing, axis=0)
    gen_out_grad = jnp.einsum("th,tsj->hsj", gen_hidden, grad_mixing, precision=highest)
    grad_hidden = jnp.einsum("tsj,hsj->th", grad_mixing, gen_out, precision=highest)
    grad_pre_low = gen_pull(grad_hidden)[0].astype(jnp.bfloat16)
    gen_in_grad = jnp.einsum(
        "tk,th->kh", gen_normed, grad_pre_low, preferred_element_type=jnp.float32
    )
    grad_gen = jnp.einsum("th,kh->tk", grad_pre_low, gen_in, preferred_element_type=jnp.float32)
    gen_gain_grad = jnp.sum(grad_gen * last * rms, axis=0)
    gained = grad_gen * gen_gain
    grad_last = rms * gained - last * (rms * rms * rms) * jnp.mean(
        gained * last, axis=-1, keepdims=True
    )
    hist_stack = jnp.stack(hist_terms[: states - 1] + [hist_terms[states - 1] + grad_last]).astype(
        jnp.bfloat16
    )
    departing = jnp.swapaxes(jnp.concatenate([new_local[None], hist_stack], axis=0), 1, 2)
    returned = lax.all_to_all(departing, "seq", split_axis=1, concat_axis=2, tiled=True)
    w_in_grad, out_total = (
        lax.psum(in_grads, "dp").astype(jnp.float32),
        lax.psum(out_grads, "dp").astype(jnp.float32),
    )
    w_out_grad = out_total[:, :width]
    w_down_grad = out_total[:, width:]
    joined = lax.psum(
        (
            gen_gain_grad,
            gen_in_grad,
            gen_out_grad,
            gen_bias_grad,
            norm_gain_grad,
            norm_bias_grad,
            in_bias_grad,
            out_bias_grad,
            stat_sums,
            stat_squares,
            stat_count,
        ),
        ("seq", "dp"),
    )
    small_totals = joined[:8]
    stat_totals = joined[8:]
    mix_mean = stat_totals[0] / stat_totals[2]
    mix_var = stat_totals[1] / stat_totals[2] - mix_mean * mix_mean
    return (
        returned[0],
        returned[1:],
        mix_mean,
        mix_var,
        small_totals[0],
        small_totals[1],
        small_totals[2],
        small_totals[3],
        small_totals[4],
        small_totals[5],
        w_in_grad,
        small_totals[6],
        w_out_grad,
        w_down_grad,
        small_totals[7],
    )


MESH = pl.DeviceIdType.MESH
HIDDEN_ROWS = 40
ROOT_HALF = math.sqrt(0.5)
INV_ROOT_2PI = 1.0 / math.sqrt(2.0 * math.pi)


def gelu_pair(x):
    half = 0.5 + 0.5 * lax.erf(x * ROOT_HALF)
    return x * half, half + x * (jnp.exp(-0.5 * x * x) * INV_ROOT_2PI)


def contract(a, b, dim_a, dim_b, precision=None):
    return lax.dot_general(
        a, b, (((dim_a,), (dim_b,)), ((), ())),
        precision=precision, preferred_element_type=jnp.float32,
    )


class Links:
    def __init__(self, n):
        self.n = n
        self.me = lax.axis_index("seq")
        core = self.me % 2
        xbit = (self.me // 2) % 2
        ybit = (self.me // 4) % 2
        flip = 1 - 2 * core
        x = self.me + 2 - 4 * xbit
        y = self.me + 4 - 8 * ybit
        self.core = core
        self.a = x * (1 - core) + y * core
        self.b = y * (1 - core) + x * core
        self.dg = x + y - self.me
        self.p = self.me + flip
        self.pa = self.b + flip
        self.pb = self.a + flip
        self.pdg = self.dg + flip

    def copy(self, src, dst, send, recv, to):
        return pltpu.make_async_remote_copy(
            src_ref=src, dst_ref=dst, send_sem=send, recv_sem=recv,
            device_id={"seq": to}, device_id_type=MESH,
        )


class Gather:
    def __init__(self, links, place, send, recv):
        self.links, self.place, self.send, self.recv = links, place, send, recv

    def _go(self, src, owner, slot, index, to):
        self.links.copy(
            src, self.place(owner), self.send.at[slot], self.recv.at[index], to
        ).start()

    def _got(self, owner, index):
        place = self.place(owner)
        self.links.copy(place, place, self.send.at[0], self.recv.at[index], self.links.p).wait_recv()

    def start(self, src):
        at = self.links
        self._go(src, at.me, 0, 0, at.a)
        self._go(src, at.me, 1, 1, at.b)
        self._go(src, at.me, 2, 3, at.p)

    def near(self):
        at = self.links
        self._got(at.a, 0)
        self._go(self.place(at.a), at.a, 3, 2, at.b)
        self._go(self.place(at.a), at.a, 4, 4, at.p)
        self._got(at.b, 1)
        self._go(self.place(at.b), at.b, 5, 5, at.p)

    def far(self):
        at = self.links
        self._got(at.dg, 2)
        self._go(self.place(at.dg), at.dg, 6, 6, at.p)

    def other(self):
        at = self.links
        for owner, index in ((at.p, 3), (at.pa, 4), (at.pb, 5), (at.pdg, 6)):
            self._got(owner, index)

    def drain(self):
        place = self.place(self.links.me)
        for slot in range(7):
            self.links.copy(
                place, place, self.send.at[slot], self.recv.at[0], self.links.p
            ).wait_send()


class Everyone:
    def __init__(self, links, source, target, arrived, send, recv):
        self.links, self.source, self.target, self.arrived = links, source, target, arrived
        self.send, self.recv = send, recv

    def start(self):
        at = self.links
        for k in range(1, at.n):
            to = (at.me + k) % at.n
            at.copy(
                self.source(to), self.target(k), self.send.at[k], self.recv.at[k], to
            ).start()

    def wait(self, k):
        at = self.links
        origin = (at.me + at.n - k) % at.n
        place = self.arrived(k, origin)
        at.copy(place, place, self.send.at[k], self.recv.at[k], at.p).wait_recv()
        return origin

    def drain(self):
        at = self.links
        for k in range(1, at.n):
            to = (at.me + k) % at.n
            place = self.source(to)
            at.copy(place, place, self.send.at[k], self.recv.at[k], at.p).wait_send()


def layer_kernel(
    n, zn,
    history, cotangent, lens, vals, gain, gin, gout, gbias, ng, nb, w_in, in_bias, w_out, w_down, out_bias,
    new_out, hist_out, totals,
    bias_tot, ngain_tot, nbias_tot, gain_tot, outb_tot, gin_tot, gout_tot,
    gbias_tot, mean_tot, var_tot,
    hist, new_state, big, cot, cols, w_turn, prm, colp, qkv, act, deriv, probs, gattn, gp, gcol, rope, masks, accs, gn,
    scaled, st3, pk, raw, part, part_in, stat, stat_in, stat_out,
    ybuf, abuf, from_a, from_b, zown, zin, zmid,
    gsum, gsum_in, gmix, gmix_in, pre, genmsg, gen_in_all, vec, vec_z, vec_sum, vec_all,
    late, late_z, late_sum, late_all, gproj, gproj_in,
    load_sem, ag_send, ag_recv, rs_send, rs_recv, ex_send, ex_recv, z_send, z_recv, out_sem,
):
    f32, bf16 = jnp.float32, jnp.bfloat16
    states, feats, tokens = hist.shape
    block = tokens // n
    width = n * feats
    hid = gin.shape[0]
    heads = feats // HEAD_DIM
    scale = HEAD_DIM ** (-0.5)
    m = 4 * states
    wide = 2 * block
    chunks = tokens // wide
    quarter = width // 4
    at = Links(n)
    me = at.me
    zc = lax.axis_index("dp")

    def rows(owner):
        return pl.ds(pl.multiple_of(owner * feats, feats), feats)

    def lanes(index, size=block):
        return pl.ds(pl.multiple_of(index * size, size), size)

    mine = rows(me)

    load_last = pltpu.make_async_copy(history.at[states - 1], hist.at[states - 1], load_sem.at[0])
    load_hist = pltpu.make_async_copy(
        history.at[pl.ds(0, states - 1)], hist.at[pl.ds(0, states - 1)], load_sem.at[1]
    )
    load_cot = pltpu.make_async_copy(cotangent, cot.at[mine, :], load_sem.at[2])
    for copy in (load_last, load_hist, load_cot):
        copy.start()
    barrier = pltpu.get_barrier_semaphore()
    for k in range(1, n):
        pl.semaphore_signal(
            barrier, inc=1, device_id={"seq": (me + k) % n}, device_id_type=MESH
        )
    for k in range(1, zn):
        pl.semaphore_signal(
            barrier, inc=1, device_id={"dp": (zc + k) % zn}, device_id_type=MESH
        )

    gathers = [
        Gather(at, lambda owner, s=s: big.at[s * n + owner], ag_send.at[s], ag_recv.at[s])
        for s in range(4)
    ]
    cots = Gather(at, lambda owner: cot.at[rows(owner), :], ag_send.at[4], ag_recv.at[4])
    parts = Everyone(
        at, lambda to: part.at[to], lambda k: part_in.at[k], lambda k, origin: part_in.at[k],
        ex_send.at[6], ex_recv.at[6],
    )
    spread_mix = Everyone(
        at, lambda to: pk.at[me], lambda k: pk.at[me], lambda k, origin: pk.at[origin],
        ex_send.at[7], ex_recv.at[7],
    )
    stats = Everyone(
        at, lambda to: stat, lambda k: stat_in.at[me], lambda k, origin: stat_in.at[origin],
        ex_send.at[8], ex_recv.at[8],
    )

    prm[...] = jnp.zeros_like(prm)
    prm[0:1, :] = gain[:, mine]
    prm[1:3, :] = ng[:, mine]
    prm[3:5, :] = nb[:, mine]
    prm[5:6, :] = out_bias[:, mine]
    prm[8:15, :] = in_bias[:, mine]
    colp[...] = prm[...].T
    accs[...] = jnp.zeros_like(accs)

    gin_mine = gin[:, mine]
    load_last.wait()
    for b in range(n):
        last = hist[states - 1, :, b * block : (b + 1) * block].astype(f32)
        product = (last * colp[:, 0:1]).astype(bf16)
        part[b, 0:hid, :] = jnp.dot(gin_mine, product, preferred_element_type=f32)
        part[b, hid : hid + 8, :] = jnp.broadcast_to(
            jnp.sum(last * last, axis=0, keepdims=True), (8, block)
        )
    pl.semaphore_wait(barrier, n - 1 + zn - 1)
    parts.start()
    load_cot.wait()
    cots.start(cot.at[mine, :])

    @pl.loop(0, n)
    def _(r):
        for j in range(4):
            ybuf[0, rows(r), j * feats : (j + 1) * feats] = w_in[3 + j, :, lanes(r, feats)].T

    load_hist.wait()
    total = part[me]
    for k in range(1, n):
        parts.wait(k)
        total = total + part_in[k]
    raw[...] = total
    rms = lax.rsqrt(total[hid : hid + 1] * (1.0 / width) + rms_eps)
    hidden, _ = gelu_pair(total[0:hid] * rms)
    table = jnp.concatenate([gout[j] for j in range(states)], axis=0)
    mixing = jnp.dot(table, hidden, precision=highest, preferred_element_type=f32)
    for j in range(states):
        pk[me, 4 * j : 4 * j + 4, :] = mixing[4 * j : 4 * j + 4] + gbias[:, j : j + 1]
    pk[me, m : m + 1, :] = rms
    for offset, value in ((1, lens[0, 0, 0]), (2, vals[0, 0, 0]), (3, vals[0, 0, 1])):
        pk[me, m + offset : m + offset + 1, :] = jnp.full((1, block), value.astype(f32))
    spread_mix.start()

    share = feats // zn
    shared_rows = pl.ds(pl.multiple_of(zc * share, share), share)

    def column_copy(to, j):
        if j == 0:
            src = w_out.at[shared_rows, rows(to)]
        else:
            src = w_down.at[
                shared_rows, pl.ds(pl.multiple_of((j - 1) * width + to * feats, feats), feats)
            ]
        return src, cols.at[me, zc, :, pl.ds(j * feats, feats)]

    for k in range(1, n):
        to = (me + k) % n
        for j in range(5):
            src, dst = column_copy(to, j)
            at.copy(src, dst, ex_send.at[9, k], ex_recv.at[9, k], to).start()
    own_cols = [
        pltpu.make_async_copy(*column_copy(me, j), load_sem.at[3 + j]) for j in range(5)
    ]
    for copy in own_cols:
        copy.start()
    cots.near()

    def line_columns(k, owner):
        part_cols = cols.at[:, owner]
        return pltpu.make_async_remote_copy(
            src_ref=part_cols, dst_ref=part_cols, send_sem=ex_send.at[10, k], recv_sem=ex_recv.at[10, k],
            device_id={"dp": (zc + k) % zn}, device_id_type=MESH,
        )

    def share_columns():
        for k in range(1, n):
            arrived = cols.at[(me + n - k) % n, zc]
            at.copy(arrived, arrived, ex_send.at[9, k], ex_recv.at[9, k], at.p).wait()
        for copy in own_cols:
            copy.wait()
        for k in range(1, zn):
            line_columns(k, zc).start()

    def wait_columns():
        for k in range(1, zn):
            line_columns(k, (zc + zn - k) % zn).wait()

    def mix_block(owner):
        where = lanes(owner)
        for half in range(2):
            part_rows = pl.ds(half * (feats // 2), feats // 2)
            sums = [None] * 4
            for j in range(states):
                value = hist[j, part_rows, where].astype(f32)
                for s in range(4):
                    weight = pk[owner, pl.ds(4 * j + s, 1), :]
                    term = weight * value
                    sums[s] = term if sums[s] is None else sums[s] + term
            for s in range(4):
                scaled[s, part_rows, where] = sums[s]
        for s in range(4):
            value = scaled[s, :, where]
            mean = jnp.sum(value, axis=0, keepdims=True) * (1.0 / feats)
            off = value - mean
            stat[pl.ds(s, 1), where] = mean
            stat[pl.ds(4 + s, 1), where] = jnp.sum(off * off, axis=0, keepdims=True)

    mix_block(me)

    @pl.loop(1, n // 2)
    def _(k):
        mix_block(spread_mix.wait(k))

    share_columns()

    @pl.loop(n // 2, n)
    def _(k):
        mix_block(spread_mix.wait(k))

    stats.start()

    spot = lax.broadcasted_iota(jnp.int32, (1, block), 1).astype(f32)
    freq = jnp.exp(
        lax.broadcasted_iota(jnp.int32, (8, block), 0).astype(f32)
        * (-2.0 * math.log(10000.0) / ROT)
    )

    def place(owner, index):
        cut = pk[owner, m + 1 : m + 2, :]
        second = index >= cut
        position = index - jnp.where(second, cut, 0.0)
        limit = jnp.where(second, pk[owner, m + 3 : m + 4, :], pk[owner, m + 2 : m + 3, :])
        return second, position, position < limit

    for b in range(n):
        where = pl.ds(b * block, block)
        _, position, valid = place(b, spot)
        angle = freq * position
        rope[0:8, where] = jnp.cos(angle)
        rope[8:16, where] = jnp.sin(angle)
        masks[0:1, where] = jnp.where(valid, 1.0, 0.0)

    cots.far()

    @pl.loop(0, n)
    def _(r):
        for s in range(3):
            w_turn[rows(r), s * feats : (s + 1) * feats] = w_in[s, :, lanes(r, feats)].T

    for k in range(1, n):
        stats.wait(k)
    stat_in[me] = stat[...]
    means = stat_in[0, 0:4, :]
    for k in range(1, n):
        means = means + stat_in[k, 0:4, :]
    means = means * (1.0 / n)
    spread = jnp.zeros_like(means)
    for k in range(n):
        away = stat_in[k, 0:4, :] - means
        spread = spread + (stat_in[k, 4:8, :] + feats * (away * away))
    stat_out[0:4, :] = means
    stat_out[4:8, :] = lax.rsqrt(spread * (1.0 / width) + ln_eps)

    def normalise(s):
        which = 0 if s < 3 else 1

        @pl.loop(0, n)
        def _(b):
            where = lanes(b)
            value = scaled[s, :, where]
            if s == 3:
                st3[:, where] = value
            xhat = (value - stat_out[s : s + 1, where]) * stat_out[4 + s : 5 + s, where]
            scaled[s, :, where] = xhat
            big[s * n + me, :, where] = (
                xhat * colp[:, 1 + which : 2 + which] + colp[:, 3 + which : 4 + which]
            ).astype(bf16)

        gathers[s].start(big.at[s * n + me])

    def rotated(value, where, sign):
        cosine, sine = rope[0:8, where], rope[8:16, where] * sign
        out = []
        for h in range(heads):
            base = h * HEAD_DIM
            former, latter = value[base : base + 8], value[base + 8 : base + 16]
            out += [
                former * cosine - latter * sine,
                latter * cosine + former * sine,
                value[base + 16 : base + HEAD_DIM],
            ]
        return jnp.concatenate(out, axis=0)

    def stream(s, where):
        return big[pl.ds(s * n, n), :, where].reshape(width, -1)

    def project(s):
        @pl.loop(0, chunks)
        def _(c):
            where = lanes(c, wide)
            value = jnp.dot(w_in[s], stream(s, where), preferred_element_type=f32)
            value = value + colp[:, 8 + s : 9 + s]
            if s < 2:
                value = rotated(value, where, 1.0)
            if s == 0:
                value = value * scale
            qkv[s, :, where] = value.astype(bf16)

    def project_up(pair):
        @pl.loop(0, chunks)
        def _(c):
            where = lanes(c, wide)
            weight = w_in[3 + 2 * pair : 5 + 2 * pair].reshape(2 * feats, width)
            both = jnp.dot(weight, stream(3, where), preferred_element_type=f32)
            for i in range(2):
                j = 2 * pair + i
                up, slope = gelu_pair(
                    both[i * feats : (i + 1) * feats] + colp[:, 11 + j : 12 + j]
                )
                act[pl.ds((1 + j) * feats, feats), where] = up.astype(bf16)
                deriv[j, :, where] = slope

    def rs_copy(i, src, dst, slot, to):
        return at.copy(src, dst, rs_send.at[i, slot], rs_recv.at[i, slot], to)

    def rs_first(i):
        return [
            rs_copy(i, ybuf.at[i, rows(owner), :], abuf.at[i, q], q, at.p)
            for q, owner in enumerate((at.p, at.pa, at.pb, at.pdg))
        ]

    def rs_second(i):
        return [
            rs_copy(i, ybuf.at[i, rows(at.a), :], from_a.at[i, 0], 4, at.a),
            rs_copy(i, ybuf.at[i, rows(at.dg), :], from_a.at[i, 1], 5, at.a),
        ]

    def rs_third(i):
        return [rs_copy(i, ybuf.at[i, rows(at.b), :], from_b.at[i], 6, at.b)]

    def rs_start(i):
        for copy in rs_first(i):
            copy.start()

    def rs_fold(i):
        for copy in rs_first(i):
            copy.wait_recv()

        @pl.loop(0, chunks)
        def _(c):
            where = lanes(c, wide)
            for q, owner in ((1, at.a), (3, at.dg)):
                ybuf[i, rows(owner), where] = (
                    ybuf[i, rows(owner), where].astype(f32) + abuf[i, q, :, where].astype(f32)
                ).astype(bf16)

        for copy in rs_second(i):
            copy.start()

    def rs_pass(i):
        for copy in rs_second(i):
            copy.wait_recv()

        @pl.loop(0, chunks)
        def _(c):
            where = lanes(c, wide)
            ybuf[i, rows(at.b), where] = (
                ybuf[i, rows(at.b), where].astype(f32)
                + abuf[i, 2, :, where].astype(f32)
                + from_a[i, 1, :, where].astype(f32)
            ).astype(bf16)

        for copy in rs_third(i):
            copy.start()

    def rs_end(i):
        for copy in rs_third(i):
            copy.wait_recv()

    def rs_value(i, where):
        return (
            ybuf[i, rows(me), where].astype(f32)
            + abuf[i, 0, :, where].astype(f32)
            + from_a[i, 0, :, where].astype(f32)
            + from_b[i, :, where].astype(f32)
        )

    def rs_drain(i):
        for copy in rs_first(i) + rs_second(i) + rs_third(i):
            copy.wait_send()

    outer = (zc == 0) | (zc == 3)
    z_in = 1 + zc // 3
    z_out = 3 * (zc - 1)
    z_over = 3 - zc

    def z_copy(c, src, dst, slot, recv_slot, to):
        return pltpu.make_async_remote_copy(
            src_ref=src, dst_ref=dst, send_sem=z_send.at[c, slot], recv_sem=z_recv.at[c, recv_slot],
            device_id={"dp": to}, device_id_type=MESH,
        )

    def z_up(c):
        return z_copy(c, zown.at[c], zin.at[c], 0, 0, z_in)

    def z_cross(c):
        return z_copy(c, zown.at[c], zmid.at[c], 1, 1, z_over)

    def z_down(c):
        return z_copy(c, zin.at[c], zin.at[c], 2, 0, z_out)

    def z_start(c):
        if zn > 1:

            @pl.when(outer)
            def _():
                z_up(c).start()

    def z_fold(c):
        if zn > 1:

            @pl.when(jnp.logical_not(outer))
            def _():
                z_up(c).wait_recv()

                @pl.loop(0, chunks)
                def _(k):
                    where = lanes(k, wide)
                    zown[c, :, where] = (
                        zown[c, :, where].astype(f32) + zin[c, :, where].astype(f32)
                    ).astype(bf16)

                z_cross(c).start()

    stages = []

    def z_end(c):
        if zn > 1:

            @pl.when(jnp.logical_not(outer))
            def _():
                z_cross(c).wait_recv()

                @pl.loop(0, chunks)
                def _(k):
                    where = lanes(k, wide)
                    zin[c, :, where] = (
                        zown[c, :, where].astype(f32) + zmid[c, :, where].astype(f32)
                    ).astype(bf16)

                z_down(c).start()

            @pl.when(outer)
            def _():
                z_up(c).wait_recv()

        source = zin if zn > 1 else zown
        stages.append(pltpu.make_async_copy(source.at[c], totals.at[c], out_sem.at[c]))
        stages[-1].start()

    def z_drain(c):
        if zn > 1:

            @pl.when(outer)
            def _():
                z_up(c).wait_send()

            @pl.when(jnp.logical_not(outer))
            def _():
                z_cross(c).wait_send()
                z_down(c).wait_send()

    z_order = (3, 4, 5, 6, 11, 10, 0, 1, 2, 9, 8, 7)
    z_actions = []
    for t in range(14):
        if t < 12:
            z_actions.append((z_fold, z_order[t]))
        if t >= 2:
            z_actions.append((z_end, z_order[t - 2]))
    z_actions = iter(z_actions)

    def z_step(count):
        for _ in range(count):
            step, c = next(z_actions)
            step(c)


    def turn_columns(which):
        @pl.loop(0, n)
        def _(r):
            for j in which:
                zown[j, :, lanes(r, feats)] = (
                    cols[r, :, :, j * feats : (j + 1) * feats].reshape(feats, feats).T
                )

    def back_up(pair):
        @pl.loop(0, chunks)
        def _(c):
            where = lanes(c, wide)
            weight = zown[1 + 2 * pair : 3 + 2 * pair].reshape(2 * feats, width)
            both = jnp.dot(weight, cot[:, where], preferred_element_type=f32)
            for i in range(2):
                j = 2 * pair + i
                value = both[i * feats : (i + 1) * feats] * deriv[j, :, where]
                accs[3 + j] = accs[3 + j] + (value[:, :block] + value[:, block:])
                gp[pl.ds((3 + j) * feats, feats), where] = value.astype(bf16)

    def out_grads(first, count):
        for r in range(4):
            grads = contract(
                cot[r * quarter : (r + 1) * quarter, :],
                act[first * feats : (first + count) * feats, :], 1, 1,
            ).astype(bf16)
            for j in range(count):
                gcol[first + j, r * quarter : (r + 1) * quarter, :] = (
                    grads[:, j * feats : (j + 1) * feats]
                )

    turns = [
        Everyone(
            at,
            lambda to, j=j: gcol.at[j, rows(to), :],
            lambda k, j=j: zown.at[7 + j, :, mine],
            lambda k, origin, j=j: zown.at[7 + j, :, rows(origin)],
            ex_send.at[(0, 11, 12, 13, 14)[j]], ex_recv.at[(0, 11, 12, 13, 14)[j]],
        )
        for j in range(5)
    ]
    keeps = [
        pltpu.make_async_copy(gcol.at[j, mine, :], zown.at[7 + j, :, mine], load_sem.at[12 + j])
        for j in range(5)
    ]

    def turn_start(j):
        turns[j].start()
        keeps[j].start()

    def turn_end(j):
        for k in range(1, n):
            turns[j].wait(k)
        keeps[j].wait()
        z_start(7 + j)

    def normed_grad(i, source, first, count):
        @pl.loop(0, chunks)
        def _(c):
            where = lanes(c, wide)
            for r in range(2):
                half = slice(r * width // 2, (r + 1) * width // 2)
                ybuf[i, half, where] = jnp.dot(
                    source[half, :], gp[first * feats : (first + count) * feats, where],
                    preferred_element_type=f32,
                ).astype(bf16)

        rs_start(i)

    def weight_grad(first, count, source):
        @pl.loop(0, 4)
        def _(r):
            part_in_rows = big[pl.ds(source * n + r * (n // 4), n // 4), :, :].reshape(quarter, tokens)
            value = contract(gp[first * feats : (first + count) * feats, :], part_in_rows, 1, 1)
            for s in range(count):
                zown[first + s, :, lanes(r, quarter)] = value[s * feats : (s + 1) * feats].astype(bf16)

        for s in range(first, first + count):
            z_start(s)

    def along_history():
        @pl.loop(0, n)
        def _(b):
            where = lanes(b)
            for j in range(states):
                past = hist[j, :, where].astype(f32)
                gproj[b, m + j : m + j + 1, :] = jnp.sum(past, axis=0, keepdims=True)
                for s in range(4):
                    gproj[b, 4 * j + s : 4 * j + s + 1, :] = jnp.sum(
                        scaled[s, :, where] * past, axis=0, keepdims=True
                    )

    projs = Everyone(
        at, lambda to: gproj.at[to], lambda k: gproj_in.at[k], lambda k, origin: gproj_in.at[k],
        ex_send.at[15], ex_recv.at[15],
    )

    def norm_sums(s):
        which = 0 if s < 3 else 1

        @pl.loop(0, n)
        def _(b):
            where = lanes(b)
            value = rs_value(s, where)
            along = value * scaled[s, :, where]
            accs[7 + which] = accs[7 + which] + along
            accs[9 + which] = accs[9 + which] + value
            factor = colp[:, 1 + which : 2 + which]
            value = value * factor
            gn[s, :, where] = value
            gsum[s : s + 1, where] = jnp.sum(value, axis=0, keepdims=True)
            gsum[4 + s : 5 + s, where] = jnp.sum(along * factor, axis=0, keepdims=True)
            if s == 3:
                direct = cot[mine, where].astype(f32)
                accs[12] = accs[12] + direct
                value = value + direct * (1.0 / stat_out[4 + s : 5 + s, where])
            for j in range(states):
                gmix[b, 4 * j + s : 4 * j + s + 1, :] = jnp.sum(
                    value * hist[j, :, where].astype(f32), axis=0, keepdims=True
                )

    normalise(3)
    normalise(0)
    cots.other()
    cots.drain()

    @pl.loop(0, n)
    def _(b):
        where = lanes(b)
        cot[:, where] = cot[:, where] * masks[0:1, where].astype(bf16)

    gathers[3].near()
    normalise(1)
    gathers[0].near()
    normalise(2)
    along_history()
    projs.start()
    gathers[3].far()
    wait_columns()
    turn_columns(range(5))

    @pl.loop(0, chunks)
    def _(c):
        where = lanes(c, wide)
        gattn[:, where] = jnp.dot(zown[0], cot[:, where], preferred_element_type=f32).astype(bf16)

    gathers[3].other()
    project_up(0)
    gathers[0].far()
    project_up(1)
    gathers[1].near()
    back_up(0)
    back_up(1)
    gathers[2].near()
    normed_grad(3, ybuf.at[0, :, 0 : 4 * feats], 3, 4)
    weight_grad(3, 4, 3)
    gathers[1].far()
    rs_fold(3)
    out_grads(1, 4)
    for j in (4, 3, 2, 1):
        turn_start(j)
    gathers[0].other()
    project(0)
    gathers[1].other()
    project(1)
    z_step(1)
    gathers[2].far()
    gathers[2].other()
    project(2)
    rs_pass(3)

    key_at = lax.broadcasted_iota(jnp.int32, (block, block), 0).astype(f32)
    query_at = lax.broadcasted_iota(jnp.int32, (block, block), 1).astype(f32)

    @pl.loop(0, n // 2)
    def _(pair):
        chains = []
        for u in range(2):
            b = 2 * pair + u
            where = lanes(b)
            cut = pk[b, m + 1 : m + 2, :]
            _, _, valid = place(b, key_at)
            same = jnp.where(key_at >= cut, 1.0, 0.0) == jnp.where(query_at >= cut, 1.0, 0.0)
            allowed = same & (key_at <= query_at) & valid
            for h in range(heads):
                rows_h = pl.ds(h * HEAD_DIM, HEAD_DIM)
                scores = contract(qkv[1, rows_h, where], qkv[0, rows_h, where], 0, 0)
                chains.append((b, h, rows_h, where, allowed, scores))
        softs = []
        for b, h, rows_h, where, allowed, scores in chains:
            scores = jnp.where(allowed, scores, masked_score)
            weights = jnp.exp(scores - jnp.max(scores, axis=0, keepdims=True))
            softs.append(weights * (1.0 / jnp.sum(weights, axis=0, keepdims=True)))
        for (b, h, rows_h, where, _, _), soft in zip(chains, softs):
            probs[b * heads + h] = soft
            act[rows_h, where] = jnp.dot(
                qkv[2, rows_h, where], soft.astype(bf16), preferred_element_type=f32
            ).astype(bf16)


    @pl.loop(0, chunks)
    def _(c):
        where = lanes(c, wide)
        for r in range(2):
            half = slice(r * width // 2, (r + 1) * width // 2)
            ybuf[4, half, where] = jnp.dot(
                cols[r * n // 2 : (r + 1) * n // 2].reshape(width // 2, 5 * feats), act[:, where],
                preferred_element_type=f32,
            ).astype(bf16)

    rs_start(4)
    z_step(1)
    out_grads(0, 1)
    turn_start(0)

    @pl.loop(0, n // 2)
    def _(pair):
        first = []
        for u in range(2):
            b = 2 * pair + u
            where = lanes(b)
            for h in range(heads):
                rows_h = pl.ds(h * HEAD_DIM, HEAD_DIM)
                soft = probs[b * heads + h]
                grad = gattn[rows_h, where]
                dprob = contract(qkv[2, rows_h, where], grad, 0, 0)
                values_grad = contract(grad, soft.astype(bf16), 1, 1)
                first.append((rows_h, where, soft, dprob, values_grad))
        lows = []
        for rows_h, where, soft, dprob, values_grad in first:
            inner = jnp.sum(soft * dprob, axis=0, keepdims=True)
            lows.append((soft * (dprob - inner)).astype(bf16))
        for u in range(2):
            where = first[u * heads][1]
            grads = [[], [], []]
            for h in range(heads):
                rows_h, _, _, _, values_grad = first[u * heads + h]
                low = lows[u * heads + h]
                grads[0].append(
                    jnp.dot(qkv[1, rows_h, where], low, preferred_element_type=f32) * scale
                )
                grads[1].append(contract(qkv[0, rows_h, where], low, 1, 1))
                grads[2].append(values_grad)
            for s in range(3):
                value = jnp.concatenate(grads[s], axis=0)
                if s < 2:
                    value = rotated(value, where, -1.0)
                accs[s] = accs[s] + value
                gp[pl.ds(s * feats, feats), where] = value.astype(bf16)

    turn_end(4)
    z_step(2)
    normed_grad(0, w_turn.at[:, 0:feats], 0, 1)
    normed_grad(1, w_turn.at[:, feats : 2 * feats], 1, 1)
    rs_fold(0)
    normed_grad(2, w_turn.at[:, 2 * feats : 3 * feats], 2, 1)
    rs_fold(1)
    turn_end(3)
    for s in range(3):
        weight_grad(s, 1, s)
    rs_fold(2)
    rs_fold(4)
    z_step(2)
    turn_end(2)
    rs_end(3)
    norm_sums(3)
    z_step(3)
    rs_pass(0)
    turn_end(1)
    z_step(3)
    rs_pass(1)
    turn_end(0)
    rs_end(0)
    norm_sums(0)
    z_step(3)
    rs_pass(2)
    rs_pass(4)
    rs_end(1)
    norm_sums(1)
    z_step(3)
    rs_end(2)
    norm_sums(2)
    sums = Everyone(
        at, lambda to: gsum, lambda k: gsum_in.at[me], lambda k, origin: gsum_in.at[origin],
        ex_send.at[1], ex_recv.at[1],
    )
    mixes = Everyone(
        at, lambda to: gmix.at[to], lambda k: gmix_in.at[k], lambda k, origin: gmix_in.at[k],
        ex_send.at[2], ex_recv.at[2],
    )
    sums.start()
    mixes.start()
    rs_end(4)

    @pl.loop(0, n)
    def _(b):
        where = lanes(b)
        new_state[:, where] = (st3[:, where] + rs_value(4, where) + colp[:, 5:6]).astype(bf16)

    keep_new = pltpu.make_async_copy(new_state, new_out, load_sem.at[9])
    keep_new.start()
    z_step(2)
    for k in range(1, n):
        sums.wait(k)
    gsum_in[me] = gsum[...]
    total = gsum_in[0]
    for k in range(1, n):
        total = total + gsum_in[k]
    pre[0:8, :] = total * (1.0 / width)

    def stream_block(b):
        where = lanes(b)
        for s in range(4):
            value = stat_out[4 + s : 5 + s, where] * (
                gn[s, :, where] - pre[s : s + 1, where] - scaled[s, :, where] * pre[4 + s : 5 + s, where]
            )
            if s == 3:
                value = value + cot[mine, where].astype(f32)
            gn[s, :, where] = value
        for j in range(states - 1):
            value = pk[b, pl.ds(4 * j, 1), :] * gn[0, :, where]
            for s in range(1, 4):
                value = value + pk[b, pl.ds(4 * j + s, 1), :] * gn[s, :, where]
            hist[j, :, where] = value.astype(bf16)

    pl.loop(0, n // 2)(stream_block)

    total = gmix[me]
    for k in range(1, n):
        mixes.wait(k)
        total = total + gmix_in[k]
    fixed = gproj[me]
    for k in range(1, n):
        projs.wait(k)
        fixed = fixed + gproj_in[k]
    own = lanes(me)

    def each_state(value):
        return jnp.concatenate([value] * states, axis=0)

    history_sum = jnp.concatenate(
        [jnp.broadcast_to(fixed[m + j : m + j + 1], (4, block)) for j in range(states)], axis=0
    )
    grad_mix = each_state(stat_out[4:8, own]) * (
        total[0:m] - each_state(pre[0:4, own]) * history_sum - each_state(pre[4:8, own]) * fixed[0:m]
    )
    table = jnp.concatenate([gout[j] for j in range(states)], axis=0)
    hidden, slope = gelu_pair(raw[0:hid, :] * pk[me, m : m + 1, :])
    grad_hidden = contract(table, grad_mix, 0, 0, precision=highest)
    low = (grad_hidden * slope).astype(bf16).astype(f32)
    genmsg[0:hid, :] = low
    genmsg[hid : hid + 8, :] = jnp.broadcast_to(
        jnp.sum(low * raw[0:hid, :], axis=0, keepdims=True) * (1.0 / width), (8, block)
    )
    owns = Everyone(
        at, lambda to: genmsg, lambda k: gen_in_all.at[me], lambda k, origin: gen_in_all.at[origin],
        ex_send.at[3], ex_recv.at[3],
    )
    owns.start()
    z_step(2)
    _, _, valid = place(me, spot)
    kept = jnp.where(valid, 1.0, 0.0)
    ones = jnp.ones((8, block), f32)
    mixing = pk[me, 0:m, :]
    vec[...] = jnp.zeros_like(vec)
    vec[16 : 16 + hid, 0:m] = contract(hidden, grad_mix, 1, 1, precision=highest)
    for index, value in enumerate((grad_mix, mixing * kept, mixing * mixing * kept)):
        vec[56 + index : 57 + index, 0:m] = contract(ones, value, 1, 1, precision=highest)[0:1]
    vec[59:60, :] = jnp.broadcast_to(jnp.sum(kept, axis=1, keepdims=True), (1, block))
    prm[...] = jnp.zeros_like(prm)
    for index in range(13):
        prm[:, index : index + 1] = jnp.sum(accs[index], axis=1, keepdims=True)
    vec[0:16, :] = prm[...].T[0:16]

    def line(ref, landing, row, k, owner):
        return pltpu.make_async_remote_copy(
            src_ref=ref, dst_ref=landing.at[owner], send_sem=ex_send.at[row, k], recv_sem=ex_recv.at[row, k],
            device_id={"dp": (zc + k) % zn}, device_id_type=MESH,
        )

    def line_start(ref, landing, row):
        for k in range(1, zn):
            line(ref, landing, row, k, zc).start()

    def line_total(ref, landing, row):
        landing[zc] = ref[...]
        for k in range(1, zn):
            line(ref, landing, row, k, (zc + zn - k) % zn).wait()
        value = landing[0]
        for k in range(1, zn):
            value = value + landing[k]
        return value

    line_start(vec, vec_z, 4)
    pl.loop(n // 2, n)(stream_block)
    keep_hist = pltpu.make_async_copy(
        hist.at[pl.ds(0, states - 1)], hist_out.at[pl.ds(0, states - 1)], load_sem.at[10]
    )
    keep_hist.start()
    alls = Everyone(
        at, lambda to: vec_sum, lambda k: vec_all.at[me], lambda k, origin: vec_all.at[origin],
        ex_send.at[5], ex_recv.at[5],
    )
    total = line_total(vec, vec_z, 4)
    vec_sum[...] = total
    vec_all[me] = total
    alls.start()
    gen_in_all[me] = genmsg[...]
    for k in range(1, n):
        owns.wait(k)
    gin_mine = gin[:, rows(me)]
    late[...] = jnp.zeros_like(late)

    @pl.loop(0, n)
    def _(b):
        where = lanes(b)
        low_b = gen_in_all[b, 0:hid, :].astype(bf16)
        rms = pk[b, m : m + 1, :]
        last = hist[states - 1, :, where].astype(f32)
        grad_gen = contract(gin_mine, low_b, 0, 0)
        accs[11] = accs[11] + grad_gen * last * rms
        normed = (last * rms * colp[:, 0:1]).astype(bf16)
        late[0:hid, :] = late[0:hid, :] + contract(low_b, normed, 1, 1)
        value = rms * grad_gen * colp[:, 0:1]
        value = value - last * (rms * rms * rms * gen_in_all[b, hid : hid + 1, :])
        for s in range(4):
            value = value + pk[b, pl.ds(4 * (states - 1) + s, 1), :] * gn[s, :, where]
        hist[states - 1, :, where] = value.astype(bf16)

    keep_last = pltpu.make_async_copy(hist.at[states - 1], hist_out.at[states - 1], load_sem.at[11])
    keep_last.start()

    prm[:, 0:1] = jnp.sum(accs[11], axis=1, keepdims=True)
    late[hid : hid + 8, :] = prm[...].T[0:8]
    line_start(late, late_z, 16)
    z_step(1)
    lates = Everyone(
        at, lambda to: late_sum, lambda k: late_all.at[me], lambda k, origin: late_all.at[origin],
        ex_send.at[17], ex_recv.at[17],
    )
    total = line_total(late, late_z, 16)
    late_sum[...] = total
    late_all[me] = total
    lates.start()
    for k in range(1, n):
        alls.wait(k)
    shared = vec_all[0, 16:64, :]
    for k in range(1, n):
        shared = shared + vec_all[k, 16:64, :]
    prm[...] = jnp.zeros_like(prm)
    prm[0:40, :] = shared[0:40]
    count = shared[43:44, 0:1]
    mean = shared[41:42] / count
    prm[40:41, :] = shared[40:41]
    prm[41:42, :] = mean
    prm[42:43, :] = shared[42:43] / count - mean * mean
    turned = prm[...].T
    for j in range(states):
        gout_tot[j] = turned[4 * j : 4 * j + 4, 0:hid]
        gbias_tot[:, j : j + 1] = turned[4 * j : 4 * j + 4, 40:41]
        mean_tot[:, j : j + 1] = turned[4 * j : 4 * j + 4, 41:42]
        var_tot[:, j : j + 1] = turned[4 * j : 4 * j + 4, 42:43]
    z_step(1)
    for k in range(1, n):
        lates.wait(k)
    for k in range(n):
        where = pl.ds(k * feats, feats)
        bias_tot[:, where] = vec_all[k, 0:7, :]
        ngain_tot[:, where] = vec_all[k, 7:9, :]
        nbias_tot[:, where] = vec_all[k, 9:11, :]
        outb_tot[:, where] = vec_all[k, 12:13, :]
        gain_tot[:, where] = late_all[k, hid : hid + 1, :]
        gin_tot[:, where] = late_all[k, 0:hid, :]
    for step, c in z_actions:
        step(c)
    for c in range(12):
        z_drain(c)
    for i in range(5):
        rs_drain(i)
    for g in gathers:
        g.drain()
    for exchange in [parts, spread_mix, stats, projs, sums, mixes, owns, alls, lates] + turns:
        exchange.drain()
    for copy in stages + [keep_new, keep_hist, keep_last]:
        copy.wait()


def layer(n, zn, history, cotangent, bucket_len, valid_len, gen_gain, gen_in, gen_out, gen_bias, norm_gain, norm_bias, w_in, in_bias, w_out, w_down, out_bias):
    f32, bf16 = jnp.float32, jnp.bfloat16
    states, feats, tokens = history.shape
    block = tokens // n
    width = n * feats
    hid = gen_in.shape[1]
    heads = feats // HEAD_DIM
    vmem = pl.BlockSpec(memory_space=pltpu.VMEM)
    smem = pl.BlockSpec(memory_space=pltpu.SMEM)
    anys = pl.BlockSpec(memory_space=pl.ANY)
    shape = jax.ShapeDtypeStruct
    dma = pltpu.SemaphoreType.DMA
    return pl.pallas_call(
        functools.partial(layer_kernel, n, zn),
        out_shape=(
            shape((feats, tokens), bf16),
            shape((states, feats, tokens), bf16),
            shape((12, feats, width), bf16),
            shape((7, width), f32),
            shape((2, width), f32),
            shape((2, width), f32),
            shape((1, width), f32),
            shape((1, width), f32),
            shape((hid, width), f32),
            shape((states, 4, hid), f32),
            shape((4, states), f32),
            shape((4, states), f32),
            shape((4, states), f32),
        ),
        in_specs=[anys] * 2 + [smem] * 2 + [vmem] * 8 + [anys] * 2 + [vmem],
        out_specs=(anys,) * 3 + (vmem,) * 10,
        scratch_shapes=[
            pltpu.VMEM((states, feats, tokens), bf16),
            pltpu.VMEM((feats, tokens), bf16),
            pltpu.VMEM((4 * n, feats, tokens), bf16),
            pltpu.VMEM((width, tokens), bf16),
            pltpu.VMEM((n, zn, feats // zn, 5 * feats), bf16),
            pltpu.VMEM((width, 3 * feats), bf16),
            pltpu.VMEM((feats, feats), f32),
            pltpu.VMEM((feats, feats), f32),
            pltpu.VMEM((3, feats, tokens), bf16),
            pltpu.VMEM((5 * feats, tokens), bf16),
            pltpu.VMEM((4, feats, tokens), f32),
            pltpu.VMEM((n * heads, block, block), f32),
            pltpu.VMEM((feats, tokens), bf16),
            pltpu.VMEM((7 * feats, tokens), bf16),
            pltpu.VMEM((5, width, feats), bf16),
            pltpu.VMEM((16, tokens), f32),
            pltpu.VMEM((8, tokens), f32),
            pltpu.VMEM((13, feats, block), f32),
            pltpu.VMEM((4, feats, tokens), f32),
            pltpu.VMEM((4, feats, tokens), f32),
            pltpu.VMEM((feats, tokens), f32),
            pltpu.VMEM((n, 40, block), f32),
            pltpu.VMEM((hid + 8, block), f32),
            pltpu.VMEM((n, hid + 8, block), f32),
            pltpu.VMEM((n, hid + 8, block), f32),
            pltpu.VMEM((8, tokens), f32),
            pltpu.VMEM((n, 8, tokens), f32),
            pltpu.VMEM((8, tokens), f32),
            pltpu.VMEM((5, width, tokens), bf16),
            pltpu.VMEM((5, 4, feats, tokens), bf16),
            pltpu.VMEM((5, 2, feats, tokens), bf16),
            pltpu.VMEM((5, feats, tokens), bf16),
            pltpu.VMEM((12, feats, width), bf16),
            pltpu.VMEM((12, feats, width), bf16),
            pltpu.VMEM((12, feats, width), bf16),
            pltpu.VMEM((8, tokens), f32),
            pltpu.VMEM((n, 8, tokens), f32),
            pltpu.VMEM((n, 40, block), f32),
            pltpu.VMEM((n, 40, block), f32),
            pltpu.VMEM((8, tokens), f32),
            pltpu.VMEM((hid + 8, block), f32),
            pltpu.VMEM((n, hid + 8, block), f32),
            pltpu.VMEM((64, feats), f32),
            pltpu.VMEM((zn, 64, feats), f32),
            pltpu.VMEM((64, feats), f32),
            pltpu.VMEM((n, 64, feats), f32),
            pltpu.VMEM((hid + 8, feats), f32),
            pltpu.VMEM((zn, hid + 8, feats), f32),
            pltpu.VMEM((hid + 8, feats), f32),
            pltpu.VMEM((n, hid + 8, feats), f32),
            pltpu.VMEM((n, 48, block), f32),
            pltpu.VMEM((n, 48, block), f32),
            dma((17,)), dma((5, 7)), dma((5, 7)), dma((5, 7)), dma((5, 7)), dma((18, n)), dma((18, n)),
            dma((12, 3)), dma((12, 2)), dma((12,)),
        ],
        compiler_params=pltpu.CompilerParams(
            collective_id=1, has_side_effects=True, vmem_limit_bytes=67043328
        ),
        name="layer",
    )(
        history, cotangent, bucket_len, valid_len, gen_gain.reshape(1, width), gen_in.T,
        gen_out.transpose(2, 1, 0), gen_bias, norm_gain, norm_bias, w_in.transpose(1, 0, 2), in_bias,
        w_out, w_down, out_bias.reshape(1, width),
    )


def finish_kernel(new_in, hist_in, totals, *refs):
    count = (len(refs) - 10) // 2
    small_in = refs[:count]
    new_out, hist_out, in_out, out_out, down_out = refs[count : count + 5]
    small_out = refs[count + 5 : 2 * count + 5]
    new_buf, hist_buf, low, full, sem_in = refs[2 * count + 5 :]
    width = totals.shape[2]
    states = hist_in.shape[0]
    sources = [(new_in, new_buf)] + [(hist_in.at[j], hist_buf.at[j]) for j in range(states)]
    sources += [(totals.at[c], low.at[c]) for c in range(12)]
    targets = [(new_buf, new_out)] + [(hist_buf.at[j], hist_out.at[j]) for j in range(states)]
    for c in range(12):
        if c < 7:
            targets.append((full.at[c], in_out.at[c]))
        elif c == 7:
            targets.append((full.at[c], out_out))
        else:
            targets.append((full.at[c], down_out.at[:, (c - 8) * width : (c - 7) * width]))
    loads = [pltpu.make_async_copy(a, b, sem_in.at[0, i]) for i, (a, b) in enumerate(sources)]
    stores = [pltpu.make_async_copy(a, b, sem_in.at[1, i]) for i, (a, b) in enumerate(targets)]
    order = list(range(1 + states, 13 + states)) + list(range(1 + states))
    for i in order:
        loads[i].start()
    for a, b in zip(small_in, small_out):
        b[...] = a[...]
    for i in order:
        loads[i].wait()
        if i > states:
            c = i - 1 - states
            full[c] = low[c].astype(jnp.float32)
        stores[i].start()
    for copy in stores:
        copy.wait()


def finish(new_state, history_grad, totals, smalls):
    f32, bf16 = jnp.float32, jnp.bfloat16
    feats, width = totals.shape[1:]
    vmem = pl.BlockSpec(memory_space=pltpu.VMEM)
    anys = pl.BlockSpec(memory_space=pl.ANY)
    shape = jax.ShapeDtypeStruct
    return pl.pallas_call(
        finish_kernel,
        out_shape=(
            shape(new_state.shape, bf16),
            shape(history_grad.shape, bf16),
            shape((7, feats, width), f32),
            shape((feats, width), f32),
            shape((feats, 4 * width), f32),
        ) + tuple(shape(x.shape, x.dtype) for x in smalls),
        in_specs=[anys] * 3 + [vmem] * len(smalls),
        out_specs=(anys,) * 5 + (vmem,) * len(smalls),
        scratch_shapes=[
            pltpu.VMEM(new_state.shape, bf16),
            pltpu.VMEM(history_grad.shape, bf16),
            pltpu.VMEM(totals.shape, bf16),
            pltpu.VMEM(totals.shape, f32),
            pltpu.SemaphoreType.DMA((2, 13 + history_grad.shape[0])),
        ],
        compiler_params=pltpu.CompilerParams(vmem_limit_bytes=67043328),
        name="finish",
    )(new_state, history_grad, totals, *smalls)


def tp_device(
    history, cotangent, bucket_len, valid_len, gen_gain, gen_in, gen_out, gen_bias,
    norm_gain, norm_bias, w_in, in_bias, w_out, w_down, out_bias,
):
    n, zn = lax.axis_size("seq"), lax.axis_size("dp")
    new_state, history_grad, totals, *smalls = layer(
        n, zn, history, cotangent, bucket_len, valid_len, gen_gain, gen_in, gen_out, gen_bias,
        norm_gain, norm_bias, w_in, in_bias, w_out, w_down, out_bias,
    )
    (
        new_state, history_grad, in_grad, out_grad, down_grad,
        bias, ngain, nbias, gain, outb, gin, gout, gbias, mean, var,
    ) = finish(new_state, history_grad, totals, smalls)
    width = gen_gain.shape[0]
    return (
        new_state, history_grad, mean, var, gain.reshape(width), gin.T, gout.transpose(2, 1, 0),
        gbias, ngain, nbias, in_grad.transpose(1, 0, 2), bias, out_grad, down_grad, outb.reshape(width),
    )


def solution(mesh):
    in_specs = (
        P(None, "seq", "dp"),
        P("seq", "dp"),
        P("dp", "seq", None),
        P("dp", "seq", None),
        P(),
        P(),
        P(),
        P(),
        P(),
        P(),
        P("seq", None, None),
        P(),
        P("seq", None),
        P("seq", None),
        P(),
    )
    out_specs = (
        P("seq", "dp"),
        P(None, "seq", "dp"),
        P(),
        P(),
        P(),
        P(),
        P(),
        P(),
        P(),
        P(),
        P("seq", None, None),
        P(),
        P("seq", None),
        P("seq", None),
        P(),
    )
    by_feature = mesh.shape["seq"] == 8 and mesh.shape["dp"] in (1, 4)
    body = tp_device if by_feature else per_device
    return jax.shard_map(
        body, mesh=mesh, in_specs=in_specs, out_specs=out_specs, check_vma=False
    )
```

```python
import functools
import math

import jax
import jax.numpy as jnp
from jax import lax
from jax.experimental import pallas as pl
from jax.experimental.pallas import tpu as pltpu
from jax.sharding import PartitionSpec as P

HEADS = 16
HEAD_DIM = 64
ROT = 16


ln_eps = 1e-05
rms_eps = 1e-06
masked_score = -1e30
highest = lax.Precision.HIGHEST


def gelu_exact(values):
    return jax.nn.gelu(values, approximate=False)


def rotary_tables(position):
    freq_index = jnp.arange(ROT // 2, dtype=jnp.float32)
    inverse_freq = jnp.exp(freq_index * (-2.0 * math.log(10000.0) / ROT))
    angles = position.astype(jnp.float32)[:, None] * inverse_freq[None, :]
    return (jnp.cos(angles), jnp.sin(angles))


def rotate(values, cosine, sine):
    half = ROT // 2
    former = values[..., :half]
    latter = values[..., half:ROT]
    cos_heads = cosine[:, None, :]
    sin_heads = sine[:, None, :]
    return jnp.concatenate(
        [
            former * cos_heads - latter * sin_heads,
            latter * cos_heads + former * sin_heads,
            values[..., ROT:],
        ],
        axis=-1,
    )


def token_layout(lengths, counts, tokens):
    index = jnp.arange(tokens, dtype=jnp.int32)
    second = index >= lengths[0]
    position = index - jnp.where(second, lengths[0], 0)
    valid = position < jnp.where(second, counts[1], counts[0])
    return (second, position, valid)


def normalize(streams):
    centre = jnp.mean(streams, axis=-1, keepdims=True)
    centred = streams - centre
    inverse = lax.rsqrt(jnp.mean(centred * centred, axis=-1, keepdims=True) + ln_eps)
    return (centred * inverse, inverse)


def normalize_back(grad_scaled, scaled, inverse):
    mean_grad = jnp.mean(grad_scaled, axis=-1, keepdims=True)
    mean_along = jnp.mean(grad_scaled * scaled, axis=-1, keepdims=True)
    return inverse * (grad_scaled - mean_grad - scaled * mean_along)


def per_device(
    history,
    cotangent,
    bucket_len,
    valid_len,
    gen_gain,
    gen_in,
    gen_out,
    gen_bias,
    norm_gain,
    norm_bias,
    w_in,
    in_bias,
    w_out,
    w_down,
    out_bias,
):
    states = history.shape[0]
    stacked = jnp.concatenate([history, cotangent[None]], axis=0)
    arrived = lax.all_to_all(stacked, "seq", split_axis=2, concat_axis=1, tiled=True)
    arrived_rows = jnp.swapaxes(arrived, 1, 2)
    hist_local = arrived_rows[:states]
    cot_local = arrived_rows[states]
    tokens = hist_local.shape[1]
    width = hist_local.shape[2]
    second, position, valid = token_layout(bucket_len.reshape(2), valid_len.reshape(2), tokens)
    valid_float = valid.astype(jnp.float32)
    last = hist_local[states - 1].astype(jnp.float32)
    rms = lax.rsqrt(jnp.mean(last * last, axis=-1, keepdims=True) + rms_eps)
    gen_normed = (last * rms * gen_gain).astype(jnp.bfloat16)
    gen_pre = jnp.dot(gen_normed, gen_in, preferred_element_type=jnp.float32)
    gen_hidden, gen_pull = jax.vjp(gelu_exact, gen_pre)
    mixing = jnp.einsum("th,hsj->tsj", gen_hidden, gen_out, precision=highest) + gen_bias
    weighted = mixing * valid_float[:, None, None]
    stat_sums = jnp.sum(weighted, axis=0)
    stat_squares = jnp.sum(weighted * mixing, axis=0)
    stat_count = jnp.sum(valid_float)
    streams = mixing[:, :, 0].T[:, :, None] * hist_local[0]
    for state in range(1, states):
        streams = streams + mixing[:, :, state].T[:, :, None] * hist_local[state]
    scaled, inverse = normalize(streams)
    normed_attn = (scaled[:3] * norm_gain[0] + norm_bias[0]).astype(jnp.bfloat16)
    normed_mlp = (scaled[3] * norm_gain[1] + norm_bias[1]).astype(jnp.bfloat16)
    piece = lax.all_gather(w_in, "seq", axis=0, tiled=True)
    attn_part = jnp.einsum(
        "stk,nsk->stn", normed_attn, piece[:, :3], preferred_element_type=jnp.float32
    )
    mlp_part = jnp.einsum(
        "tk,njk->jtn", normed_mlp, piece[:, 3:], preferred_element_type=jnp.float32
    )
    projected = jnp.concatenate([attn_part, mlp_part], axis=0) + in_bias[:, None, :]
    cosine, sine = rotary_tables(position)
    heads_shape = (tokens, HEADS, HEAD_DIM)
    queries = (rotate(projected[0].reshape(heads_shape), cosine, sine) * HEAD_DIM ** (-0.5)).astype(
        jnp.bfloat16
    )
    keys = rotate(projected[1].reshape(heads_shape), cosine, sine).astype(jnp.bfloat16)
    values = projected[2].reshape(heads_shape).astype(jnp.bfloat16)
    index = jnp.arange(tokens, dtype=jnp.int32)
    allowed = (
        (second[:, None] == second[None, :]) & (index[None, :] <= index[:, None]) & valid[None, :]
    )
    scores = jnp.einsum("qhd,khd->hqk", queries, keys, preferred_element_type=jnp.float32)
    scores = jnp.where(allowed[None], scores, masked_score)
    top = jnp.max(scores, axis=-1, keepdims=True)
    weights = jnp.exp(scores - top)
    weight_total = jnp.sum(weights, axis=-1, keepdims=True)
    log_total = top + jnp.log(weight_total)
    probs_low = (weights / weight_total).astype(jnp.bfloat16)
    attended = jnp.einsum("hqk,khd->qhd", probs_low, values, preferred_element_type=jnp.float32)
    attn_low = attended.reshape(tokens, width).astype(jnp.bfloat16)
    gelu_up, up_pull = jax.vjp(gelu_exact, projected[3:])
    gelu_low = gelu_up.astype(jnp.bfloat16)
    grad_out_low = jnp.where(valid[:, None], cot_local, jnp.zeros_like(cot_local))
    piece_out, piece_down = lax.all_gather((w_out, w_down), "seq", axis=0, tiled=True)
    down_part = piece_down.reshape(piece_down.shape[0], 4, width)
    result = jnp.einsum("tk,nk->tn", attn_low, piece_out, preferred_element_type=jnp.float32)
    branch = result + jnp.einsum(
        "jtk,njk->tn", gelu_low, down_part, preferred_element_type=jnp.float32
    )
    new_local = (streams[3] + branch + out_bias).astype(jnp.bfloat16)
    piece_out = lax.all_gather(w_out, "seq", axis=0, tiled=True)
    piece_down = lax.all_gather(w_down, "seq", axis=0, tiled=True)
    count = piece_out.shape[0]
    part = grad_out_low
    attn_add = jnp.einsum("tn,nk->tk", part, piece_out, preferred_element_type=jnp.float32)
    gelu_add = jnp.einsum(
        "tn,njk->jtk", part, piece_down.reshape(count, 4, width), preferred_element_type=jnp.float32
    )
    grad_attn = attn_add
    part = grad_out_low
    term_out = jnp.einsum("tn,tk->nk", part, attn_low, preferred_element_type=jnp.float32)
    term_down = jnp.einsum(
        "tn,jtk->njk", part, gelu_low, preferred_element_type=jnp.float32
    ).reshape(lax.axis_size("seq") * w_out.shape[0], 4 * width)
    out_grads = lax.psum_scatter(
        jnp.concatenate([term_out, term_down], axis=1).astype(jnp.bfloat16),
        "seq",
        scatter_dimension=0,
        tiled=True,
    )
    out_bias_grad = jnp.sum(grad_out_low.astype(jnp.float32), axis=0)
    grad_attended = grad_attn.astype(jnp.bfloat16).reshape(heads_shape)
    rescored = jnp.einsum("qhd,khd->hqk", queries, keys, preferred_element_type=jnp.float32)
    probs = jnp.where(allowed[None], jnp.exp(rescored - log_total), 0.0)
    grad_values = jnp.einsum(
        "hqk,qhd->khd",
        probs.astype(jnp.bfloat16),
        grad_attended,
        preferred_element_type=jnp.float32,
    )
    grad_probs = jnp.einsum(
        "qhd,khd->hqk", grad_attended, values, preferred_element_type=jnp.float32
    )
    grad_scores = (
        probs * (grad_probs - jnp.sum(probs * grad_probs, axis=-1, keepdims=True))
    ).astype(jnp.bfloat16)
    grad_queries = jnp.einsum(
        "hqk,khd->qhd", grad_scores, keys, preferred_element_type=jnp.float32
    ) * HEAD_DIM ** (-0.5)
    grad_keys = jnp.einsum("hqk,qhd->khd", grad_scores, queries, preferred_element_type=jnp.float32)
    grad_up = up_pull(gelu_add)[0]
    grad_proj = jnp.concatenate(
        [
            rotate(grad_queries, cosine, -sine).reshape(1, tokens, width),
            rotate(grad_keys, cosine, -sine).reshape(1, tokens, width),
            grad_values.reshape(1, tokens, width),
            grad_up,
        ],
        axis=0,
    )
    in_bias_grad = jnp.sum(grad_proj, axis=1)
    grad_proj_low = grad_proj.astype(jnp.bfloat16)
    piece = lax.all_gather(w_in, "seq", axis=0, tiled=True)
    part = grad_proj_low
    attn_add = jnp.einsum(
        "stn,nsk->stk", part[:3], piece[:, :3], preferred_element_type=jnp.float32
    )
    mlp_add = jnp.einsum("jtn,njk->tk", part[3:], piece[:, 3:], preferred_element_type=jnp.float32)
    part = grad_proj_low
    attn_term = jnp.einsum(
        "stn,stk->nsk", part[:3], normed_attn, preferred_element_type=jnp.float32
    )
    mlp_term = jnp.einsum("jtn,tk->njk", part[3:], normed_mlp, preferred_element_type=jnp.float32)
    in_grads = lax.psum_scatter(
        jnp.concatenate([attn_term, mlp_term], axis=1).astype(jnp.bfloat16),
        "seq",
        scatter_dimension=0,
        tiled=True,
    )
    norm_gain_grad = jnp.stack(
        [jnp.sum(attn_add * scaled[:3], axis=(0, 1)), jnp.sum(mlp_add * scaled[3], axis=0)]
    )
    norm_bias_grad = jnp.stack([jnp.sum(attn_add, axis=(0, 1)), jnp.sum(mlp_add, axis=0)])
    grad_attn_streams = normalize_back(attn_add * norm_gain[0], scaled[:3], inverse[:3])
    grad_mlp_stream = normalize_back(
        mlp_add * norm_gain[1], scaled[3], inverse[3]
    ) + grad_out_low.astype(jnp.float32)
    grad_streams = jnp.concatenate([grad_attn_streams, grad_mlp_stream[None]], axis=0)
    grad_mixing = jnp.stack(
        [
            jnp.einsum(
                "std,td->ts", grad_streams, hist_local[state].astype(jnp.float32), precision=highest
            )
            for state in range(states)
        ],
        axis=-1,
    )
    hist_terms = [
        jnp.einsum("ts,std->td", mixing[:, :, state], grad_streams, precision=highest)
        for state in range(states)
    ]
    gen_bias_grad = jnp.sum(grad_mixing, axis=0)
    gen_out_grad = jnp.einsum("th,tsj->hsj", gen_hidden, grad_mixing, precision=highest)
    grad_hidden = jnp.einsum("tsj,hsj->th", grad_mixing, gen_out, precision=highest)
    grad_pre_low = gen_pull(grad_hidden)[0].astype(jnp.bfloat16)
    gen_in_grad = jnp.einsum(
        "tk,th->kh", gen_normed, grad_pre_low, preferred_element_type=jnp.float32
    )
    grad_gen = jnp.einsum("th,kh->tk", grad_pre_low, gen_in, preferred_element_type=jnp.float32)
    gen_gain_grad = jnp.sum(grad_gen * last * rms, axis=0)
    gained = grad_gen * gen_gain
    grad_last = rms * gained - last * (rms * rms * rms) * jnp.mean(
        gained * last, axis=-1, keepdims=True
    )
    hist_stack = jnp.stack(hist_terms[: states - 1] + [hist_terms[states - 1] + grad_last]).astype(
        jnp.bfloat16
    )
    departing = jnp.swapaxes(jnp.concatenate([new_local[None], hist_stack], axis=0), 1, 2)
    returned = lax.all_to_all(departing, "seq", split_axis=1, concat_axis=2, tiled=True)
    w_in_grad, out_total = (
        lax.psum(in_grads, "dp").astype(jnp.float32),
        lax.psum(out_grads, "dp").astype(jnp.float32),
    )
    w_out_grad = out_total[:, :width]
    w_down_grad = out_total[:, width:]
    joined = lax.psum(
        (
            gen_gain_grad,
            gen_in_grad,
            gen_out_grad,
            gen_bias_grad,
            norm_gain_grad,
            norm_bias_grad,
            in_bias_grad,
            out_bias_grad,
            stat_sums,
            stat_squares,
            stat_count,
        ),
        ("seq", "dp"),
    )
    small_totals = joined[:8]
    stat_totals = joined[8:]
    mix_mean = stat_totals[0] / stat_totals[2]
    mix_var = stat_totals[1] / stat_totals[2] - mix_mean * mix_mean
    return (
        returned[0],
        returned[1:],
        mix_mean,
        mix_var,
        small_totals[0],
        small_totals[1],
        small_totals[2],
        small_totals[3],
        small_totals[4],
        small_totals[5],
        w_in_grad,
        small_totals[6],
        w_out_grad,
        w_down_grad,
        small_totals[7],
    )


MESH = pl.DeviceIdType.MESH
HIDDEN_ROWS = 40
ROOT_HALF = math.sqrt(0.5)
INV_ROOT_2PI = 1.0 / math.sqrt(2.0 * math.pi)


def gelu_pair(x):
    half = 0.5 + 0.5 * lax.erf(x * ROOT_HALF)
    return x * half, half + x * (jnp.exp(-0.5 * x * x) * INV_ROOT_2PI)


def contract(a, b, dim_a, dim_b, precision=None):
    return lax.dot_general(
        a, b, (((dim_a,), (dim_b,)), ((), ())),
        precision=precision, preferred_element_type=jnp.float32,
    )


class Links:
    def __init__(self, n):
        self.n = n
        self.me = lax.axis_index("seq")
        core = self.me % 2
        xbit = (self.me // 2) % 2
        ybit = (self.me // 4) % 2
        flip = 1 - 2 * core
        x = self.me + 2 - 4 * xbit
        y = self.me + 4 - 8 * ybit
        self.core = core
        self.a = x * (1 - core) + y * core
        self.b = y * (1 - core) + x * core
        self.dg = x + y - self.me
        self.p = self.me + flip
        self.pa = self.b + flip
        self.pb = self.a + flip
        self.pdg = self.dg + flip

    def copy(self, src, dst, send, recv, to):
        return pltpu.make_async_remote_copy(
            src_ref=src, dst_ref=dst, send_sem=send, recv_sem=recv,
            device_id={"seq": to}, device_id_type=MESH,
        )


class Gather:
    def __init__(self, links, place, send, recv):
        self.links, self.place, self.send, self.recv = links, place, send, recv

    def _go(self, src, owner, slot, index, to):
        self.links.copy(
            src, self.place(owner), self.send.at[slot], self.recv.at[index], to
        ).start()

    def _got(self, owner, index):
        place = self.place(owner)
        self.links.copy(place, place, self.send.at[0], self.recv.at[index], self.links.p).wait_recv()

    def start(self, src):
        at = self.links
        self._go(src, at.me, 0, 0, at.a)
        self._go(src, at.me, 1, 1, at.b)
        self._go(src, at.me, 2, 3, at.p)

    def near(self):
        at = self.links
        self._got(at.a, 0)
        self._go(self.place(at.a), at.a, 3, 2, at.b)
        self._go(self.place(at.a), at.a, 4, 4, at.p)
        self._got(at.b, 1)
        self._go(self.place(at.b), at.b, 5, 5, at.p)

    def far(self):
        at = self.links
        self._got(at.dg, 2)
        self._go(self.place(at.dg), at.dg, 6, 6, at.p)

    def other(self):
        at = self.links
        for owner, index in ((at.p, 3), (at.pa, 4), (at.pb, 5), (at.pdg, 6)):
            self._got(owner, index)

    def drain(self):
        place = self.place(self.links.me)
        for slot in range(7):
            self.links.copy(
                place, place, self.send.at[slot], self.recv.at[0], self.links.p
            ).wait_send()


class Everyone:
    def __init__(self, links, source, target, arrived, send, recv):
        self.links, self.source, self.target, self.arrived = links, source, target, arrived
        self.send, self.recv = send, recv

    def start(self):
        at = self.links
        for k in range(1, at.n):
            to = (at.me + k) % at.n
            at.copy(
                self.source(to), self.target(k), self.send.at[k], self.recv.at[k], to
            ).start()

    def wait(self, k):
        at = self.links
        origin = (at.me + at.n - k) % at.n
        place = self.arrived(k, origin)
        at.copy(place, place, self.send.at[k], self.recv.at[k], at.p).wait_recv()
        return origin

    def drain(self):
        at = self.links
        for k in range(1, at.n):
            to = (at.me + k) % at.n
            place = self.source(to)
            at.copy(place, place, self.send.at[k], self.recv.at[k], at.p).wait_send()


def layer_kernel(
    n, zn,
    history, cotangent, lens, vals, gain, gin, gout, gbias, ng, nb, w_all, in_bias, w_out, w_down, out_bias,
    new_out, hist_out, totals,
    bias_tot, ngain_tot, nbias_tot, gain_tot, outb_tot, gin_tot, gout_tot,
    gbias_tot, mean_tot, var_tot,
    w_in, hist, new_state, big, cot, cols, w_turn, prm, colp, qkv, act, deriv, probs, gattn, gp, gcol, rope, masks, accs, gn,
    scaled, st3, pk, raw, part, part_in, stat, stat_in, stat_out,
    ybuf, abuf, from_a, from_b, zown, zin, zmid,
    gsum, gsum_in, gmix, gmix_in, pre, genmsg, gen_in_all, vec, vec_z, vec_sum, vec_all,
    late, late_z, late_sum, late_all, gproj, gproj_in,
    load_sem, ag_send, ag_recv, rs_send, rs_recv, ex_send, ex_recv, z_send, z_recv, out_sem,
):
    f32, bf16 = jnp.float32, jnp.bfloat16
    states, feats, tokens = hist.shape
    block = tokens // n
    width = n * feats
    hid = gin.shape[0]
    heads = feats // HEAD_DIM
    scale = HEAD_DIM ** (-0.5)
    m = 4 * states
    wide = 2 * block
    chunks = tokens // wide
    quarter = width // 4
    at = Links(n)
    me = at.me
    zc = lax.axis_index("dp")

    def rows(owner):
        return pl.ds(pl.multiple_of(owner * feats, feats), feats)

    def lanes(index, size=block):
        return pl.ds(pl.multiple_of(index * size, size), size)

    mine = rows(me)

    load_last = pltpu.make_async_copy(history.at[states - 1], hist.at[states - 1], load_sem.at[0])
    load_hist = pltpu.make_async_copy(
        history.at[pl.ds(0, states - 1)], hist.at[pl.ds(0, states - 1)], load_sem.at[1]
    )
    load_cot = pltpu.make_async_copy(cotangent, cot.at[mine, :], load_sem.at[2])
    load_w = pltpu.make_async_copy(w_all, w_in, load_sem.at[17])
    for copy in (load_last, load_cot, load_hist, load_w):
        copy.start()
    barrier = pltpu.get_barrier_semaphore()
    for k in range(1, n):
        pl.semaphore_signal(
            barrier, inc=1, device_id={"seq": (me + k) % n}, device_id_type=MESH
        )
    for k in range(1, zn):
        pl.semaphore_signal(
            barrier, inc=1, device_id={"dp": (zc + k) % zn}, device_id_type=MESH
        )

    gathers = [
        Gather(at, lambda owner, s=s: big.at[s * n + owner], ag_send.at[s], ag_recv.at[s])
        for s in range(4)
    ]
    cots = Gather(at, lambda owner: cot.at[rows(owner), :], ag_send.at[4], ag_recv.at[4])
    parts = Everyone(
        at, lambda to: part.at[to], lambda k: part_in.at[k], lambda k, origin: part_in.at[k],
        ex_send.at[6], ex_recv.at[6],
    )
    spread_mix = Everyone(
        at, lambda to: pk.at[me], lambda k: pk.at[me], lambda k, origin: pk.at[origin],
        ex_send.at[7], ex_recv.at[7],
    )
    stats = Everyone(
        at, lambda to: stat, lambda k: stat_in.at[me], lambda k, origin: stat_in.at[origin],
        ex_send.at[8], ex_recv.at[8],
    )

    prm[...] = jnp.zeros_like(prm)
    prm[0:1, :] = gain[:, mine]
    prm[1:3, :] = ng[:, mine]
    prm[3:5, :] = nb[:, mine]
    prm[5:6, :] = out_bias[:, mine]
    prm[8:15, :] = in_bias[:, mine]
    colp[...] = prm[...].T
    accs[...] = jnp.zeros_like(accs)

    gin_mine = gin[:, mine]
    load_last.wait()
    for b in range(n):
        last = hist[states - 1, :, b * block : (b + 1) * block].astype(f32)
        product = (last * colp[:, 0:1]).astype(bf16)
        part[b, 0:hid, :] = jnp.dot(gin_mine, product, preferred_element_type=f32)
        part[b, hid : hid + 8, :] = jnp.broadcast_to(
            jnp.sum(last * last, axis=0, keepdims=True), (8, block)
        )
    pl.semaphore_wait(barrier, n - 1 + zn - 1)
    parts.start()
    load_cot.wait()
    cots.start(cot.at[mine, :])
    load_w.wait()

    @pl.loop(0, n)
    def _(r):
        for j in range(4):
            ybuf[0, rows(r), j * feats : (j + 1) * feats] = w_in[3 + j, :, lanes(r, feats)].T

    load_hist.wait()
    total = part[me]
    for k in range(1, n):
        parts.wait(k)
        total = total + part_in[k]
    raw[...] = total
    rms = lax.rsqrt(total[hid : hid + 1] * (1.0 / width) + rms_eps)
    hidden, _ = gelu_pair(total[0:hid] * rms)
    table = jnp.concatenate([gout[j] for j in range(states)], axis=0)
    mixing = jnp.dot(table, hidden, precision=highest, preferred_element_type=f32)
    for j in range(states):
        pk[me, 4 * j : 4 * j + 4, :] = mixing[4 * j : 4 * j + 4] + gbias[:, j : j + 1]
    pk[me, m : m + 1, :] = rms
    for offset, value in ((1, lens[0, 0, 0]), (2, vals[0, 0, 0]), (3, vals[0, 0, 1])):
        pk[me, m + offset : m + offset + 1, :] = jnp.full((1, block), value.astype(f32))
    spread_mix.start()

    share = feats // zn
    shared_rows = pl.ds(pl.multiple_of(zc * share, share), share)

    def column_copy(to, j):
        if j == 0:
            src = w_out.at[shared_rows, rows(to)]
        else:
            src = w_down.at[
                shared_rows, pl.ds(pl.multiple_of((j - 1) * width + to * feats, feats), feats)
            ]
        return src, cols.at[me, zc, :, pl.ds(j * feats, feats)]

    for k in range(1, n):
        to = (me + k) % n
        for j in range(5):
            src, dst = column_copy(to, j)
            at.copy(src, dst, ex_send.at[9, k], ex_recv.at[9, k], to).start()
    own_cols = [
        pltpu.make_async_copy(*column_copy(me, j), load_sem.at[3 + j]) for j in range(5)
    ]
    for copy in own_cols:
        copy.start()
    cots.near()

    def line_columns(k, owner):
        part_cols = cols.at[:, owner]
        return pltpu.make_async_remote_copy(
            src_ref=part_cols, dst_ref=part_cols, send_sem=ex_send.at[10, k], recv_sem=ex_recv.at[10, k],
            device_id={"dp": (zc + k) % zn}, device_id_type=MESH,
        )

    def share_columns():
        for k in range(1, n):
            arrived = cols.at[(me + n - k) % n, zc]
            at.copy(arrived, arrived, ex_send.at[9, k], ex_recv.at[9, k], at.p).wait()
        for copy in own_cols:
            copy.wait()
        for k in range(1, zn):
            line_columns(k, zc).start()

    def wait_columns():
        for k in range(1, zn):
            line_columns(k, (zc + zn - k) % zn).wait()

    def mix_block(owner):
        where = lanes(owner)
        for half in range(2):
            part_rows = pl.ds(half * (feats // 2), feats // 2)
            sums = [None] * 4
            for j in range(states):
                value = hist[j, part_rows, where].astype(f32)
                for s in range(4):
                    weight = pk[owner, pl.ds(4 * j + s, 1), :]
                    term = weight * value
                    sums[s] = term if sums[s] is None else sums[s] + term
            for s in range(4):
                scaled[s, part_rows, where] = sums[s]
        for s in range(4):
            value = scaled[s, :, where]
            mean = jnp.sum(value, axis=0, keepdims=True) * (1.0 / feats)
            off = value - mean
            stat[pl.ds(s, 1), where] = mean
            stat[pl.ds(4 + s, 1), where] = jnp.sum(off * off, axis=0, keepdims=True)

    mix_block(me)

    @pl.loop(1, n // 2)
    def _(k):
        mix_block(spread_mix.wait(k))

    share_columns()

    @pl.loop(n // 2, n)
    def _(k):
        mix_block(spread_mix.wait(k))

    stats.start()

    spot = lax.broadcasted_iota(jnp.int32, (1, block), 1).astype(f32)
    freq = jnp.exp(
        lax.broadcasted_iota(jnp.int32, (8, block), 0).astype(f32)
        * (-2.0 * math.log(10000.0) / ROT)
    )

    def place(owner, index):
        cut = pk[owner, m + 1 : m + 2, :]
        second = index >= cut
        position = index - jnp.where(second, cut, 0.0)
        limit = jnp.where(second, pk[owner, m + 3 : m + 4, :], pk[owner, m + 2 : m + 3, :])
        return second, position, position < limit

    for b in range(n):
        where = pl.ds(b * block, block)
        _, position, valid = place(b, spot)
        angle = freq * position
        rope[0:8, where] = jnp.cos(angle)
        rope[8:16, where] = jnp.sin(angle)
        masks[0:1, where] = jnp.where(valid, 1.0, 0.0)

    cots.far()

    @pl.loop(0, n)
    def _(r):
        for s in range(3):
            w_turn[rows(r), s * feats : (s + 1) * feats] = w_in[s, :, lanes(r, feats)].T

    for k in range(1, n):
        stats.wait(k)
    stat_in[me] = stat[...]
    means = stat_in[0, 0:4, :]
    for k in range(1, n):
        means = means + stat_in[k, 0:4, :]
    means = means * (1.0 / n)
    spread = jnp.zeros_like(means)
    for k in range(n):
        away = stat_in[k, 0:4, :] - means
        spread = spread + (stat_in[k, 4:8, :] + feats * (away * away))
    stat_out[0:4, :] = means
    stat_out[4:8, :] = lax.rsqrt(spread * (1.0 / width) + ln_eps)

    def normalise(s):
        which = 0 if s < 3 else 1

        @pl.loop(0, n)
        def _(b):
            where = lanes(b)
            value = scaled[s, :, where]
            if s == 3:
                st3[:, where] = value
            xhat = (value - stat_out[s : s + 1, where]) * stat_out[4 + s : 5 + s, where]
            scaled[s, :, where] = xhat
            big[s * n + me, :, where] = (
                xhat * colp[:, 1 + which : 2 + which] + colp[:, 3 + which : 4 + which]
            ).astype(bf16)

        gathers[s].start(big.at[s * n + me])

    def rotated(value, where, sign):
        cosine, sine = rope[0:8, where], rope[8:16, where] * sign
        out = []
        for h in range(heads):
            base = h * HEAD_DIM
            former, latter = value[base : base + 8], value[base + 8 : base + 16]
            out += [
                former * cosine - latter * sine,
                latter * cosine + former * sine,
                value[base + 16 : base + HEAD_DIM],
            ]
        return jnp.concatenate(out, axis=0)

    def stream(s, where):
        return big[pl.ds(s * n, n), :, where].reshape(width, -1)

    def project(s):
        @pl.loop(0, chunks)
        def _(c):
            where = lanes(c, wide)
            value = jnp.dot(w_in[s], stream(s, where), preferred_element_type=f32)
            value = value + colp[:, 8 + s : 9 + s]
            if s < 2:
                value = rotated(value, where, 1.0)
            if s == 0:
                value = value * scale
            qkv[s, :, where] = value.astype(bf16)

    def project_up(pair):
        @pl.loop(0, chunks)
        def _(c):
            where = lanes(c, wide)
            weight = w_in[3 + 2 * pair : 5 + 2 * pair].reshape(2 * feats, width)
            both = jnp.dot(weight, stream(3, where), preferred_element_type=f32)
            for i in range(2):
                j = 2 * pair + i
                up, slope = gelu_pair(
                    both[i * feats : (i + 1) * feats] + colp[:, 11 + j : 12 + j]
                )
                act[pl.ds((1 + j) * feats, feats), where] = up.astype(bf16)
                deriv[j, :, where] = slope

    def rs_copy(i, src, dst, slot, to):
        return at.copy(src, dst, rs_send.at[i, slot], rs_recv.at[i, slot], to)

    def rs_first(i):
        return [
            rs_copy(i, ybuf.at[i, rows(owner), :], abuf.at[i, q], q, at.p)
            for q, owner in enumerate((at.p, at.pa, at.pb, at.pdg))
        ]

    def rs_second(i):
        return [
            rs_copy(i, ybuf.at[i, rows(at.a), :], from_a.at[i, 0], 4, at.a),
            rs_copy(i, ybuf.at[i, rows(at.dg), :], from_a.at[i, 1], 5, at.a),
        ]

    def rs_third(i):
        return [rs_copy(i, ybuf.at[i, rows(at.b), :], from_b.at[i], 6, at.b)]

    def rs_start(i):
        for copy in rs_first(i):
            copy.start()

    def rs_fold(i):
        for copy in rs_first(i):
            copy.wait_recv()

        @pl.loop(0, chunks)
        def _(c):
            where = lanes(c, wide)
            for q, owner in ((1, at.a), (3, at.dg)):
                ybuf[i, rows(owner), where] = (
                    ybuf[i, rows(owner), where].astype(f32) + abuf[i, q, :, where].astype(f32)
                ).astype(bf16)

        for copy in rs_second(i):
            copy.start()

    def rs_pass(i):
        for copy in rs_second(i):
            copy.wait_recv()

        @pl.loop(0, chunks)
        def _(c):
            where = lanes(c, wide)
            ybuf[i, rows(at.b), where] = (
                ybuf[i, rows(at.b), where].astype(f32)
                + abuf[i, 2, :, where].astype(f32)
                + from_a[i, 1, :, where].astype(f32)
            ).astype(bf16)

        for copy in rs_third(i):
            copy.start()

    def rs_end(i):
        for copy in rs_third(i):
            copy.wait_recv()

    def rs_value(i, where):
        return (
            ybuf[i, rows(me), where].astype(f32)
            + abuf[i, 0, :, where].astype(f32)
            + from_a[i, 0, :, where].astype(f32)
            + from_b[i, :, where].astype(f32)
        )

    def rs_drain(i):
        for copy in rs_first(i) + rs_second(i) + rs_third(i):
            copy.wait_send()

    outer = (zc == 0) | (zc == 3)
    z_in = 1 + zc // 3
    z_out = 3 * (zc - 1)
    z_over = 3 - zc

    def z_copy(c, src, dst, slot, recv_slot, to):
        return pltpu.make_async_remote_copy(
            src_ref=src, dst_ref=dst, send_sem=z_send.at[c, slot], recv_sem=z_recv.at[c, recv_slot],
            device_id={"dp": to}, device_id_type=MESH,
        )

    def z_up(c):
        return z_copy(c, zown.at[c], zin.at[c], 0, 0, z_in)

    def z_cross(c):
        return z_copy(c, zown.at[c], zmid.at[c], 1, 1, z_over)

    def z_down(c):
        return z_copy(c, zin.at[c], zin.at[c], 2, 0, z_out)

    def z_start(c):
        if zn > 1:

            @pl.when(outer)
            def _():
                z_up(c).start()

    def z_fold(c):
        if zn > 1:

            @pl.when(jnp.logical_not(outer))
            def _():
                z_up(c).wait_recv()

                @pl.loop(0, chunks)
                def _(k):
                    where = lanes(k, wide)
                    zown[c, :, where] = (
                        zown[c, :, where].astype(f32) + zin[c, :, where].astype(f32)
                    ).astype(bf16)

                z_cross(c).start()

    stages = []

    def z_end(c):
        if zn > 1:

            @pl.when(jnp.logical_not(outer))
            def _():
                z_cross(c).wait_recv()

                @pl.loop(0, chunks)
                def _(k):
                    where = lanes(k, wide)
                    zin[c, :, where] = (
                        zown[c, :, where].astype(f32) + zmid[c, :, where].astype(f32)
                    ).astype(bf16)

                z_down(c).start()

            @pl.when(outer)
            def _():
                z_up(c).wait_recv()

        source = zin if zn > 1 else zown
        stages.append(pltpu.make_async_copy(source.at[c], totals.at[c], out_sem.at[c]))
        stages[-1].start()

    def z_drain(c):
        if zn > 1:

            @pl.when(outer)
            def _():
                z_up(c).wait_send()

            @pl.when(jnp.logical_not(outer))
            def _():
                z_cross(c).wait_send()
                z_down(c).wait_send()

    z_order = (3, 4, 5, 6, 11, 10, 0, 1, 2, 9, 8, 7)
    z_actions = []
    for t in range(14):
        if t < 12:
            z_actions.append((z_fold, z_order[t]))
        if t >= 2:
            z_actions.append((z_end, z_order[t - 2]))
    z_actions = iter(z_actions)

    def z_step(count):
        for _ in range(count):
            step, c = next(z_actions)
            step(c)


    def turn_columns(which):
        @pl.loop(0, n)
        def _(r):
            for j in which:
                zown[j, :, lanes(r, feats)] = (
                    cols[r, :, :, j * feats : (j + 1) * feats].reshape(feats, feats).T
                )

    def back_up(pair):
        @pl.loop(0, chunks)
        def _(c):
            where = lanes(c, wide)
            weight = zown[1 + 2 * pair : 3 + 2 * pair].reshape(2 * feats, width)
            both = jnp.dot(weight, cot[:, where], preferred_element_type=f32)
            for i in range(2):
                j = 2 * pair + i
                value = both[i * feats : (i + 1) * feats] * deriv[j, :, where]
                accs[3 + j] = accs[3 + j] + (value[:, :block] + value[:, block:])
                gp[pl.ds((3 + j) * feats, feats), where] = value.astype(bf16)

    def out_grads(first, count):
        for r in range(4):
            grads = contract(
                cot[r * quarter : (r + 1) * quarter, :],
                act[first * feats : (first + count) * feats, :], 1, 1,
            ).astype(bf16)
            for j in range(count):
                gcol[first + j, r * quarter : (r + 1) * quarter, :] = (
                    grads[:, j * feats : (j + 1) * feats]
                )

    turns = [
        Everyone(
            at,
            lambda to, j=j: gcol.at[j, rows(to), :],
            lambda k, j=j: zown.at[7 + j, :, mine],
            lambda k, origin, j=j: zown.at[7 + j, :, rows(origin)],
            ex_send.at[(0, 11, 12, 13, 14)[j]], ex_recv.at[(0, 11, 12, 13, 14)[j]],
        )
        for j in range(5)
    ]
    keeps = [
        pltpu.make_async_copy(gcol.at[j, mine, :], zown.at[7 + j, :, mine], load_sem.at[12 + j])
        for j in range(5)
    ]

    def turn_start(j):
        turns[j].start()
        keeps[j].start()

    def turn_end(j):
        for k in range(1, n):
            turns[j].wait(k)
        keeps[j].wait()
        z_start(7 + j)

    def normed_grad(i, source, first, count):
        @pl.loop(0, chunks)
        def _(c):
            where = lanes(c, wide)
            for r in range(2):
                half = slice(r * width // 2, (r + 1) * width // 2)
                ybuf[i, half, where] = jnp.dot(
                    source[half, :], gp[first * feats : (first + count) * feats, where],
                    preferred_element_type=f32,
                ).astype(bf16)

        rs_start(i)

    def weight_grad(first, count, source):
        @pl.loop(0, 4)
        def _(r):
            part_in_rows = big[pl.ds(source * n + r * (n // 4), n // 4), :, :].reshape(quarter, tokens)
            value = contract(gp[first * feats : (first + count) * feats, :], part_in_rows, 1, 1)
            for s in range(count):
                zown[first + s, :, lanes(r, quarter)] = value[s * feats : (s + 1) * feats].astype(bf16)

        for s in range(first, first + count):
            z_start(s)

    def along_history():
        @pl.loop(0, n)
        def _(b):
            where = lanes(b)
            for j in range(states):
                past = hist[j, :, where].astype(f32)
                gproj[b, m + j : m + j + 1, :] = jnp.sum(past, axis=0, keepdims=True)
                for s in range(4):
                    gproj[b, 4 * j + s : 4 * j + s + 1, :] = jnp.sum(
                        scaled[s, :, where] * past, axis=0, keepdims=True
                    )

    projs = Everyone(
        at, lambda to: gproj.at[to], lambda k: gproj_in.at[k], lambda k, origin: gproj_in.at[k],
        ex_send.at[15], ex_recv.at[15],
    )

    def norm_sums(s):
        which = 0 if s < 3 else 1

        @pl.loop(0, n)
        def _(b):
            where = lanes(b)
            value = rs_value(s, where)
            along = value * scaled[s, :, where]
            accs[7 + which] = accs[7 + which] + along
            accs[9 + which] = accs[9 + which] + value
            factor = colp[:, 1 + which : 2 + which]
            value = value * factor
            gn[s, :, where] = value
            gsum[s : s + 1, where] = jnp.sum(value, axis=0, keepdims=True)
            gsum[4 + s : 5 + s, where] = jnp.sum(along * factor, axis=0, keepdims=True)
            if s == 3:
                direct = cot[mine, where].astype(f32)
                accs[12] = accs[12] + direct
                value = value + direct * (1.0 / stat_out[4 + s : 5 + s, where])
            for j in range(states):
                gmix[b, 4 * j + s : 4 * j + s + 1, :] = jnp.sum(
                    value * hist[j, :, where].astype(f32), axis=0, keepdims=True
                )

    normalise(3)
    normalise(0)
    cots.other()
    cots.drain()

    @pl.loop(0, n)
    def _(b):
        where = lanes(b)
        cot[:, where] = cot[:, where] * masks[0:1, where].astype(bf16)

    gathers[3].near()
    normalise(1)
    gathers[0].near()
    normalise(2)
    along_history()
    projs.start()
    gathers[3].far()
    wait_columns()
    turn_columns(range(5))

    @pl.loop(0, chunks)
    def _(c):
        where = lanes(c, wide)
        gattn[:, where] = jnp.dot(zown[0], cot[:, where], preferred_element_type=f32).astype(bf16)

    gathers[3].other()
    project_up(0)
    gathers[0].far()
    project_up(1)
    gathers[1].near()
    back_up(0)
    back_up(1)
    gathers[2].near()
    normed_grad(3, ybuf.at[0, :, 0 : 4 * feats], 3, 4)
    weight_grad(3, 4, 3)
    gathers[1].far()
    rs_fold(3)
    out_grads(1, 4)
    for j in (4, 3, 2, 1):
        turn_start(j)
    gathers[0].other()
    project(0)
    gathers[1].other()
    project(1)
    z_step(1)
    gathers[2].far()
    gathers[2].other()
    project(2)
    rs_pass(3)

    key_at = lax.broadcasted_iota(jnp.int32, (block, block), 0).astype(f32)
    query_at = lax.broadcasted_iota(jnp.int32, (block, block), 1).astype(f32)

    @pl.loop(0, n // 2)
    def _(pair):
        chains = []
        for u in range(2):
            b = 2 * pair + u
            where = lanes(b)
            cut = pk[b, m + 1 : m + 2, :]
            _, _, valid = place(b, key_at)
            same = jnp.where(key_at >= cut, 1.0, 0.0) == jnp.where(query_at >= cut, 1.0, 0.0)
            allowed = same & (key_at <= query_at) & valid
            for h in range(heads):
                rows_h = pl.ds(h * HEAD_DIM, HEAD_DIM)
                scores = contract(qkv[1, rows_h, where], qkv[0, rows_h, where], 0, 0)
                chains.append((b, h, rows_h, where, allowed, scores))
        softs = []
        for b, h, rows_h, where, allowed, scores in chains:
            scores = jnp.where(allowed, scores, masked_score)
            weights = jnp.exp(scores - jnp.max(scores, axis=0, keepdims=True))
            softs.append(weights * (1.0 / jnp.sum(weights, axis=0, keepdims=True)))
        for (b, h, rows_h, where, _, _), soft in zip(chains, softs):
            probs[b * heads + h] = soft
            act[rows_h, where] = jnp.dot(
                qkv[2, rows_h, where], soft.astype(bf16), preferred_element_type=f32
            ).astype(bf16)


    @pl.loop(0, chunks)
    def _(c):
        where = lanes(c, wide)
        for r in range(2):
            half = slice(r * width // 2, (r + 1) * width // 2)
            ybuf[4, half, where] = jnp.dot(
                cols[r * n // 2 : (r + 1) * n // 2].reshape(width // 2, 5 * feats), act[:, where],
                preferred_element_type=f32,
            ).astype(bf16)

    rs_start(4)
    z_step(1)
    out_grads(0, 1)
    turn_start(0)

    @pl.loop(0, n // 2)
    def _(pair):
        first = []
        for u in range(2):
            b = 2 * pair + u
            where = lanes(b)
            for h in range(heads):
                rows_h = pl.ds(h * HEAD_DIM, HEAD_DIM)
                soft = probs[b * heads + h]
                grad = gattn[rows_h, where]
                dprob = contract(qkv[2, rows_h, where], grad, 0, 0)
                values_grad = contract(grad, soft.astype(bf16), 1, 1)
                first.append((rows_h, where, soft, dprob, values_grad))
        lows = []
        for rows_h, where, soft, dprob, values_grad in first:
            inner = jnp.sum(soft * dprob, axis=0, keepdims=True)
            lows.append((soft * (dprob - inner)).astype(bf16))
        for u in range(2):
            where = first[u * heads][1]
            grads = [[], [], []]
            for h in range(heads):
                rows_h, _, _, _, values_grad = first[u * heads + h]
                low = lows[u * heads + h]
                grads[0].append(
                    jnp.dot(qkv[1, rows_h, where], low, preferred_element_type=f32) * scale
                )
                grads[1].append(contract(qkv[0, rows_h, where], low, 1, 1))
                grads[2].append(values_grad)
            for s in range(3):
                value = jnp.concatenate(grads[s], axis=0)
                if s < 2:
                    value = rotated(value, where, -1.0)
                accs[s] = accs[s] + value
                gp[pl.ds(s * feats, feats), where] = value.astype(bf16)

    normed_grad(0, w_turn.at[:, 0:feats], 0, 1)
    normed_grad(1, w_turn.at[:, feats : 2 * feats], 1, 1)
    rs_fold(0)
    normed_grad(2, w_turn.at[:, 2 * feats : 3 * feats], 2, 1)
    rs_fold(1)
    turn_end(4)
    turn_end(3)
    z_step(2)
    for s in range(3):
        weight_grad(s, 1, s)
    rs_fold(2)
    rs_fold(4)
    z_step(2)
    turn_end(2)
    rs_end(3)
    norm_sums(3)
    z_step(3)
    rs_pass(0)
    turn_end(1)
    z_step(3)
    rs_pass(1)
    turn_end(0)
    rs_end(0)
    norm_sums(0)
    z_step(3)
    rs_pass(2)
    rs_pass(4)
    rs_end(1)
    norm_sums(1)
    z_step(3)
    rs_end(2)
    norm_sums(2)
    sums = Everyone(
        at, lambda to: gsum, lambda k: gsum_in.at[me], lambda k, origin: gsum_in.at[origin],
        ex_send.at[1], ex_recv.at[1],
    )
    mixes = Everyone(
        at, lambda to: gmix.at[to], lambda k: gmix_in.at[k], lambda k, origin: gmix_in.at[k],
        ex_send.at[2], ex_recv.at[2],
    )
    sums.start()
    mixes.start()
    rs_end(4)

    @pl.loop(0, n)
    def _(b):
        where = lanes(b)
        new_state[:, where] = (st3[:, where] + rs_value(4, where) + colp[:, 5:6]).astype(bf16)

    keep_new = pltpu.make_async_copy(new_state, new_out, load_sem.at[9])
    keep_new.start()
    z_step(2)
    for k in range(1, n):
        sums.wait(k)
    gsum_in[me] = gsum[...]
    total = gsum_in[0]
    for k in range(1, n):
        total = total + gsum_in[k]
    pre[0:8, :] = total * (1.0 / width)

    def stream_block(b):
        where = lanes(b)
        for s in range(4):
            value = stat_out[4 + s : 5 + s, where] * (
                gn[s, :, where] - pre[s : s + 1, where] - scaled[s, :, where] * pre[4 + s : 5 + s, where]
            )
            if s == 3:
                value = value + cot[mine, where].astype(f32)
            gn[s, :, where] = value
        for j in range(states - 1):
            value = pk[b, pl.ds(4 * j, 1), :] * gn[0, :, where]
            for s in range(1, 4):
                value = value + pk[b, pl.ds(4 * j + s, 1), :] * gn[s, :, where]
            hist[j, :, where] = value.astype(bf16)

    pl.loop(0, n // 2)(stream_block)

    total = gmix[me]
    for k in range(1, n):
        mixes.wait(k)
        total = total + gmix_in[k]
    fixed = gproj[me]
    for k in range(1, n):
        projs.wait(k)
        fixed = fixed + gproj_in[k]
    own = lanes(me)

    def each_state(value):
        return jnp.concatenate([value] * states, axis=0)

    history_sum = jnp.concatenate(
        [jnp.broadcast_to(fixed[m + j : m + j + 1], (4, block)) for j in range(states)], axis=0
    )
    grad_mix = each_state(stat_out[4:8, own]) * (
        total[0:m] - each_state(pre[0:4, own]) * history_sum - each_state(pre[4:8, own]) * fixed[0:m]
    )
    table = jnp.concatenate([gout[j] for j in range(states)], axis=0)
    hidden, slope = gelu_pair(raw[0:hid, :] * pk[me, m : m + 1, :])
    grad_hidden = contract(table, grad_mix, 0, 0, precision=highest)
    low = (grad_hidden * slope).astype(bf16).astype(f32)
    genmsg[0:hid, :] = low
    genmsg[hid : hid + 8, :] = jnp.broadcast_to(
        jnp.sum(low * raw[0:hid, :], axis=0, keepdims=True) * (1.0 / width), (8, block)
    )
    owns = Everyone(
        at, lambda to: genmsg, lambda k: gen_in_all.at[me], lambda k, origin: gen_in_all.at[origin],
        ex_send.at[3], ex_recv.at[3],
    )
    owns.start()
    z_step(2)
    _, _, valid = place(me, spot)
    kept = jnp.where(valid, 1.0, 0.0)
    ones = jnp.ones((8, block), f32)
    mixing = pk[me, 0:m, :]
    vec[...] = jnp.zeros_like(vec)
    vec[16 : 16 + hid, 0:m] = contract(hidden, grad_mix, 1, 1, precision=highest)
    for index, value in enumerate((grad_mix, mixing * kept, mixing * mixing * kept)):
        vec[56 + index : 57 + index, 0:m] = contract(ones, value, 1, 1, precision=highest)[0:1]
    vec[59:60, :] = jnp.broadcast_to(jnp.sum(kept, axis=1, keepdims=True), (1, block))
    prm[...] = jnp.zeros_like(prm)
    for index in range(13):
        prm[:, index : index + 1] = jnp.sum(accs[index], axis=1, keepdims=True)
    vec[0:16, :] = prm[...].T[0:16]

    def line(ref, landing, row, k, owner):
        return pltpu.make_async_remote_copy(
            src_ref=ref, dst_ref=landing.at[owner], send_sem=ex_send.at[row, k], recv_sem=ex_recv.at[row, k],
            device_id={"dp": (zc + k) % zn}, device_id_type=MESH,
        )

    def line_start(ref, landing, row):
        for k in range(1, zn):
            line(ref, landing, row, k, zc).start()

    def line_total(ref, landing, row):
        landing[zc] = ref[...]
        for k in range(1, zn):
            line(ref, landing, row, k, (zc + zn - k) % zn).wait()
        value = landing[0]
        for k in range(1, zn):
            value = value + landing[k]
        return value

    line_start(vec, vec_z, 4)
    pl.loop(n // 2, n)(stream_block)
    keep_hist = pltpu.make_async_copy(
        hist.at[pl.ds(0, states - 1)], hist_out.at[pl.ds(0, states - 1)], load_sem.at[10]
    )
    keep_hist.start()
    alls = Everyone(
        at, lambda to: vec_sum, lambda k: vec_all.at[me], lambda k, origin: vec_all.at[origin],
        ex_send.at[5], ex_recv.at[5],
    )
    total = line_total(vec, vec_z, 4)
    vec_sum[...] = total
    vec_all[me] = total
    alls.start()
    gen_in_all[me] = genmsg[...]
    for k in range(1, n):
        owns.wait(k)
    gin_mine = gin[:, rows(me)]
    late[...] = jnp.zeros_like(late)

    @pl.loop(0, n)
    def _(b):
        where = lanes(b)
        low_b = gen_in_all[b, 0:hid, :].astype(bf16)
        rms = pk[b, m : m + 1, :]
        last = hist[states - 1, :, where].astype(f32)
        grad_gen = contract(gin_mine, low_b, 0, 0)
        accs[11] = accs[11] + grad_gen * last * rms
        normed = (last * rms * colp[:, 0:1]).astype(bf16)
        late[0:hid, :] = late[0:hid, :] + contract(low_b, normed, 1, 1)
        value = rms * grad_gen * colp[:, 0:1]
        value = value - last * (rms * rms * rms * gen_in_all[b, hid : hid + 1, :])
        for s in range(4):
            value = value + pk[b, pl.ds(4 * (states - 1) + s, 1), :] * gn[s, :, where]
        hist[states - 1, :, where] = value.astype(bf16)

    keep_last = pltpu.make_async_copy(hist.at[states - 1], hist_out.at[states - 1], load_sem.at[11])
    keep_last.start()

    prm[:, 0:1] = jnp.sum(accs[11], axis=1, keepdims=True)
    late[hid : hid + 8, :] = prm[...].T[0:8]
    line_start(late, late_z, 16)
    z_step(1)
    lates = Everyone(
        at, lambda to: late_sum, lambda k: late_all.at[me], lambda k, origin: late_all.at[origin],
        ex_send.at[17], ex_recv.at[17],
    )
    total = line_total(late, late_z, 16)
    late_sum[...] = total
    late_all[me] = total
    lates.start()
    for k in range(1, n):
        alls.wait(k)
    shared = vec_all[0, 16:64, :]
    for k in range(1, n):
        shared = shared + vec_all[k, 16:64, :]
    prm[...] = jnp.zeros_like(prm)
    prm[0:40, :] = shared[0:40]
    count = shared[43:44, 0:1]
    mean = shared[41:42] / count
    prm[40:41, :] = shared[40:41]
    prm[41:42, :] = mean
    prm[42:43, :] = shared[42:43] / count - mean * mean
    turned = prm[...].T
    for j in range(states):
        gout_tot[j] = turned[4 * j : 4 * j + 4, 0:hid]
        gbias_tot[:, j : j + 1] = turned[4 * j : 4 * j + 4, 40:41]
        mean_tot[:, j : j + 1] = turned[4 * j : 4 * j + 4, 41:42]
        var_tot[:, j : j + 1] = turned[4 * j : 4 * j + 4, 42:43]
    z_step(1)
    for k in range(1, n):
        lates.wait(k)
    for k in range(n):
        where = pl.ds(k * feats, feats)
        bias_tot[:, where] = vec_all[k, 0:7, :]
        ngain_tot[:, where] = vec_all[k, 7:9, :]
        nbias_tot[:, where] = vec_all[k, 9:11, :]
        outb_tot[:, where] = vec_all[k, 12:13, :]
        gain_tot[:, where] = late_all[k, hid : hid + 1, :]
        gin_tot[:, where] = late_all[k, 0:hid, :]
    for step, c in z_actions:
        step(c)
    for c in range(12):
        z_drain(c)
    for i in range(5):
        rs_drain(i)
    for g in gathers:
        g.drain()
    for exchange in [parts, spread_mix, stats, projs, sums, mixes, owns, alls, lates] + turns:
        exchange.drain()
    for copy in stages + [keep_new, keep_hist, keep_last]:
        copy.wait()


def layer(n, zn, history, cotangent, bucket_len, valid_len, gen_gain, gen_in, gen_out, gen_bias, norm_gain, norm_bias, w_in, in_bias, w_out, w_down, out_bias):
    f32, bf16 = jnp.float32, jnp.bfloat16
    states, feats, tokens = history.shape
    block = tokens // n
    width = n * feats
    hid = gen_in.shape[1]
    heads = feats // HEAD_DIM
    vmem = pl.BlockSpec(memory_space=pltpu.VMEM)
    smem = pl.BlockSpec(memory_space=pltpu.SMEM)
    anys = pl.BlockSpec(memory_space=pl.ANY)
    shape = jax.ShapeDtypeStruct
    dma = pltpu.SemaphoreType.DMA
    return pl.pallas_call(
        functools.partial(layer_kernel, n, zn),
        out_shape=(
            shape((feats, tokens), bf16),
            shape((states, feats, tokens), bf16),
            shape((12, feats, width), bf16),
            shape((7, width), f32),
            shape((2, width), f32),
            shape((2, width), f32),
            shape((1, width), f32),
            shape((1, width), f32),
            shape((hid, width), f32),
            shape((states, 4, hid), f32),
            shape((4, states), f32),
            shape((4, states), f32),
            shape((4, states), f32),
        ),
        in_specs=[anys] * 2 + [smem] * 2 + [vmem] * 6 + [anys, vmem] + [anys] * 2 + [vmem],
        out_specs=(anys,) * 3 + (vmem,) * 10,
        scratch_shapes=[
            pltpu.VMEM((7, feats, width), bf16),
            pltpu.VMEM((states, feats, tokens), bf16),
            pltpu.VMEM((feats, tokens), bf16),
            pltpu.VMEM((4 * n, feats, tokens), bf16),
            pltpu.VMEM((width, tokens), bf16),
            pltpu.VMEM((n, zn, feats // zn, 5 * feats), bf16),
            pltpu.VMEM((width, 3 * feats), bf16),
            pltpu.VMEM((feats, feats), f32),
            pltpu.VMEM((feats, feats), f32),
            pltpu.VMEM((3, feats, tokens), bf16),
            pltpu.VMEM((5 * feats, tokens), bf16),
            pltpu.VMEM((4, feats, tokens), f32),
            pltpu.VMEM((n * heads, block, block), f32),
            pltpu.VMEM((feats, tokens), bf16),
            pltpu.VMEM((7 * feats, tokens), bf16),
            pltpu.VMEM((5, width, feats), bf16),
            pltpu.VMEM((16, tokens), f32),
            pltpu.VMEM((8, tokens), f32),
            pltpu.VMEM((13, feats, block), f32),
            pltpu.VMEM((4, feats, tokens), f32),
            pltpu.VMEM((4, feats, tokens), f32),
            pltpu.VMEM((feats, tokens), f32),
            pltpu.VMEM((n, 40, block), f32),
            pltpu.VMEM((hid + 8, block), f32),
            pltpu.VMEM((n, hid + 8, block), f32),
            pltpu.VMEM((n, hid + 8, block), f32),
            pltpu.VMEM((8, tokens), f32),
            pltpu.VMEM((n, 8, tokens), f32),
            pltpu.VMEM((8, tokens), f32),
            pltpu.VMEM((5, width, tokens), bf16),
            pltpu.VMEM((5, 4, feats, tokens), bf16),
            pltpu.VMEM((5, 2, feats, tokens), bf16),
            pltpu.VMEM((5, feats, tokens), bf16),
            pltpu.VMEM((12, feats, width), bf16),
            pltpu.VMEM((12, feats, width), bf16),
            pltpu.VMEM((12, feats, width), bf16),
            pltpu.VMEM((8, tokens), f32),
            pltpu.VMEM((n, 8, tokens), f32),
            pltpu.VMEM((n, 40, block), f32),
            pltpu.VMEM((n, 40, block), f32),
            pltpu.VMEM((8, tokens), f32),
            pltpu.VMEM((hid + 8, block), f32),
            pltpu.VMEM((n, hid + 8, block), f32),
            pltpu.VMEM((64, feats), f32),
            pltpu.VMEM((zn, 64, feats), f32),
            pltpu.VMEM((64, feats), f32),
            pltpu.VMEM((n, 64, feats), f32),
            pltpu.VMEM((hid + 8, feats), f32),
            pltpu.VMEM((zn, hid + 8, feats), f32),
            pltpu.VMEM((hid + 8, feats), f32),
            pltpu.VMEM((n, hid + 8, feats), f32),
            pltpu.VMEM((n, 48, block), f32),
            pltpu.VMEM((n, 48, block), f32),
            dma((18,)), dma((5, 7)), dma((5, 7)), dma((5, 7)), dma((5, 7)), dma((18, n)), dma((18, n)),
            dma((12, 3)), dma((12, 2)), dma((12,)),
        ],
        compiler_params=pltpu.CompilerParams(
            collective_id=1, has_side_effects=True, vmem_limit_bytes=67043328
        ),
        name="layer",
    )(
        history, cotangent, bucket_len, valid_len, gen_gain.reshape(1, width), gen_in.T,
        gen_out.transpose(2, 1, 0), gen_bias, norm_gain, norm_bias, w_in.transpose(1, 0, 2), in_bias,
        w_out, w_down, out_bias.reshape(1, width),
    )


def finish_kernel(new_in, hist_in, totals, *refs):
    count = (len(refs) - 10) // 3
    small_in = refs[:count]
    new_out, hist_out, in_out, out_out, down_out = refs[count : count + 5]
    small_out = refs[count + 5 : 2 * count + 5]
    small_buf = refs[2 * count + 5 : 3 * count + 5]
    new_buf, hist_buf, low, full, sem_in = refs[3 * count + 5 :]
    width = totals.shape[2]
    states = hist_in.shape[0]
    sources = [(new_in, new_buf)] + [(hist_in.at[j], hist_buf.at[j]) for j in range(states)]
    sources += [(totals.at[c], low.at[c]) for c in range(12)]
    targets = [(new_buf, new_out)] + [(hist_buf.at[j], hist_out.at[j]) for j in range(states)]
    for c in range(12):
        if c < 7:
            targets.append((full.at[c], in_out.at[c]))
        elif c == 7:
            targets.append((full.at[c], out_out))
        else:
            targets.append((full.at[c], down_out.at[:, (c - 8) * width : (c - 7) * width]))
    sources += list(zip(small_in, small_buf))
    targets += list(zip(small_buf, small_out))
    loads = [pltpu.make_async_copy(a, b, sem_in.at[0, i]) for i, (a, b) in enumerate(sources)]
    stores = [pltpu.make_async_copy(a, b, sem_in.at[1, i]) for i, (a, b) in enumerate(targets)]
    order = list(range(1 + states, 13 + states)) + list(range(1 + states))
    order += list(range(13 + states, len(sources)))
    for i in order:
        loads[i].start()
    for i in order:
        loads[i].wait()
        if states < i < 13 + states:
            c = i - 1 - states
            full[c] = low[c].astype(jnp.float32)
        stores[i].start()
    for copy in stores:
        copy.wait()


def finish(new_state, history_grad, totals, smalls):
    f32, bf16 = jnp.float32, jnp.bfloat16
    feats, width = totals.shape[1:]
    anys = pl.BlockSpec(memory_space=pl.ANY)
    shape = jax.ShapeDtypeStruct
    return pl.pallas_call(
        finish_kernel,
        out_shape=(
            shape(new_state.shape, bf16),
            shape(history_grad.shape, bf16),
            shape((7, feats, width), f32),
            shape((feats, width), f32),
            shape((feats, 4 * width), f32),
        ) + tuple(shape(x.shape, x.dtype) for x in smalls),
        in_specs=[anys] * (3 + len(smalls)),
        out_specs=(anys,) * (5 + len(smalls)),
        scratch_shapes=[pltpu.VMEM(x.shape, x.dtype) for x in smalls] + [
            pltpu.VMEM(new_state.shape, bf16),
            pltpu.VMEM(history_grad.shape, bf16),
            pltpu.VMEM(totals.shape, bf16),
            pltpu.VMEM(totals.shape, f32),
            pltpu.SemaphoreType.DMA((2, 13 + history_grad.shape[0] + len(smalls))),
        ],
        compiler_params=pltpu.CompilerParams(vmem_limit_bytes=67043328),
        name="finish",
    )(new_state, history_grad, totals, *smalls)


def tp_device(
    history, cotangent, bucket_len, valid_len, gen_gain, gen_in, gen_out, gen_bias,
    norm_gain, norm_bias, w_in, in_bias, w_out, w_down, out_bias,
):
    n, zn = lax.axis_size("seq"), lax.axis_size("dp")
    new_state, history_grad, totals, *smalls = layer(
        n, zn, history, cotangent, bucket_len, valid_len, gen_gain, gen_in, gen_out, gen_bias,
        norm_gain, norm_bias, w_in, in_bias, w_out, w_down, out_bias,
    )
    (
        new_state, history_grad, in_grad, out_grad, down_grad,
        bias, ngain, nbias, gain, outb, gin, gout, gbias, mean, var,
    ) = finish(new_state, history_grad, totals, smalls)
    width = gen_gain.shape[0]
    return (
        new_state, history_grad, mean, var, gain.reshape(width), gin.T, gout.transpose(2, 1, 0),
        gbias, ngain, nbias, in_grad.transpose(1, 0, 2), bias, out_grad, down_grad, outb.reshape(width),
    )


def solution(mesh):
    in_specs = (
        P(None, "seq", "dp"),
        P("seq", "dp"),
        P("dp", "seq", None),
        P("dp", "seq", None),
        P(),
        P(),
        P(),
        P(),
        P(),
        P(),
        P("seq", None, None),
        P(),
        P("seq", None),
        P("seq", None),
        P(),
    )
    out_specs = (
        P("seq", "dp"),
        P(None, "seq", "dp"),
        P(),
        P(),
        P(),
        P(),
        P(),
        P(),
        P(),
        P(),
        P("seq", None, None),
        P(),
        P("seq", None),
        P("seq", None),
        P(),
    )
    by_feature = mesh.shape["seq"] == 8 and mesh.shape["dp"] in (1, 4)
    body = tp_device if by_feature else per_device
    return jax.shard_map(
        body, mesh=mesh, in_specs=in_specs, out_specs=out_specs, check_vma=False
    )
```
